256 devices in a mesh: row: 32 (over x, z), col: 8 (over y, core).
Axes of the slice: x: 4, y: 4, z: 8, core: 2. Of those that a mesh axis runs over, the one named last changes fastest.
Arguments:
- incident: float32 [2, 36, 32768], P(None, None, 'row'), may hold values from -24 to 24
- diagonal: float32 [32768], P('row'), may hold values from 1 to 2
- near_blocks: bfloat16 [32, 8, 2, 1024, 1024], P('row', None, None, None, 'col'), may hold values from -0.046875 to 0.046875
- left_factors: bfloat16 [32, 32, 2, 64, 1024], P('row', 'col'), may hold values from -0.0390625 to 0.0390625
- right_factors: bfloat16 [32, 32, 2, 64, 1024], P('row', 'col'), may hold values from -0.1875 to 0.1875
- flags: int32 [32, 8], P('row'), may hold values from 0 to 1, as said below
- ranks: int32 [32, 32], P('row', 'col'), may hold values from 4 to 64
- harmonics: float32 [2, 36, 32768], P(None, None, 'row'), may hold values from -0.03125 to 0.03125
Outputs:
- solution: float32 [2, 36, 32768], P(None, None, 'row')
- coefficients: float32 [2, 36, 36], replicated
The draws below stay inside these ranges and needn't reach their ends.
Inputs may be any that keep to these rules, and one draw needn't show every extreme that they name: `flags`: slot 8 / 2 (the pair of a cluster with itself) is always 1; the ones of a row form one run of slots around it.
All inputs are finite; a program needn't handle non-finite values.
Results may differ from the reference program's by a relative error of at most 0.0013.
Values may be sent and summed in bfloat16 or wider, within the bound.
A program may use at most 128 MiB of HBM per device.

```python
import math
import jax
import jax.numpy as jnp
from jax import lax

ELEM = 1024
FIELDS = 36
HARM = 36
RMAX = 64
NEAR = 8
NCLUS = 32
NELEM = 32768


def draw_incident(key, part):
    cluster = (jnp.arange(NELEM) // ELEM).astype(jnp.float32)
    amplitude = 0.6 * jnp.power(3.0, cluster / (NCLUS - 1.0))
    values = jax.random.normal(key, (2, FIELDS, NELEM), jnp.float32)
    return jnp.clip(values, -6.0, 6.0) * amplitude[None, None, :]


def draw_flags(key, part):
    half_band = NEAR // 2
    lower_key, upper_key = jax.random.split(key)
    rows = jnp.arange(NCLUS)[:, None]
    lower = jax.random.randint(lower_key, (NCLUS, 1), 0, half_band + 1)
    upper = jax.random.randint(upper_key, (NCLUS, 1), 0, NEAR - half_band)
    lower = jnp.where(rows == 0, half_band, lower)
    upper = jnp.where(rows == 0, NEAR - half_band - 1, upper)
    lower = jnp.where(rows == NCLUS // 2, 0, lower)
    upper = jnp.where(rows == NCLUS // 2, 0, upper)
    offsets = jnp.arange(NEAR)[None, :] - half_band
    return ((offsets >= -lower) & (offsets <= upper)).astype(jnp.int32)


def draw_ranks(key, part):
    values = jax.random.randint(key, (NCLUS, NCLUS), 4, RMAX + 1)
    rows = jnp.arange(NCLUS)[:, None]
    columns = jnp.arange(NCLUS)[None, :]
    values = jnp.where((rows == NCLUS // 2) & (columns == 0), RMAX, values)
    values = jnp.where((rows == NCLUS // 2) & (columns == NCLUS - 1), 4, values)
    return values.astype(jnp.int32)


def levels(own_key, shape, shards, smallest, top_value):
    def one(dim, parts):
        steps = jax.random.uniform(jax.random.fold_in(jax.random.fold_in(own_key, 6), dim), (parts,), jnp.float32, smallest / len(shards), top_value / len(shards))
        return jnp.repeat(jnp.exp(steps), shape[dim] // parts).reshape((-1,) + (1,) * (len(shape) - dim - 1))

    gain = one(*shards[0])
    for cut in shards[1:]:
        gain = gain * one(*cut)
    return gain


def gaussian(stream_key, dims, deviation, limit, cuts=(), held_as=jnp.bfloat16):
    level = levels(stream_key, dims, cuts, -0.22, 0.18) if cuts else 1.0
    values = jax.random.normal(stream_key, dims, jnp.float32) * deviation * level
    return jnp.minimum(jnp.maximum(values, -limit), limit).astype(held_as)


def setup_inputs(seed: int = 0) -> dict:
    seeds = jax.random.split(jax.random.key(seed), 9)
    return {
        "incident": draw_incident(jax.random.fold_in(seeds[8], 71), 0),
        "diagonal": jnp.clip(jnp.exp(math.log(2.0) - 0.6931472 * jax.random.uniform(seeds[1], (NELEM,), jnp.float32) ** levels(seeds[1], (NELEM,), ((0, 32),), -0.2, 0.2)), 1.0, 2.0),
        "near_blocks": gaussian(seeds[2], (NCLUS, NEAR, 2, ELEM, ELEM), (16 * ELEM) ** -0.5, 0.046875, ((0, 32), (4, 8))),
        "left_factors": gaussian(seeds[3], (NCLUS, NCLUS, 2, RMAX, ELEM), (384 * RMAX) ** -0.5, 0.0390625, ((0, 32), (1, 8))),
        "right_factors": gaussian(seeds[4], (NCLUS, NCLUS, 2, RMAX, ELEM), ELEM ** -0.5, 0.1875, ((0, 32), (1, 8))),
        "flags": draw_flags(jax.random.fold_in(seeds[8], 71), 0),
        "ranks": draw_ranks(jax.random.fold_in(seeds[8], 71), 0),
        "harmonics": gaussian(seeds[7], (2, HARM, NELEM), NELEM ** -0.5, 0.03125, ((2, 32),), jnp.float32),
    }


highest = lax.Precision.HIGHEST

def dense_term(vector, block):

    def product(left, right):
        return jnp.einsum('sf,ef->se', left, right, precision=highest)
    real_out = product(vector[0], block[0]) - product(vector[1], block[1])
    imag_out = product(vector[0], block[1]) + product(vector[1], block[0])
    return jnp.stack([real_out, imag_out])

def lowrank_term(vector, left_block, right_block, rank):

    def inner(left, right):
        return jnp.einsum('sf,rf->sr', left, right, precision=highest)

    def outer(left, right):
        return jnp.einsum('sr,re->se', left, right, precision=highest)
    coeff_real = inner(vector[0], right_block[0]) - inner(vector[1], right_block[1])
    coeff_imag = inner(vector[0], right_block[1]) + inner(vector[1], right_block[0])
    keep = (jnp.arange(right_block.shape[1], dtype=jnp.int32) < rank)[None, None, :]
    coeffs = jnp.where(keep, jnp.stack([coeff_real, coeff_imag]), 0.0)
    coeffs = lax.optimization_barrier(coeffs.astype(jnp.bfloat16)).astype(jnp.float32)
    real_out = outer(coeffs[0], left_block[0]) - outer(coeffs[1], left_block[1])
    imag_out = outer(coeffs[0], left_block[1]) + outer(coeffs[1], left_block[0])
    return jnp.stack([real_out, imag_out])

def apply_operator(vector, diagonal, near_blocks, left_factors, right_factors, flags, ranks):
    rounded = lax.optimization_barrier(vector.astype(jnp.bfloat16)).astype(jnp.float32)
    pieces = rounded.reshape(2, FIELDS, NCLUS, ELEM).transpose(2, 0, 1, 3)
    half_band = NEAR // 2

    def one_row(row_index):

        def add_near(total, slot):
            target = (row_index + slot - half_band) % NCLUS
            term = lax.cond(flags[row_index, slot] == 1, lambda operand: dense_term(operand, near_blocks[row_index, slot].astype(jnp.float32)), lambda operand: jnp.zeros((2, FIELDS, ELEM), jnp.float32), pieces[target])
            return (total + term, None)

        def add_far(total, column_index):
            offset = (column_index - row_index + half_band) % NCLUS
            is_near = (offset < NEAR) & (flags[row_index, jnp.minimum(offset, NEAR - 1)] == 1)
            term = lax.cond(is_near, lambda operand: jnp.zeros((2, FIELDS, ELEM), jnp.float32), lambda operand: lowrank_term(operand, left_factors[row_index, column_index].astype(jnp.float32), right_factors[row_index, column_index].astype(jnp.float32), ranks[row_index, column_index]), pieces[column_index])
            return (total + term, None)
        total, _ = lax.scan(add_near, jnp.zeros((2, FIELDS, ELEM), jnp.float32), jnp.arange(NEAR, dtype=jnp.int32))
        total, _ = lax.scan(add_far, total, jnp.arange(NCLUS, dtype=jnp.int32))
        return total
    rows = lax.map(one_row, jnp.arange(NCLUS, dtype=jnp.int32))
    products = rows.transpose(1, 2, 0, 3).reshape(2, FIELDS, NELEM)
    return products + diagonal[None, None, :] * vector

def inner_products(first, second):
    return jnp.einsum('csn,ctn->st', first, second, precision=highest)

def combine_rows(matrix, vectors):
    return jnp.einsum('st,ctn->csn', matrix, vectors, precision=highest)

def matmul(left, right):
    return jnp.dot(left, right, precision=highest)

def lower_inverse(lower):
    identity = jnp.eye(lower.shape[0], dtype=lower.dtype)
    return lax.linalg.triangular_solve(lower, identity, left_side=True, lower=True)

def project(harmonics, vectors):

    def contract(left, right):
        return jnp.einsum('mn,sn->ms', left, right, precision=highest)
    real_out = contract(harmonics[0], vectors[0]) + contract(harmonics[1], vectors[1])
    imag_out = contract(harmonics[0], vectors[1]) - contract(harmonics[1], vectors[0])
    return jnp.stack([real_out, imag_out])

def reference(incident, diagonal, near_blocks, left_factors, right_factors, flags, ranks, harmonics):

    def operator(vector):
        return apply_operator(vector, diagonal, near_blocks, left_factors, right_factors, flags, ranks)
    lower_first = jnp.linalg.cholesky(inner_products(incident, incident))
    basis_one = combine_rows(lower_inverse(lower_first), incident)
    image = operator(basis_one)
    coupling_one = inner_products(image, basis_one)
    rest = image - combine_rows(coupling_one, basis_one)
    gram_one = inner_products(rest, rest)
    lower_second = jnp.linalg.cholesky(gram_one)
    basis_two = combine_rows(lower_inverse(lower_second), rest)
    image = operator(basis_two)
    coupling_onetwo = inner_products(image, basis_one)
    coupling_two = inner_products(image, basis_two)
    rest = image - combine_rows(coupling_onetwo, basis_one) - combine_rows(coupling_two, basis_two)
    gram_two = inner_products(rest, rest)
    upper_left = matmul(coupling_one, coupling_one.T) + gram_one
    upper_right = matmul(coupling_one, coupling_onetwo.T) + matmul(lower_second, coupling_two.T)
    lower_right = matmul(coupling_onetwo, coupling_onetwo.T) + matmul(coupling_two, coupling_two.T) + gram_two
    normal = jnp.concatenate([jnp.concatenate([upper_left, upper_right], axis=1), jnp.concatenate([upper_right.T, lower_right], axis=1)], axis=0)
    target = jnp.concatenate([matmul(lower_first, coupling_one.T), matmul(lower_first, coupling_onetwo.T)], axis=1)
    factor_inverse = lower_inverse(jnp.linalg.cholesky(normal))
    weights = matmul(factor_inverse.T, matmul(factor_inverse, target.T)).T
    solution = combine_rows(weights[:, :FIELDS], basis_one) + combine_rows(weights[:, FIELDS:], basis_two)
    return (solution, project(harmonics, solution))
```

```python
from functools import partial

import jax
import jax.numpy as jnp
from jax import lax
from jax.experimental import pallas as pl
from jax.experimental.pallas import tpu as pltpu
from jax.sharding import PartitionSpec as P

highest = lax.Precision.HIGHEST
MESH = pl.DeviceIdType.MESH


def allreduce_kernel(n, x_ref, o_ref, buf, send_sems, recv_sems):
    me = lax.axis_index("row")
    col = lax.axis_index("col")
    barrier = pltpu.get_barrier_semaphore()
    for d in range(1, n):
        pl.semaphore_signal(
            barrier, inc=1, device_id=(lax.rem(me + d, n), col), device_id_type=MESH
        )
    pl.semaphore_wait(barrier, n - 1)
    copies = []
    for d in range(1, n):
        copy = pltpu.make_async_remote_copy(
            src_ref=x_ref,
            dst_ref=buf.at[d],
            send_sem=send_sems.at[d],
            recv_sem=recv_sems.at[d],
            device_id=(lax.rem(me + d, n), col),
            device_id_type=MESH,
        )
        copy.start()
        copies.append(copy)
    buf[0] = x_ref[...]
    for copy in copies:
        copy.wait()
    total = buf[me]
    for source in range(1, n):
        total = total + buf[lax.rem(me + n - source, n)]
    o_ref[...] = total


def row_allreduce(packed, collective_id):
    n = lax.axis_size("row")
    rows, lanes = packed.shape
    return pl.pallas_call(
        partial(allreduce_kernel, n),
        out_shape=jax.ShapeDtypeStruct((rows, lanes), jnp.float32),
        in_specs=[pl.BlockSpec(memory_space=pltpu.VMEM)],
        out_specs=pl.BlockSpec(memory_space=pltpu.VMEM),
        scratch_shapes=[
            pltpu.VMEM((n, rows, lanes), jnp.float32),
            pltpu.SemaphoreType.DMA((n,)),
            pltpu.SemaphoreType.DMA((n,)),
        ],
        compiler_params=pltpu.CompilerParams(collective_id=collective_id, has_side_effects=True),
    )(packed)


def row_psum(ids, *arrays):
    flat = [a.reshape(-1) for a in arrays]
    sizes = [f.shape[0] for f in flat]
    total = sum(sizes)
    padded = -(-total // 1024) * 1024
    packed = jnp.concatenate(flat + [jnp.zeros((padded - total,), jnp.float32)]).reshape(-1, 128)
    summed = row_allreduce(packed, len(ids)).reshape(-1)
    ids.append(None)
    outs = []
    start = 0
    for a, size in zip(arrays, sizes):
        outs.append(summed[start : start + size].reshape(a.shape))
        start += size
    return outs[0] if len(outs) == 1 else tuple(outs)


def dense_term(vector, block):

    def product(left, right):
        return jnp.einsum("sf,ef->se", left, right, preferred_element_type=jnp.float32)

    real_out = product(vector[0], block[0]) - product(vector[1], block[1])
    imag_out = product(vector[0], block[1]) + product(vector[1], block[0])
    return jnp.stack([real_out, imag_out])


def lowrank_term(vector, left_block, right_block, rank):

    def inner(left, right):
        return jnp.einsum("sf,rf->sr", left, right, preferred_element_type=jnp.float32)

    def outer(left, right):
        return jnp.einsum("sr,re->se", left, right, preferred_element_type=jnp.float32)

    coeff_real = inner(vector[0], right_block[0]) - inner(vector[1], right_block[1])
    coeff_imag = inner(vector[0], right_block[1]) + inner(vector[1], right_block[0])
    keep = (jnp.arange(right_block.shape[1], dtype=jnp.int32) < rank)[None, None, :]
    coeffs = jnp.where(keep, jnp.stack([coeff_real, coeff_imag]), 0.0).astype(jnp.bfloat16)
    real_out = outer(coeffs[0], left_block[0]) - outer(coeffs[1], left_block[1])
    imag_out = outer(coeffs[0], left_block[1]) + outer(coeffs[1], left_block[0])
    return jnp.stack([real_out, imag_out])


def inner_products(first, second):
    return jnp.einsum("csn,ctn->st", first, second, precision=highest)


def combine_rows(matrix, vectors):
    return jnp.einsum("st,ctn->csn", matrix, vectors, precision=highest)


def matmul(left, right):
    return jnp.dot(left, right, precision=highest)


def lower_inverse(lower):
    identity = jnp.eye(lower.shape[0], dtype=lower.dtype)
    return lax.linalg.triangular_solve(lower, identity, left_side=True, lower=True)


def project(harmonics, vectors):

    def contract(left, right):
        return jnp.einsum("mn,sn->ms", left, right, precision=highest)

    real_out = contract(harmonics[0], vectors[0]) + contract(harmonics[1], vectors[1])
    imag_out = contract(harmonics[0], vectors[1]) - contract(harmonics[1], vectors[0])
    return jnp.stack([real_out, imag_out])


def body(incident, diagonal, near_blocks, left_factors, right_factors, flags, ranks, harmonics):
    blocks = left_factors.shape[1]
    slots = near_blocks.shape[1]
    width = near_blocks.shape[4]
    half_band = slots // 2
    elements = incident.shape[2]
    fields = incident.shape[1]
    clusters = lax.axis_size("row")
    row_index = lax.axis_index("row")
    column = lax.axis_index("col")
    empty = jnp.zeros((2, fields, elements), jnp.float32)
    ids = []

    def far_term(number, piece):
        cluster = column * blocks + number
        offset = (cluster - row_index + half_band) % clusters
        is_near = (offset < slots) & (flags[0, jnp.minimum(offset, slots - 1)] == 1)
        return lax.cond(
            is_near,
            lambda operand: empty,
            partial(
                lowrank_term,
                left_block=left_factors[0, number],
                right_block=right_factors[0, number],
                rank=ranks[0, number],
            ),
            piece,
        )

    def near_term(slot, piece):
        return lax.cond(
            flags[0, slot] == 1,
            partial(dense_term, block=near_blocks[0, slot]),
            lambda operand: empty,
            piece,
        )

    def apply_operator(vector):
        rounded = vector.astype(jnp.bfloat16)
        gathered = lax.all_gather(rounded, "row", axis=2, tiled=True)
        far_pieces = [
            lax.dynamic_slice_in_dim(gathered, (column * blocks + number) * elements, elements, 2)
            for number in range(blocks)
        ]
        near_pieces = [
            lax.dynamic_slice_in_dim(
                gathered,
                (row_index + slot - half_band) % clusters * elements + column * width,
                width,
                2,
            )
            for slot in range(slots)
        ]
        total = near_term(0, near_pieces[0])
        for slot in range(1, slots):
            total = total + near_term(slot, near_pieces[slot])
        for number in range(blocks):
            total = total + far_term(number, far_pieces[number])
        summed = lax.psum(total, "col")
        return summed + diagonal[None, None, :] * vector

    lower_first = jnp.linalg.cholesky(row_psum(ids, inner_products(incident, incident)))
    basis_one = combine_rows(lower_inverse(lower_first), incident)
    image = apply_operator(basis_one)
    coupling_one = row_psum(ids, inner_products(image, basis_one))
    rest = image - combine_rows(coupling_one, basis_one)
    gram_one = row_psum(ids, inner_products(rest, rest))
    lower_second = jnp.linalg.cholesky(gram_one)
    basis_two = combine_rows(lower_inverse(lower_second), rest)
    image = apply_operator(basis_two)
    coupling_onetwo, coupling_two = row_psum(
        ids, inner_products(image, basis_one), inner_products(image, basis_two)
    )
    rest = image - combine_rows(coupling_onetwo, basis_one) - combine_rows(coupling_two, basis_two)
    gram_two = row_psum(ids, inner_products(rest, rest))
    upper_left = matmul(coupling_one, coupling_one.T) + gram_one
    upper_right = matmul(coupling_one, coupling_onetwo.T) + matmul(lower_second, coupling_two.T)
    lower_right = (
        matmul(coupling_onetwo, coupling_onetwo.T) + matmul(coupling_two, coupling_two.T) + gram_two
    )
    normal = jnp.concatenate(
        [
            jnp.concatenate([upper_left, upper_right], axis=1),
            jnp.concatenate([upper_right.T, lower_right], axis=1),
        ],
        axis=0,
    )
    target = jnp.concatenate(
        [matmul(lower_first, coupling_one.T), matmul(lower_first, coupling_onetwo.T)], axis=1
    )
    factor_inverse = lower_inverse(jnp.linalg.cholesky(normal))
    weights = matmul(factor_inverse.T, matmul(factor_inverse, target.T)).T
    first_weights = weights[:, :fields]
    second_weights = weights[:, fields:]
    solution = combine_rows(first_weights, basis_one) + combine_rows(second_weights, basis_two)
    coefficients = row_psum(ids, project(harmonics, solution))
    return (solution, coefficients)


def solution(mesh):
    in_specs = (
        P(None, None, "row"),
        P("row"),
        P("row", None, None, None, "col"),
        P("row", "col", None, None, None),
        P("row", "col", None, None, None),
        P("row", None),
        P("row", "col"),
        P(None, None, "row"),
    )
    out_specs = (P(None, None, "row"), P())
    return jax.shard_map(body, mesh=mesh, in_specs=in_specs, out_specs=out_specs, check_vma=False)
```

```python
from functools import partial

import jax
import jax.numpy as jnp
from jax import lax
from jax.experimental import pallas as pl
from jax.experimental.pallas import tpu as pltpu
from jax.sharding import PartitionSpec as P

highest = lax.Precision.HIGHEST
MESH = pl.DeviceIdType.MESH


def allreduce_kernel(n, x_ref, o_ref, buf, send_sems, recv_sems):
    me = lax.axis_index("row")
    col = lax.axis_index("col")
    barrier = pltpu.get_barrier_semaphore()

    def peer(d):
        return (lax.rem(me + d, n), col)

    def copy(d):
        return pltpu.make_async_remote_copy(
            src_ref=x_ref,
            dst_ref=buf.at[d],
            send_sem=send_sems.at[d],
            recv_sem=recv_sems.at[d],
            device_id=peer(d),
            device_id_type=MESH,
        )

    def greet(d, carry):
        pl.semaphore_signal(barrier, inc=1, device_id=peer(d), device_id_type=MESH)
        return carry

    def start(d, carry):
        copy(d).start()
        return carry

    def finish(d, carry):
        copy(d).wait()
        return carry

    def add(source, total):
        return total + buf[lax.rem(me + n - source, n)]

    lax.fori_loop(1, n, greet, 0)
    pl.semaphore_wait(barrier, n - 1)
    lax.fori_loop(1, n, start, 0)
    buf[0] = x_ref[...]
    lax.fori_loop(1, n, finish, 0)
    o_ref[...] = lax.fori_loop(1, n, add, buf[me])


def row_allreduce(packed, collective_id):
    n = lax.axis_size("row")
    rows, lanes = packed.shape
    return pl.pallas_call(
        partial(allreduce_kernel, n),
        out_shape=jax.ShapeDtypeStruct((rows, lanes), jnp.float32),
        in_specs=[pl.BlockSpec(memory_space=pltpu.VMEM)],
        out_specs=pl.BlockSpec(memory_space=pltpu.VMEM),
        scratch_shapes=[
            pltpu.VMEM((n, rows, lanes), jnp.float32),
            pltpu.SemaphoreType.DMA((n,)),
            pltpu.SemaphoreType.DMA((n,)),
        ],
        compiler_params=pltpu.CompilerParams(collective_id=collective_id, has_side_effects=True),
    )(packed)


def row_psum(ids, *arrays):
    flat = [a.reshape(-1) for a in arrays]
    sizes = [f.shape[0] for f in flat]
    total = sum(sizes)
    padded = -(-total // 1024) * 1024
    packed = jnp.concatenate(flat + [jnp.zeros((padded - total,), jnp.float32)]).reshape(-1, 128)
    summed = row_allreduce(packed, len(ids)).reshape(-1)
    ids.append(None)
    outs = []
    start = 0
    for a, size in zip(arrays, sizes):
        outs.append(summed[start : start + size].reshape(a.shape))
        start += size
    return outs[0] if len(outs) == 1 else tuple(outs)


def complex_lhs(values, part_axis):
    real = jnp.take(values, 0, axis=part_axis)
    imag = jnp.take(values, 1, axis=part_axis)
    return jnp.stack([jnp.stack([real, -imag]), jnp.stack([imag, real])])


def inner_products(first, second):
    return jnp.einsum("csn,ctn->st", first, second, precision=highest)


def combine_rows(matrix, vectors):
    return jnp.einsum("st,ctn->csn", matrix, vectors, precision=highest)


def matmul(left, right):
    return jnp.dot(left, right, precision=highest)


def lower_inverse(lower):
    identity = jnp.eye(lower.shape[0], dtype=lower.dtype)
    return lax.linalg.triangular_solve(lower, identity, left_side=True, lower=True)


def project(harmonics, vectors):

    def contract(left, right):
        return jnp.einsum("mn,sn->ms", left, right, precision=highest)

    real_out = contract(harmonics[0], vectors[0]) + contract(harmonics[1], vectors[1])
    imag_out = contract(harmonics[0], vectors[1]) - contract(harmonics[1], vectors[0])
    return jnp.stack([real_out, imag_out])


def body(incident, diagonal, near_blocks, left_factors, right_factors, flags, ranks, harmonics):
    blocks = left_factors.shape[1]
    slots = near_blocks.shape[1]
    width = near_blocks.shape[4]
    half_band = slots // 2
    elements = incident.shape[2]
    fields = incident.shape[1]
    clusters = lax.axis_size("row")
    row_index = lax.axis_index("row")
    column = lax.axis_index("col")
    ids = []

    def operator_terms(near_pieces, far_pieces):
        near_on = flags[0] == 1
        near_vector = jnp.where(near_on[:, None, None, None], near_pieces, 0).astype(jnp.bfloat16)
        near_out = jnp.einsum(
            "caksf,kaef->cse",
            complex_lhs(near_vector, 1),
            near_blocks[0],
            preferred_element_type=jnp.float32,
        )
        cluster = column * blocks + jnp.arange(blocks, dtype=jnp.int32)
        offset = (cluster - row_index + half_band) % clusters
        is_near = (offset < slots) & (flags[0, jnp.minimum(offset, slots - 1)] == 1)
        keep = (~is_near)[:, None] & (
            jnp.arange(right_factors.shape[3], dtype=jnp.int32)[None, :] < ranks[0][:, None]
        )
        coeffs = jnp.einsum(
            "cansf,narf->cnsr",
            complex_lhs(far_pieces, 1),
            right_factors[0],
            preferred_element_type=jnp.float32,
        )
        coeffs = jnp.where(keep[None, :, None, :], coeffs, 0.0).astype(jnp.bfloat16)
        far_out = jnp.einsum(
            "cansr,nare->cse",
            complex_lhs(coeffs, 0),
            left_factors[0],
            preferred_element_type=jnp.float32,
        )
        return near_out + far_out

    def apply_operator(vector):
        rounded = vector.astype(jnp.bfloat16)
        gathered = lax.all_gather(rounded, "row", axis=2, tiled=True)
        far_pieces = jnp.stack(
            [
                lax.dynamic_slice_in_dim(gathered, (column * blocks + number) * elements, elements, 2)
                for number in range(blocks)
            ]
        )
        near_pieces = jnp.stack(
            [
                lax.dynamic_slice_in_dim(
                    gathered,
                    (row_index + slot - half_band) % clusters * elements + column * width,
                    width,
                    2,
                )
                for slot in range(slots)
            ]
        )
        total = operator_terms(near_pieces, far_pieces)
        summed = lax.psum(total, "col")
        return summed + diagonal[None, None, :] * vector

    lower_first = jnp.linalg.cholesky(row_psum(ids, inner_products(incident, incident)))
    basis_one = combine_rows(lower_inverse(lower_first), incident)
    image = apply_operator(basis_one)
    coupling_one = row_psum(ids, inner_products(image, basis_one))
    rest = image - combine_rows(coupling_one, basis_one)
    gram_one = row_psum(ids, inner_products(rest, rest))
    lower_second = jnp.linalg.cholesky(gram_one)
    basis_two = combine_rows(lower_inverse(lower_second), rest)
    image = apply_operator(basis_two)
    coupling_onetwo, coupling_two = row_psum(
        ids, inner_products(image, basis_one), inner_products(image, basis_two)
    )
    rest = image - combine_rows(coupling_onetwo, basis_one) - combine_rows(coupling_two, basis_two)
    gram_two = row_psum(ids, inner_products(rest, rest))
    upper_left = matmul(coupling_one, coupling_one.T) + gram_one
    upper_right = matmul(coupling_one, coupling_onetwo.T) + matmul(lower_second, coupling_two.T)
    lower_right = (
        matmul(coupling_onetwo, coupling_onetwo.T) + matmul(coupling_two, coupling_two.T) + gram_two
    )
    normal = jnp.concatenate(
        [
            jnp.concatenate([upper_left, upper_right], axis=1),
            jnp.concatenate([upper_right.T, lower_right], axis=1),
        ],
        axis=0,
    )
    target = jnp.concatenate(
        [matmul(lower_first, coupling_one.T), matmul(lower_first, coupling_onetwo.T)], axis=1
    )
    factor_inverse = lower_inverse(jnp.linalg.cholesky(normal))
    weights = matmul(factor_inverse.T, matmul(factor_inverse, target.T)).T
    first_weights = weights[:, :fields]
    second_weights = weights[:, fields:]
    solution = combine_rows(first_weights, basis_one) + combine_rows(second_weights, basis_two)
    coefficients = row_psum(ids, project(harmonics, solution))
    return (solution, coefficients)


def solution(mesh):
    in_specs = (
        P(None, None, "row"),
        P("row"),
        P("row", None, None, None, "col"),
        P("row", "col", None, None, None),
        P("row", "col", None, None, None),
        P("row", None),
        P("row", "col"),
        P(None, None, "row"),
    )
    out_specs = (P(None, None, "row"), P())
    return jax.shard_map(body, mesh=mesh, in_specs=in_specs, out_specs=out_specs, check_vma=False)
```

```python
from functools import partial

import jax
import jax.numpy as jnp
from jax import lax
from jax.experimental import pallas as pl
from jax.experimental.pallas import tpu as pltpu
from jax.sharding import PartitionSpec as P

highest = lax.Precision.HIGHEST
MESH = pl.DeviceIdType.MESH


def allreduce_kernel(n, x_ref, o_ref, buf, send_sems, recv_sems):
    me = lax.axis_index("row")
    col = lax.axis_index("col")
    barrier = pltpu.get_barrier_semaphore()

    def peer(d):
        return (lax.rem(me + d, n), col)

    def copy(d):
        return pltpu.make_async_remote_copy(
            src_ref=x_ref,
            dst_ref=buf.at[d],
            send_sem=send_sems.at[d],
            recv_sem=recv_sems.at[d],
            device_id=peer(d),
            device_id_type=MESH,
        )

    def greet(d, carry):
        pl.semaphore_signal(barrier, inc=1, device_id=peer(d), device_id_type=MESH)
        return carry

    def start(d, carry):
        copy(d).start()
        return carry

    def finish(d, carry):
        copy(d).wait()
        return carry

    def add(source, total):
        return total + buf[lax.rem(me + n - source, n)]

    lax.fori_loop(1, n, greet, 0)
    pl.semaphore_wait(barrier, n - 1)
    lax.fori_loop(1, n, start, 0)
    buf[0] = x_ref[...]
    lax.fori_loop(1, n, finish, 0)
    o_ref[...] = lax.fori_loop(1, n, add, buf[me])


def row_allreduce(packed, collective_id):
    n = lax.axis_size("row")
    rows, lanes = packed.shape
    return pl.pallas_call(
        partial(allreduce_kernel, n),
        out_shape=jax.ShapeDtypeStruct((rows, lanes), jnp.float32),
        in_specs=[pl.BlockSpec(memory_space=pltpu.VMEM)],
        out_specs=pl.BlockSpec(memory_space=pltpu.VMEM),
        scratch_shapes=[
            pltpu.VMEM((n, rows, lanes), jnp.float32),
            pltpu.SemaphoreType.DMA((n,)),
            pltpu.SemaphoreType.DMA((n,)),
        ],
        compiler_params=pltpu.CompilerParams(collective_id=collective_id, has_side_effects=True),
    )(packed)


def gather_kernel(rows, cols, blocks, half, v_ref, near_ref, far_ref, slices, far_buf,
                  first_send, first_recv, second_send, second_recv, local_sems):
    me = lax.axis_index("row")
    col = lax.axis_index("col")
    width = slices.shape[-1]
    barrier = pltpu.get_barrier_semaphore()

    def row_peer(d):
        return (lax.rem(me + d, rows), col)

    def col_peer(e):
        return (me, lax.rem(col + e, cols))

    def window(c):
        return pl.ds(pl.multiple_of(c * width, width), width)

    own = v_ref.at[:, :, window(col)]

    def first(d):
        return pltpu.make_async_remote_copy(
            src_ref=own,
            dst_ref=slices.at[d],
            send_sem=first_send.at[d],
            recv_sem=first_recv.at[d],
            device_id=row_peer(d),
            device_id_type=MESH,
        )

    def second(t):
        e = 1 + t // blocks
        n = t % blocks
        target = lax.rem(col + e, cols)
        slot = lax.rem(me + rows - blocks * target - n, rows)
        return pltpu.make_async_remote_copy(
            src_ref=slices.at[slot],
            dst_ref=far_buf.at[n, :, :, window(col)],
            send_sem=second_send.at[t],
            recv_sem=second_recv.at[t],
            device_id=col_peer(e),
            device_id_type=MESH,
        )

    def greet_row(d, carry):
        pl.semaphore_signal(barrier, inc=1, device_id=row_peer(d), device_id_type=MESH)
        return carry

    def greet_col(e, carry):
        pl.semaphore_signal(barrier, inc=1, device_id=col_peer(e), device_id_type=MESH)
        return carry

    def start_first(d, carry):
        first(d).start()
        return carry

    def finish_first(d, carry):
        first(d).wait()
        return carry

    def start_second(t, carry):
        second(t).start()
        return carry

    def finish_second(t, carry):
        second(t).wait()
        return carry

    lax.fori_loop(1, rows, greet_row, 0)
    lax.fori_loop(1, cols, greet_col, 0)
    pl.semaphore_wait(barrier, rows - 1 + cols - 1)
    lax.fori_loop(1, rows, start_first, 0)
    local = pltpu.make_async_copy(own, slices.at[0], local_sems.at[blocks])
    local.start()
    lax.fori_loop(1, rows, finish_first, 0)
    local.wait()
    lax.fori_loop(0, (cols - 1) * blocks, start_second, 0)
    mine = []
    for n in range(blocks):
        slot = lax.rem(me + rows - blocks * col - n, rows)
        copy = pltpu.make_async_copy(slices.at[slot], far_buf.at[n, :, :, window(col)], local_sems.at[n])
        copy.start()
        mine.append(copy)
    for k in range(2 * half):
        near_ref[k] = slices[(half - k) % rows]
    lax.fori_loop(0, (cols - 1) * blocks, finish_second, 0)
    for copy in mine:
        copy.wait()
    far_ref[...] = far_buf[...]


def gather_pieces(vector, blocks, half, width, collective_id):
    rows = lax.axis_size("row")
    cols = lax.axis_size("col")
    parts, fields, elements = vector.shape
    return pl.pallas_call(
        partial(gather_kernel, rows, cols, blocks, half),
        out_shape=(
            jax.ShapeDtypeStruct((2 * half, parts, fields, width), vector.dtype),
            jax.ShapeDtypeStruct((blocks, parts, fields, elements), vector.dtype),
        ),
        in_specs=[pl.BlockSpec(memory_space=pltpu.VMEM)],
        out_specs=(pl.BlockSpec(memory_space=pltpu.VMEM), pl.BlockSpec(memory_space=pltpu.VMEM)),
        scratch_shapes=[
            pltpu.VMEM((rows, parts, fields, width), vector.dtype),
            pltpu.VMEM((blocks, parts, fields, elements), vector.dtype),
            pltpu.SemaphoreType.DMA((rows,)),
            pltpu.SemaphoreType.DMA((rows,)),
            pltpu.SemaphoreType.DMA(((cols - 1) * blocks,)),
            pltpu.SemaphoreType.DMA(((cols - 1) * blocks,)),
            pltpu.SemaphoreType.DMA((blocks + 1,)),
        ],
        compiler_params=pltpu.CompilerParams(collective_id=collective_id, has_side_effects=True),
    )(vector)


def row_psum(ids, *arrays):
    flat = [a.reshape(-1) for a in arrays]
    sizes = [f.shape[0] for f in flat]
    total = sum(sizes)
    padded = -(-total // 1024) * 1024
    packed = jnp.concatenate(flat + [jnp.zeros((padded - total,), jnp.float32)]).reshape(-1, 128)
    summed = row_allreduce(packed, len(ids)).reshape(-1)
    ids.append(None)
    outs = []
    start = 0
    for a, size in zip(arrays, sizes):
        outs.append(summed[start : start + size].reshape(a.shape))
        start += size
    return outs[0] if len(outs) == 1 else tuple(outs)


def complex_lhs(values, part_axis):
    real = jnp.take(values, 0, axis=part_axis)
    imag = jnp.take(values, 1, axis=part_axis)
    return jnp.stack([jnp.stack([real, -imag]), jnp.stack([imag, real])])


def inner_products(first, second):
    return jnp.einsum("csn,ctn->st", first, second, precision=highest)


def combine_rows(matrix, vectors):
    return jnp.einsum("st,ctn->csn", matrix, vectors, precision=highest)


def matmul(left, right):
    return jnp.dot(left, right, precision=highest)


def lower_inverse(lower):
    identity = jnp.eye(lower.shape[0], dtype=lower.dtype)
    return lax.linalg.triangular_solve(lower, identity, left_side=True, lower=True)


def project(harmonics, vectors):

    def contract(left, right):
        return jnp.einsum("mn,sn->ms", left, right, precision=highest)

    real_out = contract(harmonics[0], vectors[0]) + contract(harmonics[1], vectors[1])
    imag_out = contract(harmonics[0], vectors[1]) - contract(harmonics[1], vectors[0])
    return jnp.stack([real_out, imag_out])


def body(incident, diagonal, near_blocks, left_factors, right_factors, flags, ranks, harmonics):
    blocks = left_factors.shape[1]
    slots = near_blocks.shape[1]
    width = near_blocks.shape[4]
    half_band = slots // 2
    elements = incident.shape[2]
    fields = incident.shape[1]
    clusters = lax.axis_size("row")
    row_index = lax.axis_index("row")
    column = lax.axis_index("col")
    ids = []

    def operator_terms(near_pieces, far_pieces):
        near_on = flags[0] == 1
        near_vector = jnp.where(near_on[:, None, None, None], near_pieces, 0).astype(jnp.bfloat16)
        near_out = jnp.einsum(
            "caksf,kaef->cse",
            complex_lhs(near_vector, 1),
            near_blocks[0],
            preferred_element_type=jnp.float32,
        )
        cluster = column * blocks + jnp.arange(blocks, dtype=jnp.int32)
        offset = (cluster - row_index + half_band) % clusters
        is_near = (offset < slots) & (flags[0, jnp.minimum(offset, slots - 1)] == 1)
        keep = (~is_near)[:, None] & (
            jnp.arange(right_factors.shape[3], dtype=jnp.int32)[None, :] < ranks[0][:, None]
        )
        coeffs = jnp.einsum(
            "cansf,narf->cnsr",
            complex_lhs(far_pieces, 1),
            right_factors[0],
            preferred_element_type=jnp.float32,
        )
        coeffs = jnp.where(keep[None, :, None, :], coeffs, 0.0).astype(jnp.bfloat16)
        far_out = jnp.einsum(
            "cansr,nare->cse",
            complex_lhs(coeffs, 0),
            left_factors[0],
            preferred_element_type=jnp.float32,
        )
        return near_out + far_out

    def apply_operator(vector):
        rounded = vector.astype(jnp.bfloat16)
        near_pieces, far_pieces = gather_pieces(rounded, blocks, half_band, width, 16 + len(ids))
        ids.append(None)
        total = operator_terms(near_pieces, far_pieces)
        summed = lax.psum(total, "col")
        return summed + diagonal[None, None, :] * vector

    lower_first = jnp.linalg.cholesky(row_psum(ids, inner_products(incident, incident)))
    basis_one = combine_rows(lower_inverse(lower_first), incident)
    image = apply_operator(basis_one)
    coupling_one = row_psum(ids, inner_products(image, basis_one))
    rest = image - combine_rows(coupling_one, basis_one)
    gram_one = row_psum(ids, inner_products(rest, rest))
    lower_second = jnp.linalg.cholesky(gram_one)
    basis_two = combine_rows(lower_inverse(lower_second), rest)
    image = apply_operator(basis_two)
    coupling_onetwo, coupling_two = row_psum(
        ids, inner_products(image, basis_one), inner_products(image, basis_two)
    )
    rest = image - combine_rows(coupling_onetwo, basis_one) - combine_rows(coupling_two, basis_two)
    gram_two = row_psum(ids, inner_products(rest, rest))
    upper_left = matmul(coupling_one, coupling_one.T) + gram_one
    upper_right = matmul(coupling_one, coupling_onetwo.T) + matmul(lower_second, coupling_two.T)
    lower_right = (
        matmul(coupling_onetwo, coupling_onetwo.T) + matmul(coupling_two, coupling_two.T) + gram_two
    )
    normal = jnp.concatenate(
        [
            jnp.concatenate([upper_left, upper_right], axis=1),
            jnp.concatenate([upper_right.T, lower_right], axis=1),
        ],
        axis=0,
    )
    target = jnp.concatenate(
        [matmul(lower_first, coupling_one.T), matmul(lower_first, coupling_onetwo.T)], axis=1
    )
    factor_inverse = lower_inverse(jnp.linalg.cholesky(normal))
    weights = matmul(factor_inverse.T, matmul(factor_inverse, target.T)).T
    first_weights = weights[:, :fields]
    second_weights = weights[:, fields:]
    solution = combine_rows(first_weights, basis_one) + combine_rows(second_weights, basis_two)
    coefficients = row_psum(ids, project(harmonics, solution))
    return (solution, coefficients)


def solution(mesh):
    in_specs = (
        P(None, None, "row"),
        P("row"),
        P("row", None, None, None, "col"),
        P("row", "col", None, None, None),
        P("row", "col", None, None, None),
        P("row", None),
        P("row", "col"),
        P(None, None, "row"),
    )
    out_specs = (P(None, None, "row"), P())
    return jax.shard_map(body, mesh=mesh, in_specs=in_specs, out_specs=out_specs, check_vma=False)
```

```python
from functools import partial

import jax
import jax.numpy as jnp
from jax import lax
from jax.experimental import pallas as pl
from jax.experimental.pallas import tpu as pltpu
from jax.sharding import PartitionSpec as P

highest = lax.Precision.HIGHEST
MESH = pl.DeviceIdType.MESH


def allreduce_kernel(n, x_ref, o_ref, buf, send_sems, recv_sems):
    me = lax.axis_index("row")
    col = lax.axis_index("col")
    barrier = pltpu.get_barrier_semaphore()

    def peer(d):
        return (lax.rem(me + d, n), col)

    def copy(d):
        return pltpu.make_async_remote_copy(
            src_ref=x_ref,
            dst_ref=buf.at[d],
            send_sem=send_sems.at[d],
            recv_sem=recv_sems.at[d],
            device_id=peer(d),
            device_id_type=MESH,
        )

    def greet(d, carry):
        pl.semaphore_signal(barrier, inc=1, device_id=peer(d), device_id_type=MESH)
        return carry

    def start(d, carry):
        copy(d).start()
        return carry

    def finish(d, carry):
        copy(d).wait()
        return carry

    def add(source, total):
        return total + buf[lax.rem(me + n - source, n)]

    lax.fori_loop(1, n, greet, 0)
    pl.semaphore_wait(barrier, n - 1)
    lax.fori_loop(1, n, start, 0)
    buf[0] = x_ref[...]
    lax.fori_loop(1, n, finish, 0)
    o_ref[...] = lax.fori_loop(1, n, add, buf[me])


def row_allreduce(packed, collective_id):
    n = lax.axis_size("row")
    rows, lanes = packed.shape
    return pl.pallas_call(
        partial(allreduce_kernel, n),
        out_shape=jax.ShapeDtypeStruct((rows, lanes), jnp.float32),
        in_specs=[pl.BlockSpec(memory_space=pltpu.VMEM)],
        out_specs=pl.BlockSpec(memory_space=pltpu.VMEM),
        scratch_shapes=[
            pltpu.VMEM((n, rows, lanes), jnp.float32),
            pltpu.SemaphoreType.DMA((n,)),
            pltpu.SemaphoreType.DMA((n,)),
        ],
        compiler_params=pltpu.CompilerParams(collective_id=collective_id, has_side_effects=True),
    )(packed)


def gather_kernel(rows, cols, blocks, half, v_ref, near_ref, far_ref, slices, far_buf,
                  first_send, first_recv, second_send, second_recv, local_sems):
    me = lax.axis_index("row")
    col = lax.axis_index("col")
    width = slices.shape[-1]
    barrier = pltpu.get_barrier_semaphore()

    def row_peer(d):
        return (lax.rem(me + d, rows), col)

    def col_peer(e):
        return (me, lax.rem(col + e, cols))

    def window(c):
        return pl.ds(pl.multiple_of(c * width, width), width)

    own = v_ref.at[:, :, window(col)]

    def first(d):
        return pltpu.make_async_remote_copy(
            src_ref=own,
            dst_ref=slices.at[d],
            send_sem=first_send.at[d],
            recv_sem=first_recv.at[d],
            device_id=row_peer(d),
            device_id_type=MESH,
        )

    def second(t):
        e = 1 + t // blocks
        n = t % blocks
        target = lax.rem(col + e, cols)
        slot = lax.rem(me + rows - blocks * target - n, rows)
        return pltpu.make_async_remote_copy(
            src_ref=slices.at[slot],
            dst_ref=far_buf.at[n, :, :, window(col)],
            send_sem=second_send.at[t],
            recv_sem=second_recv.at[t],
            device_id=col_peer(e),
            device_id_type=MESH,
        )

    def greet_row(d, carry):
        pl.semaphore_signal(barrier, inc=1, device_id=row_peer(d), device_id_type=MESH)
        return carry

    def greet_col(e, carry):
        pl.semaphore_signal(barrier, inc=1, device_id=col_peer(e), device_id_type=MESH)
        return carry

    def start_first(d, carry):
        first(d).start()
        return carry

    def finish_first(d, carry):
        first(d).wait()
        return carry

    def start_second(t, carry):
        second(t).start()
        return carry

    def finish_second(t, carry):
        second(t).wait()
        return carry

    lax.fori_loop(1, rows, greet_row, 0)
    lax.fori_loop(1, cols, greet_col, 0)
    pl.semaphore_wait(barrier, rows - 1 + cols - 1)
    lax.fori_loop(1, rows, start_first, 0)
    local = pltpu.make_async_copy(own, slices.at[0], local_sems.at[blocks])
    local.start()
    lax.fori_loop(1, rows, finish_first, 0)
    local.wait()
    lax.fori_loop(0, (cols - 1) * blocks, start_second, 0)
    mine = []
    for n in range(blocks):
        slot = lax.rem(me + rows - blocks * col - n, rows)
        copy = pltpu.make_async_copy(slices.at[slot], far_buf.at[n, :, :, window(col)], local_sems.at[n])
        copy.start()
        mine.append(copy)
    for k in range(2 * half):
        near_ref[k] = slices[(half - k) % rows]
    lax.fori_loop(0, (cols - 1) * blocks, finish_second, 0)
    for copy in mine:
        copy.wait()
    far_ref[...] = far_buf[...]


def gather_pieces(vector, blocks, half, width, collective_id):
    rows = lax.axis_size("row")
    cols = lax.axis_size("col")
    parts, fields, elements = vector.shape
    return pl.pallas_call(
        partial(gather_kernel, rows, cols, blocks, half),
        out_shape=(
            jax.ShapeDtypeStruct((2 * half, parts, fields, width), vector.dtype),
            jax.ShapeDtypeStruct((blocks, parts, fields, elements), vector.dtype),
        ),
        in_specs=[pl.BlockSpec(memory_space=pltpu.VMEM)],
        out_specs=(pl.BlockSpec(memory_space=pltpu.VMEM), pl.BlockSpec(memory_space=pltpu.VMEM)),
        scratch_shapes=[
            pltpu.VMEM((rows, parts, fields, width), vector.dtype),
            pltpu.VMEM((blocks, parts, fields, elements), vector.dtype),
            pltpu.SemaphoreType.DMA((rows,)),
            pltpu.SemaphoreType.DMA((rows,)),
            pltpu.SemaphoreType.DMA(((cols - 1) * blocks,)),
            pltpu.SemaphoreType.DMA(((cols - 1) * blocks,)),
            pltpu.SemaphoreType.DMA((blocks + 1,)),
        ],
        compiler_params=pltpu.CompilerParams(collective_id=collective_id, has_side_effects=True),
    )(vector)


def reduce_kernel(cols, x_ref, o_ref, parts_buf, full, first_send, first_recv, second_send, second_recv):
    me = lax.axis_index("row")
    col = lax.axis_index("col")
    width = parts_buf.shape[-1]
    barrier = pltpu.get_barrier_semaphore()

    def col_peer(e):
        return (me, lax.rem(col + e, cols))

    def window(c):
        return pl.ds(pl.multiple_of(c * width, width), width)

    def first(e):
        return pltpu.make_async_remote_copy(
            src_ref=x_ref.at[:, :, window(lax.rem(col + e, cols))],
            dst_ref=parts_buf.at[e],
            send_sem=first_send.at[e],
            recv_sem=first_recv.at[e],
            device_id=col_peer(e),
            device_id_type=MESH,
        )

    def second(e):
        return pltpu.make_async_remote_copy(
            src_ref=full.at[:, :, window(col)],
            dst_ref=full.at[:, :, window(col)],
            send_sem=second_send.at[e],
            recv_sem=second_recv.at[e],
            device_id=col_peer(e),
            device_id_type=MESH,
        )

    def greet(e, carry):
        pl.semaphore_signal(barrier, inc=1, device_id=col_peer(e), device_id_type=MESH)
        return carry

    def start_first(e, carry):
        first(e).start()
        return carry

    def finish_first(e, carry):
        first(e).wait()
        return carry

    def start_second(e, carry):
        second(e).start()
        return carry

    def finish_second(e, carry):
        second(e).wait_send()
        pltpu.make_async_remote_copy(
            src_ref=full.at[:, :, window(col)],
            dst_ref=full.at[:, :, window(lax.rem(col + cols - e, cols))],
            send_sem=second_send.at[e],
            recv_sem=second_recv.at[e],
            device_id=col_peer(e),
            device_id_type=MESH,
        ).wait_recv()
        return carry

    def add(source, total):
        return total + parts_buf[lax.rem(col + cols - source, cols)]

    lax.fori_loop(1, cols, greet, 0)
    pl.semaphore_wait(barrier, cols - 1)
    lax.fori_loop(1, cols, start_first, 0)
    parts_buf[0] = x_ref[:, :, window(col)]
    lax.fori_loop(1, cols, finish_first, 0)
    full[:, :, window(col)] = lax.fori_loop(1, cols, add, parts_buf[col])
    lax.fori_loop(1, cols, start_second, 0)
    lax.fori_loop(1, cols, finish_second, 0)
    o_ref[...] = full[...]


def col_reduce(partial_sum, collective_id):
    cols = lax.axis_size("col")
    parts, fields, elements = partial_sum.shape
    width = elements // cols
    return pl.pallas_call(
        partial(reduce_kernel, cols),
        out_shape=jax.ShapeDtypeStruct(partial_sum.shape, jnp.float32),
        in_specs=[pl.BlockSpec(memory_space=pltpu.VMEM)],
        out_specs=pl.BlockSpec(memory_space=pltpu.VMEM),
        scratch_shapes=[
            pltpu.VMEM((cols, parts, fields, width), jnp.float32),
            pltpu.VMEM((parts, fields, elements), jnp.float32),
            pltpu.SemaphoreType.DMA((cols,)),
            pltpu.SemaphoreType.DMA((cols,)),
            pltpu.SemaphoreType.DMA((cols,)),
            pltpu.SemaphoreType.DMA((cols,)),
        ],
        compiler_params=pltpu.CompilerParams(collective_id=collective_id, has_side_effects=True),
    )(partial_sum)


def row_psum(ids, *arrays):
    flat = [a.reshape(-1) for a in arrays]
    sizes = [f.shape[0] for f in flat]
    total = sum(sizes)
    padded = -(-total // 1024) * 1024
    packed = jnp.concatenate(flat + [jnp.zeros((padded - total,), jnp.float32)]).reshape(-1, 128)
    summed = row_allreduce(packed, len(ids)).reshape(-1)
    ids.append(None)
    outs = []
    start = 0
    for a, size in zip(arrays, sizes):
        outs.append(summed[start : start + size].reshape(a.shape))
        start += size
    return outs[0] if len(outs) == 1 else tuple(outs)


def complex_lhs(values, part_axis):
    real = jnp.take(values, 0, axis=part_axis)
    imag = jnp.take(values, 1, axis=part_axis)
    return jnp.stack([jnp.stack([real, -imag]), jnp.stack([imag, real])])


def inner_products(first, second):
    return jnp.einsum("csn,ctn->st", first, second, precision=highest)


def combine_rows(matrix, vectors):
    return jnp.einsum("st,ctn->csn", matrix, vectors, precision=highest)


def matmul(left, right):
    return jnp.dot(left, right, precision=highest)


def lower_inverse(lower):
    identity = jnp.eye(lower.shape[0], dtype=lower.dtype)
    return lax.linalg.triangular_solve(lower, identity, left_side=True, lower=True)


def project(harmonics, vectors):

    def contract(left, right):
        return jnp.einsum("mn,sn->ms", left, right, precision=highest)

    real_out = contract(harmonics[0], vectors[0]) + contract(harmonics[1], vectors[1])
    imag_out = contract(harmonics[0], vectors[1]) - contract(harmonics[1], vectors[0])
    return jnp.stack([real_out, imag_out])


def body(incident, diagonal, near_blocks, left_factors, right_factors, flags, ranks, harmonics):
    blocks = left_factors.shape[1]
    slots = near_blocks.shape[1]
    width = near_blocks.shape[4]
    half_band = slots // 2
    elements = incident.shape[2]
    fields = incident.shape[1]
    clusters = lax.axis_size("row")
    row_index = lax.axis_index("row")
    column = lax.axis_index("col")
    ids = []

    def operator_terms(near_pieces, far_pieces):
        near_on = flags[0] == 1
        near_vector = jnp.where(near_on[:, None, None, None], near_pieces, 0).astype(jnp.bfloat16)
        near_out = jnp.einsum(
            "caksf,kaef->cse",
            complex_lhs(near_vector, 1),
            near_blocks[0],
            preferred_element_type=jnp.float32,
        )
        cluster = column * blocks + jnp.arange(blocks, dtype=jnp.int32)
        offset = (cluster - row_index + half_band) % clusters
        is_near = (offset < slots) & (flags[0, jnp.minimum(offset, slots - 1)] == 1)
        keep = (~is_near)[:, None] & (
            jnp.arange(right_factors.shape[3], dtype=jnp.int32)[None, :] < ranks[0][:, None]
        )
        coeffs = jnp.einsum(
            "cansf,narf->cnsr",
            complex_lhs(far_pieces, 1),
            right_factors[0],
            preferred_element_type=jnp.float32,
        )
        coeffs = jnp.where(keep[None, :, None, :], coeffs, 0.0).astype(jnp.bfloat16)
        far_out = jnp.einsum(
            "cansr,nare->cse",
            complex_lhs(coeffs, 0),
            left_factors[0],
            preferred_element_type=jnp.float32,
        )
        return near_out + far_out

    def apply_operator(vector):
        rounded = vector.astype(jnp.bfloat16)
        near_pieces, far_pieces = gather_pieces(rounded, blocks, half_band, width, 16 + len(ids))
        ids.append(None)
        total = operator_terms(near_pieces, far_pieces)
        summed = col_reduce(total, 32 + len(ids))
        ids.append(None)
        return summed + diagonal[None, None, :] * vector

    lower_first = jnp.linalg.cholesky(row_psum(ids, inner_products(incident, incident)))
    basis_one = combine_rows(lower_inverse(lower_first), incident)
    image = apply_operator(basis_one)
    coupling_one = row_psum(ids, inner_products(image, basis_one))
    rest = image - combine_rows(coupling_one, basis_one)
    gram_one = row_psum(ids, inner_products(rest, rest))
    lower_second = jnp.linalg.cholesky(gram_one)
    basis_two = combine_rows(lower_inverse(lower_second), rest)
    image = apply_operator(basis_two)
    coupling_onetwo, coupling_two = row_psum(
        ids, inner_products(image, basis_one), inner_products(image, basis_two)
    )
    rest = image - combine_rows(coupling_onetwo, basis_one) - combine_rows(coupling_two, basis_two)
    gram_two = row_psum(ids, inner_products(rest, rest))
    upper_left = matmul(coupling_one, coupling_one.T) + gram_one
    upper_right = matmul(coupling_one, coupling_onetwo.T) + matmul(lower_second, coupling_two.T)
    lower_right = (
        matmul(coupling_onetwo, coupling_onetwo.T) + matmul(coupling_two, coupling_two.T) + gram_two
    )
    normal = jnp.concatenate(
        [
            jnp.concatenate([upper_left, upper_right], axis=1),
            jnp.concatenate([upper_right.T, lower_right], axis=1),
        ],
        axis=0,
    )
    target = jnp.concatenate(
        [matmul(lower_first, coupling_one.T), matmul(lower_first, coupling_onetwo.T)], axis=1
    )
    factor_inverse = lower_inverse(jnp.linalg.cholesky(normal))
    weights = matmul(factor_inverse.T, matmul(factor_inverse, target.T)).T
    first_weights = weights[:, :fields]
    second_weights = weights[:, fields:]
    solution = combine_rows(first_weights, basis_one) + combine_rows(second_weights, basis_two)
    coefficients = row_psum(ids, project(harmonics, solution))
    return (solution, coefficients)


def solution(mesh):
    in_specs = (
        P(None, None, "row"),
        P("row"),
        P("row", None, None, None, "col"),
        P("row", "col", None, None, None),
        P("row", "col", None, None, None),
        P("row", None),
        P("row", "col"),
        P(None, None, "row"),
    )
    out_specs = (P(None, None, "row"), P())
    return jax.shard_map(body, mesh=mesh, in_specs=in_specs, out_specs=out_specs, check_vma=False)
```

```python
from functools import partial

import jax
import jax.numpy as jnp
from jax import lax
from jax.experimental import pallas as pl
from jax.experimental.pallas import tpu as pltpu
from jax.sharding import PartitionSpec as P

highest = lax.Precision.HIGHEST
MESH = pl.DeviceIdType.MESH


def allreduce_kernel(n, x_ref, o_ref, buf, send_sems, recv_sems):
    me = lax.axis_index("row")
    col = lax.axis_index("col")
    barrier = pltpu.get_barrier_semaphore()

    def peer(d):
        return (lax.rem(me + d, n), col)

    def copy(d):
        return pltpu.make_async_remote_copy(
            src_ref=x_ref,
            dst_ref=buf.at[d],
            send_sem=send_sems.at[d],
            recv_sem=recv_sems.at[d],
            device_id=peer(d),
            device_id_type=MESH,
        )

    def greet(d, carry):
        pl.semaphore_signal(barrier, inc=1, device_id=peer(d), device_id_type=MESH)
        return carry

    def start(d, carry):
        copy(d).start()
        return carry

    def finish(d, carry):
        copy(d).wait()
        return carry

    def add(source, total):
        return total + buf[lax.rem(me + n - source, n)]

    lax.fori_loop(1, n, greet, 0)
    pl.semaphore_wait(barrier, n - 1)
    lax.fori_loop(1, n, start, 0)
    buf[0] = x_ref[...]
    lax.fori_loop(1, n, finish, 0)
    o_ref[...] = lax.fori_loop(1, n, add, buf[me])


def row_allreduce(packed, collective_id):
    n = lax.axis_size("row")
    rows, lanes = packed.shape
    return pl.pallas_call(
        partial(allreduce_kernel, n),
        out_shape=jax.ShapeDtypeStruct((rows, lanes), jnp.float32),
        in_specs=[pl.BlockSpec(memory_space=pltpu.VMEM)],
        out_specs=pl.BlockSpec(memory_space=pltpu.VMEM),
        scratch_shapes=[
            pltpu.VMEM((n, rows, lanes), jnp.float32),
            pltpu.SemaphoreType.DMA((n,)),
            pltpu.SemaphoreType.DMA((n,)),
        ],
        compiler_params=pltpu.CompilerParams(collective_id=collective_id, has_side_effects=True),
    )(packed)


def gather_kernel(rows, cols, blocks, half, v_ref, near_ref, far_ref, slices, far_buf,
                  first_send, first_recv, second_send, second_recv, local_sems):
    me = lax.axis_index("row")
    col = lax.axis_index("col")
    width = slices.shape[-1]
    barrier = pltpu.get_barrier_semaphore()

    def row_peer(d):
        return (lax.rem(me + d, rows), col)

    def col_peer(e):
        return (me, lax.rem(col + e, cols))

    def window(c):
        return pl.ds(pl.multiple_of(c * width, width), width)

    own = v_ref.at[:, :, window(col)]

    def first(d):
        return pltpu.make_async_remote_copy(
            src_ref=own,
            dst_ref=slices.at[d],
            send_sem=first_send.at[d],
            recv_sem=first_recv.at[d],
            device_id=row_peer(d),
            device_id_type=MESH,
        )

    def second(t):
        e = 1 + t // blocks
        n = t % blocks
        target = lax.rem(col + e, cols)
        slot = lax.rem(me + rows - blocks * target - n, rows)
        return pltpu.make_async_remote_copy(
            src_ref=slices.at[slot],
            dst_ref=far_buf.at[n, :, :, window(col)],
            send_sem=second_send.at[t],
            recv_sem=second_recv.at[t],
            device_id=col_peer(e),
            device_id_type=MESH,
        )

    def greet_row(d, carry):
        pl.semaphore_signal(barrier, inc=1, device_id=row_peer(d), device_id_type=MESH)
        return carry

    def greet_col(e, carry):
        pl.semaphore_signal(barrier, inc=1, device_id=col_peer(e), device_id_type=MESH)
        return carry

    def start_first(d, carry):
        first(d).start()
        return carry

    def finish_first(d, carry):
        first(d).wait()
        return carry

    def start_second(t, carry):
        second(t).start()
        return carry

    def finish_second(t, carry):
        second(t).wait()
        return carry

    lax.fori_loop(1, rows, greet_row, 0)
    lax.fori_loop(1, cols, greet_col, 0)
    pl.semaphore_wait(barrier, rows - 1 + cols - 1)
    lax.fori_loop(1, rows, start_first, 0)
    local = pltpu.make_async_copy(own, slices.at[0], local_sems.at[blocks])
    local.start()
    lax.fori_loop(1, rows, finish_first, 0)
    local.wait()
    lax.fori_loop(0, (cols - 1) * blocks, start_second, 0)
    mine = []
    for n in range(blocks):
        slot = lax.rem(me + rows - blocks * col - n, rows)
        copy = pltpu.make_async_copy(slices.at[slot], far_buf.at[n, :, :, window(col)], local_sems.at[n])
        copy.start()
        mine.append(copy)
    for k in range(2 * half):
        near_ref[k] = slices[(half - k) % rows]
    lax.fori_loop(0, (cols - 1) * blocks, finish_second, 0)
    for copy in mine:
        copy.wait()
    far_ref[...] = far_buf[...]


def gather_pieces(vector, blocks, half, width, collective_id):
    rows = lax.axis_size("row")
    cols = lax.axis_size("col")
    parts, fields, elements = vector.shape
    return pl.pallas_call(
        partial(gather_kernel, rows, cols, blocks, half),
        out_shape=(
            jax.ShapeDtypeStruct((2 * half, parts, fields, width), vector.dtype),
            jax.ShapeDtypeStruct((blocks, parts, fields, elements), vector.dtype),
        ),
        in_specs=[pl.BlockSpec(memory_space=pltpu.VMEM)],
        out_specs=(pl.BlockSpec(memory_space=pltpu.VMEM), pl.BlockSpec(memory_space=pltpu.VMEM)),
        scratch_shapes=[
            pltpu.VMEM((rows, parts, fields, width), vector.dtype),
            pltpu.VMEM((blocks, parts, fields, elements), vector.dtype),
            pltpu.SemaphoreType.DMA((rows,)),
            pltpu.SemaphoreType.DMA((rows,)),
            pltpu.SemaphoreType.DMA(((cols - 1) * blocks,)),
            pltpu.SemaphoreType.DMA(((cols - 1) * blocks,)),
            pltpu.SemaphoreType.DMA((blocks + 1,)),
        ],
        compiler_params=pltpu.CompilerParams(collective_id=collective_id, has_side_effects=True),
    )(vector)


def reduce_kernel(cols, x_ref, o_ref, parts_buf, full, first_send, first_recv, second_send, second_recv):
    me = lax.axis_index("row")
    col = lax.axis_index("col")
    width = parts_buf.shape[-1]
    barrier = pltpu.get_barrier_semaphore()

    def col_peer(e):
        return (me, lax.rem(col + e, cols))

    def window(c):
        return pl.ds(pl.multiple_of(c * width, width), width)

    def first(e):
        return pltpu.make_async_remote_copy(
            src_ref=x_ref.at[:, :, window(lax.rem(col + e, cols))],
            dst_ref=parts_buf.at[e],
            send_sem=first_send.at[e],
            recv_sem=first_recv.at[e],
            device_id=col_peer(e),
            device_id_type=MESH,
        )

    def second(e):
        return pltpu.make_async_remote_copy(
            src_ref=full.at[:, :, window(col)],
            dst_ref=full.at[:, :, window(col)],
            send_sem=second_send.at[e],
            recv_sem=second_recv.at[e],
            device_id=col_peer(e),
            device_id_type=MESH,
        )

    def greet(e, carry):
        pl.semaphore_signal(barrier, inc=1, device_id=col_peer(e), device_id_type=MESH)
        return carry

    def start_first(e, carry):
        first(e).start()
        return carry

    def finish_first(e, carry):
        first(e).wait()
        return carry

    def start_second(e, carry):
        second(e).start()
        return carry

    def finish_second(e, carry):
        second(e).wait_send()
        pltpu.make_async_remote_copy(
            src_ref=full.at[:, :, window(col)],
            dst_ref=full.at[:, :, window(lax.rem(col + cols - e, cols))],
            send_sem=second_send.at[e],
            recv_sem=second_recv.at[e],
            device_id=col_peer(e),
            device_id_type=MESH,
        ).wait_recv()
        return carry

    def add(source, total):
        return total + parts_buf[lax.rem(col + cols - source, cols)]

    lax.fori_loop(1, cols, greet, 0)
    pl.semaphore_wait(barrier, cols - 1)
    lax.fori_loop(1, cols, start_first, 0)
    parts_buf[0] = x_ref[:, :, window(col)]
    lax.fori_loop(1, cols, finish_first, 0)
    full[:, :, window(col)] = lax.fori_loop(1, cols, add, parts_buf[col])
    lax.fori_loop(1, cols, start_second, 0)
    lax.fori_loop(1, cols, finish_second, 0)
    o_ref[...] = full[...]


def col_reduce(partial_sum, collective_id):
    cols = lax.axis_size("col")
    parts, fields, elements = partial_sum.shape
    width = elements // cols
    return pl.pallas_call(
        partial(reduce_kernel, cols),
        out_shape=jax.ShapeDtypeStruct(partial_sum.shape, jnp.float32),
        in_specs=[pl.BlockSpec(memory_space=pltpu.VMEM)],
        out_specs=pl.BlockSpec(memory_space=pltpu.VMEM),
        scratch_shapes=[
            pltpu.VMEM((cols, parts, fields, width), jnp.float32),
            pltpu.VMEM((parts, fields, elements), jnp.float32),
            pltpu.SemaphoreType.DMA((cols,)),
            pltpu.SemaphoreType.DMA((cols,)),
            pltpu.SemaphoreType.DMA((cols,)),
            pltpu.SemaphoreType.DMA((cols,)),
        ],
        compiler_params=pltpu.CompilerParams(collective_id=collective_id, has_side_effects=True),
    )(partial_sum)


def row_psum(ids, *arrays):
    flat = [a.reshape(-1) for a in arrays]
    sizes = [f.shape[0] for f in flat]
    total = sum(sizes)
    padded = -(-total // 1024) * 1024
    packed = jnp.concatenate(flat + [jnp.zeros((padded - total,), jnp.float32)]).reshape(-1, 128)
    summed = row_allreduce(packed, len(ids)).reshape(-1)
    ids.append(None)
    outs = []
    start = 0
    for a, size in zip(arrays, sizes):
        outs.append(summed[start : start + size].reshape(a.shape))
        start += size
    return outs[0] if len(outs) == 1 else tuple(outs)


def complex_lhs(values, part_axis):
    real = jnp.take(values, 0, axis=part_axis)
    imag = jnp.take(values, 1, axis=part_axis)
    return jnp.stack([jnp.stack([real, -imag]), jnp.stack([imag, real])])


def inner_products(first, second):
    return jnp.einsum("csn,ctn->st", first, second, precision=highest)


def combine_rows(matrix, vectors):
    return jnp.einsum("st,ctn->csn", matrix, vectors, precision=highest)


def matmul(left, right):
    return jnp.dot(left, right, precision=highest)


def lower_inverse(lower):
    identity = jnp.eye(lower.shape[0], dtype=lower.dtype)
    return lax.linalg.triangular_solve(lower, identity, left_side=True, lower=True)


def project(harmonics, vectors):

    def contract(left, right):
        return jnp.einsum("mn,sn->ms", left, right, precision=highest)

    real_out = contract(harmonics[0], vectors[0]) + contract(harmonics[1], vectors[1])
    imag_out = contract(harmonics[0], vectors[1]) - contract(harmonics[1], vectors[0])
    return jnp.stack([real_out, imag_out])


def body(incident, diagonal, near_blocks, left_factors, right_factors, flags, ranks, harmonics):
    blocks = left_factors.shape[1]
    slots = near_blocks.shape[1]
    width = near_blocks.shape[4]
    half_band = slots // 2
    elements = incident.shape[2]
    fields = incident.shape[1]
    clusters = lax.axis_size("row")
    row_index = lax.axis_index("row")
    column = lax.axis_index("col")
    ids = []

    def operator_terms(near_pieces, far_pieces):
        near_on = flags[0] == 1
        near_vector = jnp.where(near_on[:, None, None, None], near_pieces, 0).astype(jnp.bfloat16)
        near_out = jnp.einsum(
            "caksf,kaef->cse",
            complex_lhs(near_vector, 1),
            near_blocks[0],
            preferred_element_type=jnp.float32,
        )
        cluster = column * blocks + jnp.arange(blocks, dtype=jnp.int32)
        offset = (cluster - row_index + half_band) % clusters
        is_near = (offset < slots) & (flags[0, jnp.minimum(offset, slots - 1)] == 1)
        keep = (~is_near)[:, None] & (
            jnp.arange(right_factors.shape[3], dtype=jnp.int32)[None, :] < ranks[0][:, None]
        )
        coeffs = jnp.einsum(
            "cansf,narf->cnsr",
            complex_lhs(far_pieces, 1),
            right_factors[0],
            preferred_element_type=jnp.float32,
        )
        coeffs = jnp.where(keep[None, :, None, :], coeffs, 0.0).astype(jnp.bfloat16)
        far_out = jnp.einsum(
            "cansr,nare->cse",
            complex_lhs(coeffs, 0),
            left_factors[0],
            preferred_element_type=jnp.float32,
        )
        return near_out + far_out

    def apply_operator(vector):
        rounded = vector.astype(jnp.bfloat16)
        near_pieces, far_pieces = gather_pieces(rounded, blocks, half_band, width, 16 + len(ids))
        ids.append(None)
        total = operator_terms(near_pieces, far_pieces)
        summed = col_reduce(total, 32 + len(ids))
        ids.append(None)
        return summed + diagonal[None, None, :] * vector

    lower_first = jnp.linalg.cholesky(row_psum(ids, inner_products(incident, incident)))
    basis_one = combine_rows(lower_inverse(lower_first), incident)
    image = apply_operator(basis_one)
    coupling_one, harmonics_one, self_one = row_psum(
        ids,
        inner_products(image, basis_one),
        project(harmonics, basis_one),
        inner_products(basis_one, basis_one),
    )
    rest = image - combine_rows(coupling_one, basis_one)
    gram_one = row_psum(ids, inner_products(rest, rest))
    lower_second = jnp.linalg.cholesky(gram_one)
    basis_two = combine_rows(lower_inverse(lower_second), rest)
    image = apply_operator(basis_two)
    coupling_onetwo, coupling_two, image_gram, cross, self_two, harmonics_two = row_psum(
        ids,
        inner_products(image, basis_one),
        inner_products(image, basis_two),
        inner_products(image, image),
        inner_products(basis_one, basis_two),
        inner_products(basis_two, basis_two),
        project(harmonics, basis_two),
    )
    coupling = jnp.concatenate([coupling_onetwo, coupling_two], axis=1)
    basis_gram = jnp.concatenate(
        [
            jnp.concatenate([self_one, cross], axis=1),
            jnp.concatenate([cross.T, self_two], axis=1),
        ],
        axis=0,
    )
    gram_two = (
        image_gram
        - 2.0 * matmul(coupling, coupling.T)
        + matmul(coupling, matmul(basis_gram, coupling.T))
    )
    upper_left = matmul(coupling_one, coupling_one.T) + gram_one
    upper_right = matmul(coupling_one, coupling_onetwo.T) + matmul(lower_second, coupling_two.T)
    lower_right = (
        matmul(coupling_onetwo, coupling_onetwo.T) + matmul(coupling_two, coupling_two.T) + gram_two
    )
    normal = jnp.concatenate(
        [
            jnp.concatenate([upper_left, upper_right], axis=1),
            jnp.concatenate([upper_right.T, lower_right], axis=1),
        ],
        axis=0,
    )
    target = jnp.concatenate(
        [matmul(lower_first, coupling_one.T), matmul(lower_first, coupling_onetwo.T)], axis=1
    )
    factor_inverse = lower_inverse(jnp.linalg.cholesky(normal))
    weights = matmul(factor_inverse.T, matmul(factor_inverse, target.T)).T
    first_weights = weights[:, :fields]
    second_weights = weights[:, fields:]
    solution = combine_rows(first_weights, basis_one) + combine_rows(second_weights, basis_two)
    coefficients = jnp.einsum(
        "cmt,st->cms", harmonics_one, first_weights, precision=highest
    ) + jnp.einsum("cmt,st->cms", harmonics_two, second_weights, precision=highest)
    return (solution, coefficients)


def solution(mesh):
    in_specs = (
        P(None, None, "row"),
        P("row"),
        P("row", None, None, None, "col"),
        P("row", "col", None, None, None),
        P("row", "col", None, None, None),
        P("row", None),
        P("row", "col"),
        P(None, None, "row"),
    )
    out_specs = (P(None, None, "row"), P())
    return jax.shard_map(body, mesh=mesh, in_specs=in_specs, out_specs=out_specs, check_vma=False)
```

```python
from functools import partial

import jax
import jax.numpy as jnp
from jax import lax
from jax.experimental import pallas as pl
from jax.experimental.pallas import tpu as pltpu
from jax.sharding import PartitionSpec as P

highest = lax.Precision.HIGHEST
MESH = pl.DeviceIdType.MESH


def allreduce_kernel(inner, outer, x_ref, o_ref, buf, partial_buf,
                     first_send, first_recv, second_send, second_recv):
    me = lax.axis_index("row")
    col = lax.axis_index("col")
    high = me // inner
    low = me % inner
    barrier = pltpu.get_barrier_semaphore()

    def inner_peer(d):
        return (high * inner + lax.rem(low + d, inner), col)

    def outer_peer(d):
        return (lax.rem(high + d, outer) * inner + low, col)

    def first(d):
        return pltpu.make_async_remote_copy(
            src_ref=x_ref,
            dst_ref=buf.at[d],
            send_sem=first_send.at[d],
            recv_sem=first_recv.at[d],
            device_id=inner_peer(d),
            device_id_type=MESH,
        )

    def second(d):
        return pltpu.make_async_remote_copy(
            src_ref=partial_buf.at[0],
            dst_ref=partial_buf.at[d],
            send_sem=second_send.at[d],
            recv_sem=second_recv.at[d],
            device_id=outer_peer(d),
            device_id_type=MESH,
        )

    def greet_inner(d, carry):
        pl.semaphore_signal(barrier, inc=1, device_id=inner_peer(d), device_id_type=MESH)
        return carry

    def greet_outer(d, carry):
        pl.semaphore_signal(barrier, inc=1, device_id=outer_peer(d), device_id_type=MESH)
        return carry

    def start_first(d, carry):
        first(d).start()
        return carry

    def finish_first(d, carry):
        first(d).wait()
        return carry

    def start_second(d, carry):
        second(d).start()
        return carry

    def finish_second(d, carry):
        second(d).wait()
        return carry

    def add_inner(source, total):
        return total + buf[lax.rem(low + inner - source, inner)]

    def add_outer(source, total):
        return total + partial_buf[lax.rem(high + outer - source, outer)]

    lax.fori_loop(1, inner, greet_inner, 0)
    lax.fori_loop(1, outer, greet_outer, 0)
    pl.semaphore_wait(barrier, inner - 1 + outer - 1)
    lax.fori_loop(1, inner, start_first, 0)
    buf[0] = x_ref[...]
    lax.fori_loop(1, inner, finish_first, 0)
    partial_buf[0] = lax.fori_loop(1, inner, add_inner, buf[low])
    lax.fori_loop(1, outer, start_second, 0)
    lax.fori_loop(1, outer, finish_second, 0)
    o_ref[...] = lax.fori_loop(1, outer, add_outer, partial_buf[high])


def row_allreduce(packed, collective_id):
    n = lax.axis_size("row")
    inner = 8 if n % 8 == 0 else n
    outer = n // inner
    rows, lanes = packed.shape
    return pl.pallas_call(
        partial(allreduce_kernel, inner, outer),
        out_shape=jax.ShapeDtypeStruct((rows, lanes), jnp.float32),
        in_specs=[pl.BlockSpec(memory_space=pltpu.VMEM)],
        out_specs=pl.BlockSpec(memory_space=pltpu.VMEM),
        scratch_shapes=[
            pltpu.VMEM((inner, rows, lanes), jnp.float32),
            pltpu.VMEM((outer, rows, lanes), jnp.float32),
            pltpu.SemaphoreType.DMA((inner,)),
            pltpu.SemaphoreType.DMA((inner,)),
            pltpu.SemaphoreType.DMA((outer,)),
            pltpu.SemaphoreType.DMA((outer,)),
        ],
        compiler_params=pltpu.CompilerParams(collective_id=collective_id, has_side_effects=True),
    )(packed)


def gather_kernel(rows, cols, blocks, half, v_ref, near_ref, far_ref, slices, far_buf,
                  first_send, first_recv, second_send, second_recv, local_sems):
    me = lax.axis_index("row")
    col = lax.axis_index("col")
    width = slices.shape[-1]
    barrier = pltpu.get_barrier_semaphore()

    def row_peer(d):
        return (lax.rem(me + d, rows), col)

    def col_peer(e):
        return (me, lax.rem(col + e, cols))

    def window(c):
        return pl.ds(pl.multiple_of(c * width, width), width)

    own = v_ref.at[:, :, window(col)]

    def first(d):
        return pltpu.make_async_remote_copy(
            src_ref=own,
            dst_ref=slices.at[d],
            send_sem=first_send.at[d],
            recv_sem=first_recv.at[d],
            device_id=row_peer(d),
            device_id_type=MESH,
        )

    def second(t):
        e = 1 + t // blocks
        n = t % blocks
        target = lax.rem(col + e, cols)
        slot = lax.rem(me + rows - blocks * target - n, rows)
        return pltpu.make_async_remote_copy(
            src_ref=slices.at[slot],
            dst_ref=far_buf.at[n, :, :, window(col)],
            send_sem=second_send.at[t],
            recv_sem=second_recv.at[t],
            device_id=col_peer(e),
            device_id_type=MESH,
        )

    def greet_row(d, carry):
        pl.semaphore_signal(barrier, inc=1, device_id=row_peer(d), device_id_type=MESH)
        return carry

    def greet_col(e, carry):
        pl.semaphore_signal(barrier, inc=1, device_id=col_peer(e), device_id_type=MESH)
        return carry

    def start_first(d, carry):
        first(d).start()
        return carry

    def finish_first(d, carry):
        first(d).wait()
        return carry

    def start_second(t, carry):
        second(t).start()
        return carry

    def finish_second(t, carry):
        second(t).wait()
        return carry

    lax.fori_loop(1, rows, greet_row, 0)
    lax.fori_loop(1, cols, greet_col, 0)
    pl.semaphore_wait(barrier, rows - 1 + cols - 1)
    lax.fori_loop(1, rows, start_first, 0)
    local = pltpu.make_async_copy(own, slices.at[0], local_sems.at[blocks])
    local.start()
    lax.fori_loop(1, rows, finish_first, 0)
    local.wait()
    lax.fori_loop(0, (cols - 1) * blocks, start_second, 0)
    mine = []
    for n in range(blocks):
        slot = lax.rem(me + rows - blocks * col - n, rows)
        copy = pltpu.make_async_copy(slices.at[slot], far_buf.at[n, :, :, window(col)], local_sems.at[n])
        copy.start()
        mine.append(copy)
    for k in range(2 * half):
        near_ref[k] = slices[(half - k) % rows]
    lax.fori_loop(0, (cols - 1) * blocks, finish_second, 0)
    for copy in mine:
        copy.wait()
    far_ref[...] = far_buf[...]


def gather_pieces(vector, blocks, half, width, collective_id):
    rows = lax.axis_size("row")
    cols = lax.axis_size("col")
    parts, fields, elements = vector.shape
    return pl.pallas_call(
        partial(gather_kernel, rows, cols, blocks, half),
        out_shape=(
            jax.ShapeDtypeStruct((2 * half, parts, fields, width), vector.dtype),
            jax.ShapeDtypeStruct((blocks, parts, fields, elements), vector.dtype),
        ),
        in_specs=[pl.BlockSpec(memory_space=pltpu.VMEM)],
        out_specs=(pl.BlockSpec(memory_space=pltpu.VMEM), pl.BlockSpec(memory_space=pltpu.VMEM)),
        scratch_shapes=[
            pltpu.VMEM((rows, parts, fields, width), vector.dtype),
            pltpu.VMEM((blocks, parts, fields, elements), vector.dtype),
            pltpu.SemaphoreType.DMA((rows,)),
            pltpu.SemaphoreType.DMA((rows,)),
            pltpu.SemaphoreType.DMA(((cols - 1) * blocks,)),
            pltpu.SemaphoreType.DMA(((cols - 1) * blocks,)),
            pltpu.SemaphoreType.DMA((blocks + 1,)),
        ],
        compiler_params=pltpu.CompilerParams(collective_id=collective_id, has_side_effects=True),
    )(vector)


def reduce_kernel(cols, x_ref, o_ref, parts_buf, full, first_send, first_recv, second_send, second_recv):
    me = lax.axis_index("row")
    col = lax.axis_index("col")
    width = parts_buf.shape[-1]
    barrier = pltpu.get_barrier_semaphore()

    def col_peer(e):
        return (me, lax.rem(col + e, cols))

    def window(c):
        return pl.ds(pl.multiple_of(c * width, width), width)

    def first(e):
        return pltpu.make_async_remote_copy(
            src_ref=x_ref.at[:, :, window(lax.rem(col + e, cols))],
            dst_ref=parts_buf.at[e],
            send_sem=first_send.at[e],
            recv_sem=first_recv.at[e],
            device_id=col_peer(e),
            device_id_type=MESH,
        )

    def second(e):
        return pltpu.make_async_remote_copy(
            src_ref=full.at[:, :, window(col)],
            dst_ref=full.at[:, :, window(col)],
            send_sem=second_send.at[e],
            recv_sem=second_recv.at[e],
            device_id=col_peer(e),
            device_id_type=MESH,
        )

    def greet(e, carry):
        pl.semaphore_signal(barrier, inc=1, device_id=col_peer(e), device_id_type=MESH)
        return carry

    def start_first(e, carry):
        first(e).start()
        return carry

    def finish_first(e, carry):
        first(e).wait()
        return carry

    def start_second(e, carry):
        second(e).start()
        return carry

    def finish_second(e, carry):
        second(e).wait_send()
        pltpu.make_async_remote_copy(
            src_ref=full.at[:, :, window(col)],
            dst_ref=full.at[:, :, window(lax.rem(col + cols - e, cols))],
            send_sem=second_send.at[e],
            recv_sem=second_recv.at[e],
            device_id=col_peer(e),
            device_id_type=MESH,
        ).wait_recv()
        return carry

    def add(source, total):
        return total + parts_buf[lax.rem(col + cols - source, cols)]

    lax.fori_loop(1, cols, greet, 0)
    pl.semaphore_wait(barrier, cols - 1)
    lax.fori_loop(1, cols, start_first, 0)
    parts_buf[0] = x_ref[:, :, window(col)]
    lax.fori_loop(1, cols, finish_first, 0)
    full[:, :, window(col)] = lax.fori_loop(1, cols, add, parts_buf[col])
    lax.fori_loop(1, cols, start_second, 0)
    lax.fori_loop(1, cols, finish_second, 0)
    o_ref[...] = full[...]


def col_reduce(partial_sum, collective_id):
    cols = lax.axis_size("col")
    parts, fields, elements = partial_sum.shape
    width = elements // cols
    return pl.pallas_call(
        partial(reduce_kernel, cols),
        out_shape=jax.ShapeDtypeStruct(partial_sum.shape, jnp.float32),
        in_specs=[pl.BlockSpec(memory_space=pltpu.VMEM)],
        out_specs=pl.BlockSpec(memory_space=pltpu.VMEM),
        scratch_shapes=[
            pltpu.VMEM((cols, parts, fields, width), jnp.float32),
            pltpu.VMEM((parts, fields, elements), jnp.float32),
            pltpu.SemaphoreType.DMA((cols,)),
            pltpu.SemaphoreType.DMA((cols,)),
            pltpu.SemaphoreType.DMA((cols,)),
            pltpu.SemaphoreType.DMA((cols,)),
        ],
        compiler_params=pltpu.CompilerParams(collective_id=collective_id, has_side_effects=True),
    )(partial_sum)


def row_psum(ids, *arrays):
    flat = [a.reshape(-1) for a in arrays]
    sizes = [f.shape[0] for f in flat]
    total = sum(sizes)
    padded = -(-total // 1024) * 1024
    packed = jnp.concatenate(flat + [jnp.zeros((padded - total,), jnp.float32)]).reshape(-1, 128)
    summed = row_allreduce(packed, len(ids)).reshape(-1)
    ids.append(None)
    outs = []
    start = 0
    for a, size in zip(arrays, sizes):
        outs.append(summed[start : start + size].reshape(a.shape))
        start += size
    return outs[0] if len(outs) == 1 else tuple(outs)


def complex_lhs(values, part_axis):
    real = jnp.take(values, 0, axis=part_axis)
    imag = jnp.take(values, 1, axis=part_axis)
    return jnp.stack([jnp.stack([real, -imag]), jnp.stack([imag, real])])


def inner_products(first, second):
    return jnp.einsum("csn,ctn->st", first, second, precision=highest)


def combine_rows(matrix, vectors):
    return jnp.einsum("st,ctn->csn", matrix, vectors, precision=highest)


def matmul(left, right):
    return jnp.dot(left, right, precision=highest)


def lower_inverse(lower):
    identity = jnp.eye(lower.shape[0], dtype=lower.dtype)
    return lax.linalg.triangular_solve(lower, identity, left_side=True, lower=True)


def project(harmonics, vectors):

    def contract(left, right):
        return jnp.einsum("mn,sn->ms", left, right, precision=highest)

    real_out = contract(harmonics[0], vectors[0]) + contract(harmonics[1], vectors[1])
    imag_out = contract(harmonics[0], vectors[1]) - contract(harmonics[1], vectors[0])
    return jnp.stack([real_out, imag_out])


def body(incident, diagonal, near_blocks, left_factors, right_factors, flags, ranks, harmonics):
    blocks = left_factors.shape[1]
    slots = near_blocks.shape[1]
    width = near_blocks.shape[4]
    half_band = slots // 2
    elements = incident.shape[2]
    fields = incident.shape[1]
    clusters = lax.axis_size("row")
    row_index = lax.axis_index("row")
    column = lax.axis_index("col")
    ids = []

    def operator_terms(near_pieces, far_pieces):
        near_on = flags[0] == 1
        near_vector = jnp.where(near_on[:, None, None, None], near_pieces, 0).astype(jnp.bfloat16)
        near_out = jnp.einsum(
            "caksf,kaef->cse",
            complex_lhs(near_vector, 1),
            near_blocks[0],
            preferred_element_type=jnp.float32,
        )
        cluster = column * blocks + jnp.arange(blocks, dtype=jnp.int32)
        offset = (cluster - row_index + half_band) % clusters
        is_near = (offset < slots) & (flags[0, jnp.minimum(offset, slots - 1)] == 1)
        keep = (~is_near)[:, None] & (
            jnp.arange(right_factors.shape[3], dtype=jnp.int32)[None, :] < ranks[0][:, None]
        )
        coeffs = jnp.einsum(
            "cansf,narf->cnsr",
            complex_lhs(far_pieces, 1),
            right_factors[0],
            preferred_element_type=jnp.float32,
        )
        coeffs = jnp.where(keep[None, :, None, :], coeffs, 0.0).astype(jnp.bfloat16)
        far_out = jnp.einsum(
            "cansr,nare->cse",
            complex_lhs(coeffs, 0),
            left_factors[0],
            preferred_element_type=jnp.float32,
        )
        return near_out + far_out

    def apply_operator(vector):
        rounded = vector.astype(jnp.bfloat16)
        near_pieces, far_pieces = gather_pieces(rounded, blocks, half_band, width, 16 + len(ids))
        ids.append(None)
        total = operator_terms(near_pieces, far_pieces)
        summed = col_reduce(total, 32 + len(ids))
        ids.append(None)
        return summed + diagonal[None, None, :] * vector

    lower_first = jnp.linalg.cholesky(row_psum(ids, inner_products(incident, incident)))
    basis_one = combine_rows(lower_inverse(lower_first), incident)
    image = apply_operator(basis_one)
    coupling_one, harmonics_one, self_one = row_psum(
        ids,
        inner_products(image, basis_one),
        project(harmonics, basis_one),
        inner_products(basis_one, basis_one),
    )
    rest = image - combine_rows(coupling_one, basis_one)
    gram_one = row_psum(ids, inner_products(rest, rest))
    lower_second = jnp.linalg.cholesky(gram_one)
    basis_two = combine_rows(lower_inverse(lower_second), rest)
    image = apply_operator(basis_two)
    coupling_onetwo, coupling_two, image_gram, cross, self_two, harmonics_two = row_psum(
        ids,
        inner_products(image, basis_one),
        inner_products(image, basis_two),
        inner_products(image, image),
        inner_products(basis_one, basis_two),
        inner_products(basis_two, basis_two),
        project(harmonics, basis_two),
    )
    coupling = jnp.concatenate([coupling_onetwo, coupling_two], axis=1)
    basis_gram = jnp.concatenate(
        [
            jnp.concatenate([self_one, cross], axis=1),
            jnp.concatenate([cross.T, self_two], axis=1),
        ],
        axis=0,
    )
    gram_two = (
        image_gram
        - 2.0 * matmul(coupling, coupling.T)
        + matmul(coupling, matmul(basis_gram, coupling.T))
    )
    upper_left = matmul(coupling_one, coupling_one.T) + gram_one
    upper_right = matmul(coupling_one, coupling_onetwo.T) + matmul(lower_second, coupling_two.T)
    lower_right = (
        matmul(coupling_onetwo, coupling_onetwo.T) + matmul(coupling_two, coupling_two.T) + gram_two
    )
    normal = jnp.concatenate(
        [
            jnp.concatenate([upper_left, upper_right], axis=1),
            jnp.concatenate([upper_right.T, lower_right], axis=1),
        ],
        axis=0,
    )
    target = jnp.concatenate(
        [matmul(lower_first, coupling_one.T), matmul(lower_first, coupling_onetwo.T)], axis=1
    )
    factor_inverse = lower_inverse(jnp.linalg.cholesky(normal))
    weights = matmul(factor_inverse.T, matmul(factor_inverse, target.T)).T
    first_weights = weights[:, :fields]
    second_weights = weights[:, fields:]
    solution = combine_rows(first_weights, basis_one) + combine_rows(second_weights, basis_two)
    coefficients = jnp.einsum(
        "cmt,st->cms", harmonics_one, first_weights, precision=highest
    ) + jnp.einsum("cmt,st->cms", harmonics_two, second_weights, precision=highest)
    return (solution, coefficients)


def solution(mesh):
    in_specs = (
        P(None, None, "row"),
        P("row"),
        P("row", None, None, None, "col"),
        P("row", "col", None, None, None),
        P("row", "col", None, None, None),
        P("row", None),
        P("row", "col"),
        P(None, None, "row"),
    )
    out_specs = (P(None, None, "row"), P())
    return jax.shard_map(body, mesh=mesh, in_specs=in_specs, out_specs=out_specs, check_vma=False)
```

```python
from functools import partial

import jax
import jax.numpy as jnp
from jax import lax
from jax.experimental import pallas as pl
from jax.experimental.pallas import tpu as pltpu
from jax.sharding import PartitionSpec as P

highest = lax.Precision.HIGHEST
MESH = pl.DeviceIdType.MESH


def allreduce_kernel(inner, outer, x_ref, o_ref, buf, partial_buf,
                     first_send, first_recv, second_send, second_recv):
    me = lax.axis_index("row")
    col = lax.axis_index("col")
    high = me // inner
    low = me % inner
    barrier = pltpu.get_barrier_semaphore()

    def inner_peer(d):
        return (high * inner + lax.rem(low + d, inner), col)

    def outer_peer(d):
        return (lax.rem(high + d, outer) * inner + low, col)

    def first(d):
        return pltpu.make_async_remote_copy(
            src_ref=x_ref,
            dst_ref=buf.at[d],
            send_sem=first_send.at[d],
            recv_sem=first_recv.at[d],
            device_id=inner_peer(d),
            device_id_type=MESH,
        )

    def second(d):
        return pltpu.make_async_remote_copy(
            src_ref=partial_buf.at[0],
            dst_ref=partial_buf.at[d],
            send_sem=second_send.at[d],
            recv_sem=second_recv.at[d],
            device_id=outer_peer(d),
            device_id_type=MESH,
        )

    def greet_inner(d, carry):
        pl.semaphore_signal(barrier, inc=1, device_id=inner_peer(d), device_id_type=MESH)
        return carry

    def greet_outer(d, carry):
        pl.semaphore_signal(barrier, inc=1, device_id=outer_peer(d), device_id_type=MESH)
        return carry

    def start_first(d, carry):
        first(d).start()
        return carry

    def finish_first(d, carry):
        first(d).wait()
        return carry

    def start_second(d, carry):
        second(d).start()
        return carry

    def finish_second(d, carry):
        second(d).wait()
        return carry

    def add_inner(source, total):
        return total + buf[lax.rem(low + inner - source, inner)]

    def add_outer(source, total):
        return total + partial_buf[lax.rem(high + outer - source, outer)]

    lax.fori_loop(1, inner, greet_inner, 0)
    lax.fori_loop(1, outer, greet_outer, 0)
    pl.semaphore_wait(barrier, inner - 1 + outer - 1)
    lax.fori_loop(1, inner, start_first, 0)
    buf[0] = x_ref[...]
    lax.fori_loop(1, inner, finish_first, 0)
    partial_buf[0] = lax.fori_loop(1, inner, add_inner, buf[low])
    lax.fori_loop(1, outer, start_second, 0)
    lax.fori_loop(1, outer, finish_second, 0)
    o_ref[...] = lax.fori_loop(1, outer, add_outer, partial_buf[high])


def row_allreduce(packed, collective_id):
    n = lax.axis_size("row")
    inner = 8 if n % 8 == 0 else n
    outer = n // inner
    rows, lanes = packed.shape
    return pl.pallas_call(
        partial(allreduce_kernel, inner, outer),
        out_shape=jax.ShapeDtypeStruct((rows, lanes), jnp.float32),
        in_specs=[pl.BlockSpec(memory_space=pltpu.VMEM)],
        out_specs=pl.BlockSpec(memory_space=pltpu.VMEM),
        scratch_shapes=[
            pltpu.VMEM((inner, rows, lanes), jnp.float32),
            pltpu.VMEM((outer, rows, lanes), jnp.float32),
            pltpu.SemaphoreType.DMA((inner,)),
            pltpu.SemaphoreType.DMA((inner,)),
            pltpu.SemaphoreType.DMA((outer,)),
            pltpu.SemaphoreType.DMA((outer,)),
        ],
        compiler_params=pltpu.CompilerParams(collective_id=collective_id, has_side_effects=True),
    )(packed)


def gather_kernel(rows, cols, blocks, half, v_ref, near_ref, far_ref, slices, far_buf,
                  first_send, first_recv, second_send, second_recv, local_sems):
    me = lax.axis_index("row")
    col = lax.axis_index("col")
    width = slices.shape[-1]
    barrier = pltpu.get_barrier_semaphore()

    def row_peer(d):
        return (lax.rem(me + d, rows), col)

    def col_peer(e):
        return (me, lax.rem(col + e, cols))

    def window(c):
        return pl.ds(pl.multiple_of(c * width, width), width)

    own = v_ref.at[:, :, window(col)]

    def first(d):
        return pltpu.make_async_remote_copy(
            src_ref=own,
            dst_ref=slices.at[d],
            send_sem=first_send.at[d],
            recv_sem=first_recv.at[d],
            device_id=row_peer(d),
            device_id_type=MESH,
        )

    def second(t):
        e = 1 + t // blocks
        n = t % blocks
        target = lax.rem(col + e, cols)
        slot = lax.rem(me + rows - blocks * target - n, rows)
        return pltpu.make_async_remote_copy(
            src_ref=slices.at[slot],
            dst_ref=far_buf.at[n, :, :, window(col)],
            send_sem=second_send.at[t],
            recv_sem=second_recv.at[t],
            device_id=col_peer(e),
            device_id_type=MESH,
        )

    def greet_row(d, carry):
        pl.semaphore_signal(barrier, inc=1, device_id=row_peer(d), device_id_type=MESH)
        return carry

    def greet_col(e, carry):
        pl.semaphore_signal(barrier, inc=1, device_id=col_peer(e), device_id_type=MESH)
        return carry

    def start_first(d, carry):
        first(d).start()
        return carry

    def finish_second(t, carry):
        second(t).wait()
        return carry

    def arrived(slot):
        pltpu.make_async_remote_copy(
            src_ref=own,
            dst_ref=slices.at[slot],
            send_sem=first_send.at[slot],
            recv_sem=first_recv.at[slot],
            device_id=row_peer(slot),
            device_id_type=MESH,
        ).wait_recv()

    def forward(t, carry):
        target = lax.rem(col + 1 + t // blocks, cols)
        arrived(lax.rem(me + rows - blocks * target - t % blocks, rows))
        second(t).start()
        return carry

    def sent_first(d, carry):
        first(d).wait_send()
        return carry

    lax.fori_loop(1, rows, greet_row, 0)
    lax.fori_loop(1, cols, greet_col, 0)
    pl.semaphore_wait(barrier, rows - 1 + cols - 1)
    lax.fori_loop(1, rows, start_first, 0)
    pltpu.make_async_copy(own, slices.at[0], first_recv.at[0]).start()
    lax.fori_loop(0, (cols - 1) * blocks, forward, 0)
    mine = []
    for n in range(blocks):
        slot = lax.rem(me + rows - blocks * col - n, rows)
        arrived(slot)
        copy = pltpu.make_async_copy(slices.at[slot], far_buf.at[n, :, :, window(col)], local_sems.at[n])
        copy.start()
        mine.append(copy)
    lax.fori_loop(1, rows, sent_first, 0)
    for k in range(2 * half):
        near_ref[k] = slices[(half - k) % rows]
    lax.fori_loop(0, (cols - 1) * blocks, finish_second, 0)
    for copy in mine:
        copy.wait()
    far_ref[...] = far_buf[...]


def gather_pieces(vector, blocks, half, width, collective_id):
    rows = lax.axis_size("row")
    cols = lax.axis_size("col")
    parts, fields, elements = vector.shape
    return pl.pallas_call(
        partial(gather_kernel, rows, cols, blocks, half),
        out_shape=(
            jax.ShapeDtypeStruct((2 * half, parts, fields, width), vector.dtype),
            jax.ShapeDtypeStruct((blocks, parts, fields, elements), vector.dtype),
        ),
        in_specs=[pl.BlockSpec(memory_space=pltpu.VMEM)],
        out_specs=(pl.BlockSpec(memory_space=pltpu.VMEM), pl.BlockSpec(memory_space=pltpu.VMEM)),
        scratch_shapes=[
            pltpu.VMEM((rows, parts, fields, width), vector.dtype),
            pltpu.VMEM((blocks, parts, fields, elements), vector.dtype),
            pltpu.SemaphoreType.DMA((rows,)),
            pltpu.SemaphoreType.DMA((rows,)),
            pltpu.SemaphoreType.DMA(((cols - 1) * blocks,)),
            pltpu.SemaphoreType.DMA(((cols - 1) * blocks,)),
            pltpu.SemaphoreType.DMA((blocks + 1,)),
        ],
        compiler_params=pltpu.CompilerParams(collective_id=collective_id, has_side_effects=True),
    )(vector)


def reduce_kernel(cols, x_ref, o_ref, parts_buf, full, first_send, first_recv, second_send, second_recv):
    me = lax.axis_index("row")
    col = lax.axis_index("col")
    width = parts_buf.shape[-1]
    barrier = pltpu.get_barrier_semaphore()

    def col_peer(e):
        return (me, lax.rem(col + e, cols))

    def window(c):
        return pl.ds(pl.multiple_of(c * width, width), width)

    def first(e):
        return pltpu.make_async_remote_copy(
            src_ref=x_ref.at[:, :, window(lax.rem(col + e, cols))],
            dst_ref=parts_buf.at[e],
            send_sem=first_send.at[e],
            recv_sem=first_recv.at[e],
            device_id=col_peer(e),
            device_id_type=MESH,
        )

    def second(e):
        return pltpu.make_async_remote_copy(
            src_ref=full.at[:, :, window(col)],
            dst_ref=full.at[:, :, window(col)],
            send_sem=second_send.at[e],
            recv_sem=second_recv.at[e],
            device_id=col_peer(e),
            device_id_type=MESH,
        )

    def greet(e, carry):
        pl.semaphore_signal(barrier, inc=1, device_id=col_peer(e), device_id_type=MESH)
        return carry

    def start_first(e, carry):
        first(e).start()
        return carry

    def finish_first(e, carry):
        first(e).wait()
        return carry

    def start_second(e, carry):
        second(e).start()
        return carry

    def finish_second(e, carry):
        second(e).wait_send()
        pltpu.make_async_remote_copy(
            src_ref=full.at[:, :, window(col)],
            dst_ref=full.at[:, :, window(lax.rem(col + cols - e, cols))],
            send_sem=second_send.at[e],
            recv_sem=second_recv.at[e],
            device_id=col_peer(e),
            device_id_type=MESH,
        ).wait_recv()
        return carry

    def add(source, total):
        return total + parts_buf[lax.rem(col + cols - source, cols)]

    lax.fori_loop(1, cols, greet, 0)
    pl.semaphore_wait(barrier, cols - 1)
    lax.fori_loop(1, cols, start_first, 0)
    parts_buf[0] = x_ref[:, :, window(col)]
    lax.fori_loop(1, cols, finish_first, 0)
    full[:, :, window(col)] = lax.fori_loop(1, cols, add, parts_buf[col])
    lax.fori_loop(1, cols, start_second, 0)
    lax.fori_loop(1, cols, finish_second, 0)
    o_ref[...] = full[...]


def col_reduce(partial_sum, collective_id):
    cols = lax.axis_size("col")
    parts, fields, elements = partial_sum.shape
    width = elements // cols
    return pl.pallas_call(
        partial(reduce_kernel, cols),
        out_shape=jax.ShapeDtypeStruct(partial_sum.shape, jnp.float32),
        in_specs=[pl.BlockSpec(memory_space=pltpu.VMEM)],
        out_specs=pl.BlockSpec(memory_space=pltpu.VMEM),
        scratch_shapes=[
            pltpu.VMEM((cols, parts, fields, width), jnp.float32),
            pltpu.VMEM((parts, fields, elements), jnp.float32),
            pltpu.SemaphoreType.DMA((cols,)),
            pltpu.SemaphoreType.DMA((cols,)),
            pltpu.SemaphoreType.DMA((cols,)),
            pltpu.SemaphoreType.DMA((cols,)),
        ],
        compiler_params=pltpu.CompilerParams(collective_id=collective_id, has_side_effects=True),
    )(partial_sum)


def row_psum(ids, *arrays):
    flat = [a.reshape(-1) for a in arrays]
    sizes = [f.shape[0] for f in flat]
    total = sum(sizes)
    padded = -(-total // 1024) * 1024
    packed = jnp.concatenate(flat + [jnp.zeros((padded - total,), jnp.float32)]).reshape(-1, 128)
    summed = row_allreduce(packed, len(ids)).reshape(-1)
    ids.append(None)
    outs = []
    start = 0
    for a, size in zip(arrays, sizes):
        outs.append(summed[start : start + size].reshape(a.shape))
        start += size
    return outs[0] if len(outs) == 1 else tuple(outs)


def complex_lhs(values, part_axis):
    real = jnp.take(values, 0, axis=part_axis)
    imag = jnp.take(values, 1, axis=part_axis)
    return jnp.stack([jnp.stack([real, -imag]), jnp.stack([imag, real])])


def inner_products(first, second):
    return jnp.einsum("csn,ctn->st", first, second, precision=highest)


def combine_rows(matrix, vectors):
    return jnp.einsum("st,ctn->csn", matrix, vectors, precision=highest)


def matmul(left, right):
    return jnp.dot(left, right, precision=highest)


def lower_inverse(lower):
    identity = jnp.eye(lower.shape[0], dtype=lower.dtype)
    return lax.linalg.triangular_solve(lower, identity, left_side=True, lower=True)


def project(harmonics, vectors):

    def contract(left, right):
        return jnp.einsum("mn,sn->ms", left, right, precision=highest)

    real_out = contract(harmonics[0], vectors[0]) + contract(harmonics[1], vectors[1])
    imag_out = contract(harmonics[0], vectors[1]) - contract(harmonics[1], vectors[0])
    return jnp.stack([real_out, imag_out])


def body(incident, diagonal, near_blocks, left_factors, right_factors, flags, ranks, harmonics):
    blocks = left_factors.shape[1]
    slots = near_blocks.shape[1]
    width = near_blocks.shape[4]
    half_band = slots // 2
    elements = incident.shape[2]
    fields = incident.shape[1]
    clusters = lax.axis_size("row")
    row_index = lax.axis_index("row")
    column = lax.axis_index("col")
    ids = []

    def operator_terms(near_pieces, far_pieces):
        near_on = flags[0] == 1
        near_vector = jnp.where(near_on[:, None, None, None], near_pieces, 0).astype(jnp.bfloat16)
        near_out = jnp.einsum(
            "caksf,kaef->cse",
            complex_lhs(near_vector, 1),
            near_blocks[0],
            preferred_element_type=jnp.float32,
        )
        cluster = column * blocks + jnp.arange(blocks, dtype=jnp.int32)
        offset = (cluster - row_index + half_band) % clusters
        is_near = (offset < slots) & (flags[0, jnp.minimum(offset, slots - 1)] == 1)
        keep = (~is_near)[:, None] & (
            jnp.arange(right_factors.shape[3], dtype=jnp.int32)[None, :] < ranks[0][:, None]
        )
        coeffs = jnp.einsum(
            "cansf,narf->cnsr",
            complex_lhs(far_pieces, 1),
            right_factors[0],
            preferred_element_type=jnp.float32,
        )
        coeffs = jnp.where(keep[None, :, None, :], coeffs, 0.0).astype(jnp.bfloat16)
        far_out = jnp.einsum(
            "cansr,nare->cse",
            complex_lhs(coeffs, 0),
            left_factors[0],
            preferred_element_type=jnp.float32,
        )
        return near_out + far_out

    def apply_operator(vector):
        rounded = vector.astype(jnp.bfloat16)
        near_pieces, far_pieces = gather_pieces(rounded, blocks, half_band, width, 16 + len(ids))
        ids.append(None)
        total = operator_terms(near_pieces, far_pieces)
        summed = col_reduce(total, 32 + len(ids))
        ids.append(None)
        return summed + diagonal[None, None, :] * vector

    lower_first = jnp.linalg.cholesky(row_psum(ids, inner_products(incident, incident)))
    basis_one = combine_rows(lower_inverse(lower_first), incident)
    image = apply_operator(basis_one)
    coupling_one, harmonics_one, self_one = row_psum(
        ids,
        inner_products(image, basis_one),
        project(harmonics, basis_one),
        inner_products(basis_one, basis_one),
    )
    rest = image - combine_rows(coupling_one, basis_one)
    gram_one = row_psum(ids, inner_products(rest, rest))
    lower_second = jnp.linalg.cholesky(gram_one)
    basis_two = combine_rows(lower_inverse(lower_second), rest)
    image = apply_operator(basis_two)
    coupling_onetwo, coupling_two, image_gram, cross, self_two, harmonics_two = row_psum(
        ids,
        inner_products(image, basis_one),
        inner_products(image, basis_two),
        inner_products(image, image),
        inner_products(basis_one, basis_two),
        inner_products(basis_two, basis_two),
        project(harmonics, basis_two),
    )
    coupling = jnp.concatenate([coupling_onetwo, coupling_two], axis=1)
    basis_gram = jnp.concatenate(
        [
            jnp.concatenate([self_one, cross], axis=1),
            jnp.concatenate([cross.T, self_two], axis=1),
        ],
        axis=0,
    )
    gram_two = (
        image_gram
        - 2.0 * matmul(coupling, coupling.T)
        + matmul(coupling, matmul(basis_gram, coupling.T))
    )
    upper_left = matmul(coupling_one, coupling_one.T) + gram_one
    upper_right = matmul(coupling_one, coupling_onetwo.T) + matmul(lower_second, coupling_two.T)
    lower_right = (
        matmul(coupling_onetwo, coupling_onetwo.T) + matmul(coupling_two, coupling_two.T) + gram_two
    )
    normal = jnp.concatenate(
        [
            jnp.concatenate([upper_left, upper_right], axis=1),
            jnp.concatenate([upper_right.T, lower_right], axis=1),
        ],
        axis=0,
    )
    target = jnp.concatenate(
        [matmul(lower_first, coupling_one.T), matmul(lower_first, coupling_onetwo.T)], axis=1
    )
    factor_inverse = lower_inverse(jnp.linalg.cholesky(normal))
    weights = matmul(factor_inverse.T, matmul(factor_inverse, target.T)).T
    first_weights = weights[:, :fields]
    second_weights = weights[:, fields:]
    solution = combine_rows(first_weights, basis_one) + combine_rows(second_weights, basis_two)
    coefficients = jnp.einsum(
        "cmt,st->cms", harmonics_one, first_weights, precision=highest
    ) + jnp.einsum("cmt,st->cms", harmonics_two, second_weights, precision=highest)
    return (solution, coefficients)


def solution(mesh):
    in_specs = (
        P(None, None, "row"),
        P("row"),
        P("row", None, None, None, "col"),
        P("row", "col", None, None, None),
        P("row", "col", None, None, None),
        P("row", None),
        P("row", "col"),
        P(None, None, "row"),
    )
    out_specs = (P(None, None, "row"), P())
    return jax.shard_map(body, mesh=mesh, in_specs=in_specs, out_specs=out_specs, check_vma=False)
```

```python
from functools import partial

import jax
import jax.numpy as jnp
from jax import lax
from jax.experimental import pallas as pl
from jax.experimental.pallas import tpu as pltpu
from jax.sharding import PartitionSpec as P

highest = lax.Precision.HIGHEST
MESH = pl.DeviceIdType.MESH


def allreduce_kernel(inner, outer, x_ref, o_ref, buf, partial_buf,
                     first_send, first_recv, second_send, second_recv):
    me = lax.axis_index("row")
    col = lax.axis_index("col")
    high = me // inner
    low = me % inner
    barrier = pltpu.get_barrier_semaphore()

    def inner_peer(d):
        return (high * inner + lax.rem(low + d, inner), col)

    def outer_peer(d):
        return (lax.rem(high + d, outer) * inner + low, col)

    def first(d):
        return pltpu.make_async_remote_copy(
            src_ref=x_ref,
            dst_ref=buf.at[d],
            send_sem=first_send.at[d],
            recv_sem=first_recv.at[d],
            device_id=inner_peer(d),
            device_id_type=MESH,
        )

    def second(d):
        return pltpu.make_async_remote_copy(
            src_ref=partial_buf.at[0],
            dst_ref=partial_buf.at[d],
            send_sem=second_send.at[d],
            recv_sem=second_recv.at[d],
            device_id=outer_peer(d),
            device_id_type=MESH,
        )

    def greet_inner(d, carry):
        pl.semaphore_signal(barrier, inc=1, device_id=inner_peer(d), device_id_type=MESH)
        return carry

    def greet_outer(d, carry):
        pl.semaphore_signal(barrier, inc=1, device_id=outer_peer(d), device_id_type=MESH)
        return carry

    def start_first(d, carry):
        first(d).start()
        return carry

    def finish_first(d, carry):
        first(d).wait()
        return carry

    def start_second(d, carry):
        second(d).start()
        return carry

    def finish_second(d, carry):
        second(d).wait()
        return carry

    def add_inner(source, total):
        return total + buf[lax.rem(low + inner - source, inner)]

    def add_outer(source, total):
        return total + partial_buf[lax.rem(high + outer - source, outer)]

    lax.fori_loop(1, inner, greet_inner, 0)
    lax.fori_loop(1, outer, greet_outer, 0)
    pl.semaphore_wait(barrier, inner - 1 + outer - 1)
    lax.fori_loop(1, inner, start_first, 0)
    buf[0] = x_ref[...]
    lax.fori_loop(1, inner, finish_first, 0)
    partial_buf[0] = lax.fori_loop(1, inner, add_inner, buf[low])
    lax.fori_loop(1, outer, start_second, 0)
    lax.fori_loop(1, outer, finish_second, 0)
    o_ref[...] = lax.fori_loop(1, outer, add_outer, partial_buf[high])


def row_allreduce(packed, collective_id):
    n = lax.axis_size("row")
    inner = 8 if n % 8 == 0 else n
    outer = n // inner
    rows, lanes = packed.shape
    return pl.pallas_call(
        partial(allreduce_kernel, inner, outer),
        out_shape=jax.ShapeDtypeStruct((rows, lanes), jnp.float32),
        in_specs=[pl.BlockSpec(memory_space=pltpu.VMEM)],
        out_specs=pl.BlockSpec(memory_space=pltpu.VMEM),
        scratch_shapes=[
            pltpu.VMEM((inner, rows, lanes), jnp.float32),
            pltpu.VMEM((outer, rows, lanes), jnp.float32),
            pltpu.SemaphoreType.DMA((inner,)),
            pltpu.SemaphoreType.DMA((inner,)),
            pltpu.SemaphoreType.DMA((outer,)),
            pltpu.SemaphoreType.DMA((outer,)),
        ],
        compiler_params=pltpu.CompilerParams(collective_id=collective_id, has_side_effects=True),
    )(packed)


def gather_kernel(rows, cols, blocks, half, v_ref, near_ref, far_ref, slices, far_buf,
                  first_send, first_recv, second_send, second_recv, local_sems):
    me = lax.axis_index("row")
    col = lax.axis_index("col")
    width = slices.shape[-1]
    barrier = pltpu.get_barrier_semaphore()

    def row_peer(d):
        return (lax.rem(me + d, rows), col)

    def col_peer(e):
        return (me, lax.rem(col + e, cols))

    def window(c):
        return pl.ds(pl.multiple_of(c * width, width), width)

    own = v_ref.at[:, window(col)]

    def first(d):
        return pltpu.make_async_remote_copy(
            src_ref=own,
            dst_ref=slices.at[d],
            send_sem=first_send.at[d],
            recv_sem=first_recv.at[d],
            device_id=row_peer(d),
            device_id_type=MESH,
        )

    def second(t):
        e = 1 + t // blocks
        n = t % blocks
        target = lax.rem(col + e, cols)
        slot = lax.rem(me + rows - blocks * target - n, rows)
        return pltpu.make_async_remote_copy(
            src_ref=slices.at[slot],
            dst_ref=far_buf.at[n, :, window(col)],
            send_sem=second_send.at[t],
            recv_sem=second_recv.at[t],
            device_id=col_peer(e),
            device_id_type=MESH,
        )

    def greet_row(d, carry):
        pl.semaphore_signal(barrier, inc=1, device_id=row_peer(d), device_id_type=MESH)
        return carry

    def greet_col(e, carry):
        pl.semaphore_signal(barrier, inc=1, device_id=col_peer(e), device_id_type=MESH)
        return carry

    def start_first(d, carry):
        first(d).start()
        return carry

    def finish_second(t, carry):
        second(t).wait()
        return carry

    def arrived(slot):
        pltpu.make_async_remote_copy(
            src_ref=own,
            dst_ref=slices.at[slot],
            send_sem=first_send.at[slot],
            recv_sem=first_recv.at[slot],
            device_id=row_peer(slot),
            device_id_type=MESH,
        ).wait_recv()

    def forward(t, carry):
        target = lax.rem(col + 1 + t // blocks, cols)
        arrived(lax.rem(me + rows - blocks * target - t % blocks, rows))
        second(t).start()
        return carry

    def sent_first(d, carry):
        first(d).wait_send()
        return carry

    lax.fori_loop(1, rows, greet_row, 0)
    lax.fori_loop(1, cols, greet_col, 0)
    pl.semaphore_wait(barrier, rows - 1 + cols - 1)
    lax.fori_loop(1, rows, start_first, 0)
    pltpu.make_async_copy(own, slices.at[0], first_recv.at[0]).start()
    lax.fori_loop(0, (cols - 1) * blocks, forward, 0)
    mine = []
    for n in range(blocks):
        slot = lax.rem(me + rows - blocks * col - n, rows)
        arrived(slot)
        copy = pltpu.make_async_copy(slices.at[slot], far_buf.at[n, :, window(col)], local_sems.at[n])
        copy.start()
        mine.append(copy)
    lax.fori_loop(1, rows, sent_first, 0)
    for k in range(2 * half):
        near_ref[k] = slices[(half - k) % rows]
    lax.fori_loop(0, (cols - 1) * blocks, finish_second, 0)
    for copy in mine:
        copy.wait()
    far_ref[...] = far_buf[...]


def gather_pieces(vector, blocks, half, width, collective_id):
    rows = lax.axis_size("row")
    cols = lax.axis_size("col")
    parts, fields, elements = vector.shape
    flat = vector.reshape(parts * fields, elements)
    near, far = pl.pallas_call(
        partial(gather_kernel, rows, cols, blocks, half),
        out_shape=(
            jax.ShapeDtypeStruct((2 * half, parts * fields, width), vector.dtype),
            jax.ShapeDtypeStruct((blocks, parts * fields, elements), vector.dtype),
        ),
        in_specs=[pl.BlockSpec(memory_space=pltpu.VMEM)],
        out_specs=(pl.BlockSpec(memory_space=pltpu.VMEM), pl.BlockSpec(memory_space=pltpu.VMEM)),
        scratch_shapes=[
            pltpu.VMEM((rows, parts * fields, width), vector.dtype),
            pltpu.VMEM((blocks, parts * fields, elements), vector.dtype),
            pltpu.SemaphoreType.DMA((rows,)),
            pltpu.SemaphoreType.DMA((rows,)),
            pltpu.SemaphoreType.DMA(((cols - 1) * blocks,)),
            pltpu.SemaphoreType.DMA(((cols - 1) * blocks,)),
            pltpu.SemaphoreType.DMA((blocks + 1,)),
        ],
        compiler_params=pltpu.CompilerParams(collective_id=collective_id, has_side_effects=True),
    )(flat)
    return (
        near.reshape(2 * half, parts, fields, width),
        far.reshape(blocks, parts, fields, elements),
    )


def reduce_kernel(cols, x_ref, o_ref, parts_buf, full, first_send, first_recv, second_send, second_recv):
    me = lax.axis_index("row")
    col = lax.axis_index("col")
    width = parts_buf.shape[-1]
    barrier = pltpu.get_barrier_semaphore()

    def col_peer(e):
        return (me, lax.rem(col + e, cols))

    def window(c):
        return pl.ds(pl.multiple_of(c * width, width), width)

    def first(e):
        return pltpu.make_async_remote_copy(
            src_ref=x_ref.at[:, :, window(lax.rem(col + e, cols))],
            dst_ref=parts_buf.at[e],
            send_sem=first_send.at[e],
            recv_sem=first_recv.at[e],
            device_id=col_peer(e),
            device_id_type=MESH,
        )

    def second(e):
        return pltpu.make_async_remote_copy(
            src_ref=full.at[:, :, window(col)],
            dst_ref=full.at[:, :, window(col)],
            send_sem=second_send.at[e],
            recv_sem=second_recv.at[e],
            device_id=col_peer(e),
            device_id_type=MESH,
        )

    def greet(e, carry):
        pl.semaphore_signal(barrier, inc=1, device_id=col_peer(e), device_id_type=MESH)
        return carry

    def start_first(e, carry):
        first(e).start()
        return carry

    def finish_first(e, carry):
        first(e).wait()
        return carry

    def start_second(e, carry):
        second(e).start()
        return carry

    def finish_second(e, carry):
        second(e).wait_send()
        pltpu.make_async_remote_copy(
            src_ref=full.at[:, :, window(col)],
            dst_ref=full.at[:, :, window(lax.rem(col + cols - e, cols))],
            send_sem=second_send.at[e],
            recv_sem=second_recv.at[e],
            device_id=col_peer(e),
            device_id_type=MESH,
        ).wait_recv()
        return carry

    def add(source, total):
        return total + parts_buf[lax.rem(col + cols - source, cols)]

    lax.fori_loop(1, cols, greet, 0)
    pl.semaphore_wait(barrier, cols - 1)
    lax.fori_loop(1, cols, start_first, 0)
    parts_buf[0] = x_ref[:, :, window(col)]
    lax.fori_loop(1, cols, finish_first, 0)
    full[:, :, window(col)] = lax.fori_loop(1, cols, add, parts_buf[col])
    lax.fori_loop(1, cols, start_second, 0)
    lax.fori_loop(1, cols, finish_second, 0)
    o_ref[...] = full[...]


def col_reduce(partial_sum, collective_id):
    cols = lax.axis_size("col")
    parts, fields, elements = partial_sum.shape
    width = elements // cols
    return pl.pallas_call(
        partial(reduce_kernel, cols),
        out_shape=jax.ShapeDtypeStruct(partial_sum.shape, jnp.float32),
        in_specs=[pl.BlockSpec(memory_space=pltpu.VMEM)],
        out_specs=pl.BlockSpec(memory_space=pltpu.VMEM),
        scratch_shapes=[
            pltpu.VMEM((cols, parts, fields, width), jnp.float32),
            pltpu.VMEM((parts, fields, elements), jnp.float32),
            pltpu.SemaphoreType.DMA((cols,)),
            pltpu.SemaphoreType.DMA((cols,)),
            pltpu.SemaphoreType.DMA((cols,)),
            pltpu.SemaphoreType.DMA((cols,)),
        ],
        compiler_params=pltpu.CompilerParams(collective_id=collective_id, has_side_effects=True),
    )(partial_sum)


def row_psum(ids, *arrays):
    flat = [a.reshape(-1) for a in arrays]
    sizes = [f.shape[0] for f in flat]
    total = sum(sizes)
    padded = -(-total // 1024) * 1024
    packed = jnp.concatenate(flat + [jnp.zeros((padded - total,), jnp.float32)]).reshape(-1, 128)
    summed = row_allreduce(packed, len(ids)).reshape(-1)
    ids.append(None)
    outs = []
    start = 0
    for a, size in zip(arrays, sizes):
        outs.append(summed[start : start + size].reshape(a.shape))
        start += size
    return outs[0] if len(outs) == 1 else tuple(outs)


def complex_lhs(values, part_axis):
    real = jnp.take(values, 0, axis=part_axis)
    imag = jnp.take(values, 1, axis=part_axis)
    return jnp.stack([jnp.stack([real, -imag]), jnp.stack([imag, real])])


def inner_products(first, second):
    return jnp.einsum("csn,ctn->st", first, second, precision=highest)


def combine_rows(matrix, vectors):
    return jnp.einsum("st,ctn->csn", matrix, vectors, precision=highest)


def matmul(left, right):
    return jnp.dot(left, right, precision=highest)


def lower_inverse(lower):
    identity = jnp.eye(lower.shape[0], dtype=lower.dtype)
    return lax.linalg.triangular_solve(lower, identity, left_side=True, lower=True)


def project(harmonics, vectors):

    def contract(left, right):
        return jnp.einsum("mn,sn->ms", left, right, precision=highest)

    real_out = contract(harmonics[0], vectors[0]) + contract(harmonics[1], vectors[1])
    imag_out = contract(harmonics[0], vectors[1]) - contract(harmonics[1], vectors[0])
    return jnp.stack([real_out, imag_out])


def body(incident, diagonal, near_blocks, left_factors, right_factors, flags, ranks, harmonics):
    blocks = left_factors.shape[1]
    slots = near_blocks.shape[1]
    width = near_blocks.shape[4]
    half_band = slots // 2
    elements = incident.shape[2]
    fields = incident.shape[1]
    clusters = lax.axis_size("row")
    row_index = lax.axis_index("row")
    column = lax.axis_index("col")
    ids = []

    def operator_terms(near_pieces, far_pieces):
        near_on = flags[0] == 1
        near_vector = jnp.where(near_on[:, None, None, None], near_pieces, 0).astype(jnp.bfloat16)
        near_out = jnp.einsum(
            "caksf,kaef->cse",
            complex_lhs(near_vector, 1),
            near_blocks[0],
            preferred_element_type=jnp.float32,
        )
        cluster = column * blocks + jnp.arange(blocks, dtype=jnp.int32)
        offset = (cluster - row_index + half_band) % clusters
        is_near = (offset < slots) & (flags[0, jnp.minimum(offset, slots - 1)] == 1)
        keep = (~is_near)[:, None] & (
            jnp.arange(right_factors.shape[3], dtype=jnp.int32)[None, :] < ranks[0][:, None]
        )
        coeffs = jnp.einsum(
            "cansf,narf->cnsr",
            complex_lhs(far_pieces, 1),
            right_factors[0],
            preferred_element_type=jnp.float32,
        )
        coeffs = jnp.where(keep[None, :, None, :], coeffs, 0.0).astype(jnp.bfloat16)
        far_out = jnp.einsum(
            "cansr,nare->cse",
            complex_lhs(coeffs, 0),
            left_factors[0],
            preferred_element_type=jnp.float32,
        )
        return near_out + far_out

    def apply_operator(vector):
        rounded = vector.astype(jnp.bfloat16)
        near_pieces, far_pieces = gather_pieces(rounded, blocks, half_band, width, 16 + len(ids))
        ids.append(None)
        total = operator_terms(near_pieces, far_pieces)
        summed = col_reduce(total, 32 + len(ids))
        ids.append(None)
        return summed + diagonal[None, None, :] * vector

    lower_first = jnp.linalg.cholesky(row_psum(ids, inner_products(incident, incident)))
    basis_one = combine_rows(lower_inverse(lower_first), incident)
    image = apply_operator(basis_one)
    coupling_one, harmonics_one, self_one = row_psum(
        ids,
        inner_products(image, basis_one),
        project(harmonics, basis_one),
        inner_products(basis_one, basis_one),
    )
    rest = image - combine_rows(coupling_one, basis_one)
    gram_one = row_psum(ids, inner_products(rest, rest))
    lower_second = jnp.linalg.cholesky(gram_one)
    basis_two = combine_rows(lower_inverse(lower_second), rest)
    image = apply_operator(basis_two)
    coupling_onetwo, coupling_two, image_gram, cross, self_two, harmonics_two = row_psum(
        ids,
        inner_products(image, basis_one),
        inner_products(image, basis_two),
        inner_products(image, image),
        inner_products(basis_one, basis_two),
        inner_products(basis_two, basis_two),
        project(harmonics, basis_two),
    )
    coupling = jnp.concatenate([coupling_onetwo, coupling_two], axis=1)
    basis_gram = jnp.concatenate(
        [
            jnp.concatenate([self_one, cross], axis=1),
            jnp.concatenate([cross.T, self_two], axis=1),
        ],
        axis=0,
    )
    gram_two = (
        image_gram
        - 2.0 * matmul(coupling, coupling.T)
        + matmul(coupling, matmul(basis_gram, coupling.T))
    )
    upper_left = matmul(coupling_one, coupling_one.T) + gram_one
    upper_right = matmul(coupling_one, coupling_onetwo.T) + matmul(lower_second, coupling_two.T)
    lower_right = (
        matmul(coupling_onetwo, coupling_onetwo.T) + matmul(coupling_two, coupling_two.T) + gram_two
    )
    normal = jnp.concatenate(
        [
            jnp.concatenate([upper_left, upper_right], axis=1),
            jnp.concatenate([upper_right.T, lower_right], axis=1),
        ],
        axis=0,
    )
    target = jnp.concatenate(
        [matmul(lower_first, coupling_one.T), matmul(lower_first, coupling_onetwo.T)], axis=1
    )
    factor_inverse = lower_inverse(jnp.linalg.cholesky(normal))
    weights = matmul(factor_inverse.T, matmul(factor_inverse, target.T)).T
    first_weights = weights[:, :fields]
    second_weights = weights[:, fields:]
    solution = combine_rows(first_weights, basis_one) + combine_rows(second_weights, basis_two)
    coefficients = jnp.einsum(
        "cmt,st->cms", harmonics_one, first_weights, precision=highest
    ) + jnp.einsum("cmt,st->cms", harmonics_two, second_weights, precision=highest)
    return (solution, coefficients)


def solution(mesh):
    in_specs = (
        P(None, None, "row"),
        P("row"),
        P("row", None, None, None, "col"),
        P("row", "col", None, None, None),
        P("row", "col", None, None, None),
        P("row", None),
        P("row", "col"),
        P(None, None, "row"),
    )
    out_specs = (P(None, None, "row"), P())
    return jax.shard_map(body, mesh=mesh, in_specs=in_specs, out_specs=out_specs, check_vma=False)
```

```python
from functools import partial

import jax
import jax.numpy as jnp
from jax import lax
from jax.experimental import pallas as pl
from jax.experimental.pallas import tpu as pltpu
from jax.sharding import PartitionSpec as P

highest = lax.Precision.HIGHEST
MESH = pl.DeviceIdType.MESH


def allreduce_kernel(inner, outer, x_ref, o_ref, buf, partial_buf,
                     first_send, first_recv, second_send, second_recv):
    me = lax.axis_index("row")
    col = lax.axis_index("col")
    high = me // inner
    low = me % inner
    barrier = pltpu.get_barrier_semaphore()

    def inner_peer(d):
        return (high * inner + lax.rem(low + d, inner), col)

    def outer_peer(d):
        return (lax.rem(high + d, outer) * inner + low, col)

    def first(d):
        return pltpu.make_async_remote_copy(
            src_ref=x_ref,
            dst_ref=buf.at[d],
            send_sem=first_send.at[d],
            recv_sem=first_recv.at[d],
            device_id=inner_peer(d),
            device_id_type=MESH,
        )

    def second(d):
        return pltpu.make_async_remote_copy(
            src_ref=partial_buf.at[0],
            dst_ref=partial_buf.at[d],
            send_sem=second_send.at[d],
            recv_sem=second_recv.at[d],
            device_id=outer_peer(d),
            device_id_type=MESH,
        )

    def greet_inner(d, carry):
        pl.semaphore_signal(barrier, inc=1, device_id=inner_peer(d), device_id_type=MESH)
        return carry

    def greet_outer(d, carry):
        pl.semaphore_signal(barrier, inc=1, device_id=outer_peer(d), device_id_type=MESH)
        return carry

    def start_first(d, carry):
        first(d).start()
        return carry

    def finish_first(d, carry):
        first(d).wait()
        return carry

    def start_second(d, carry):
        second(d).start()
        return carry

    def finish_second(d, carry):
        second(d).wait()
        return carry

    def add_inner(source, total):
        return total + buf[lax.rem(low + inner - source, inner)]

    def add_outer(source, total):
        return total + partial_buf[lax.rem(high + outer - source, outer)]

    lax.fori_loop(1, inner, greet_inner, 0)
    lax.fori_loop(1, outer, greet_outer, 0)
    pl.semaphore_wait(barrier, inner - 1 + outer - 1)
    lax.fori_loop(1, inner, start_first, 0)
    buf[0] = x_ref[...]
    lax.fori_loop(1, inner, finish_first, 0)
    partial_buf[0] = lax.fori_loop(1, inner, add_inner, buf[low])
    lax.fori_loop(1, outer, start_second, 0)
    lax.fori_loop(1, outer, finish_second, 0)
    o_ref[...] = lax.fori_loop(1, outer, add_outer, partial_buf[high])


def row_allreduce(packed, collective_id):
    n = lax.axis_size("row")
    inner = 8 if n % 8 == 0 else n
    outer = n // inner
    rows, lanes = packed.shape
    return pl.pallas_call(
        partial(allreduce_kernel, inner, outer),
        out_shape=jax.ShapeDtypeStruct((rows, lanes), jnp.float32),
        in_specs=[pl.BlockSpec(memory_space=pltpu.VMEM)],
        out_specs=pl.BlockSpec(memory_space=pltpu.VMEM),
        scratch_shapes=[
            pltpu.VMEM((inner, rows, lanes), jnp.float32),
            pltpu.VMEM((outer, rows, lanes), jnp.float32),
            pltpu.SemaphoreType.DMA((inner,)),
            pltpu.SemaphoreType.DMA((inner,)),
            pltpu.SemaphoreType.DMA((outer,)),
            pltpu.SemaphoreType.DMA((outer,)),
        ],
        compiler_params=pltpu.CompilerParams(collective_id=collective_id, has_side_effects=True),
    )(packed)


def gather_kernel(rows, cols, blocks, half, v_ref, near_ref, far_ref, slices, far_buf,
                  first_send, first_recv, second_send, second_recv, local_sems):
    me = lax.axis_index("row")
    col = lax.axis_index("col")
    width = slices.shape[-1]
    barrier = pltpu.get_barrier_semaphore()

    def row_peer(d):
        return (lax.rem(me + d, rows), col)

    def col_peer(e):
        return (me, lax.rem(col + e, cols))

    def window(c):
        return pl.ds(pl.multiple_of(c * width, width), width)

    own = v_ref.at[:, window(col)]

    def first(d):
        return pltpu.make_async_remote_copy(
            src_ref=own,
            dst_ref=slices.at[d],
            send_sem=first_send.at[d],
            recv_sem=first_recv.at[d],
            device_id=row_peer(d),
            device_id_type=MESH,
        )

    def second(t):
        e = 1 + t // blocks
        n = t % blocks
        target = lax.rem(col + e, cols)
        slot = lax.rem(me + rows - blocks * target - n, rows)
        return pltpu.make_async_remote_copy(
            src_ref=slices.at[slot],
            dst_ref=far_buf.at[n, :, window(col)],
            send_sem=second_send.at[t],
            recv_sem=second_recv.at[t],
            device_id=col_peer(e),
            device_id_type=MESH,
        )

    def greet_row(d, carry):
        pl.semaphore_signal(barrier, inc=1, device_id=row_peer(d), device_id_type=MESH)
        return carry

    def greet_col(e, carry):
        pl.semaphore_signal(barrier, inc=1, device_id=col_peer(e), device_id_type=MESH)
        return carry

    def start_first(d, carry):
        first(d).start()
        return carry

    def finish_second(t, carry):
        second(t).wait()
        return carry

    def arrived(slot):
        pltpu.make_async_remote_copy(
            src_ref=own,
            dst_ref=slices.at[slot],
            send_sem=first_send.at[slot],
            recv_sem=first_recv.at[slot],
            device_id=row_peer(slot),
            device_id_type=MESH,
        ).wait_recv()

    def forward(t, carry):
        target = lax.rem(col + 1 + t // blocks, cols)
        arrived(lax.rem(me + rows - blocks * target - t % blocks, rows))
        second(t).start()
        return carry

    def sent_first(d, carry):
        first(d).wait_send()
        return carry

    lax.fori_loop(1, rows, greet_row, 0)
    lax.fori_loop(1, cols, greet_col, 0)
    pl.semaphore_wait(barrier, rows - 1 + cols - 1)
    lax.fori_loop(1, rows, start_first, 0)
    pltpu.make_async_copy(own, slices.at[0], first_recv.at[0]).start()
    lax.fori_loop(0, (cols - 1) * blocks, forward, 0)
    mine = []
    for n in range(blocks):
        slot = lax.rem(me + rows - blocks * col - n, rows)
        arrived(slot)
        copy = pltpu.make_async_copy(slices.at[slot], far_buf.at[n, :, window(col)], local_sems.at[n])
        copy.start()
        mine.append(copy)
    lax.fori_loop(1, rows, sent_first, 0)
    for k in range(2 * half):
        near_ref[k] = slices[(half - k) % rows]
    lax.fori_loop(0, (cols - 1) * blocks, finish_second, 0)
    for copy in mine:
        copy.wait()
    far_ref[...] = far_buf[...]


def gather_pieces(vector, blocks, half, width, collective_id):
    rows = lax.axis_size("row")
    cols = lax.axis_size("col")
    parts, fields, elements = vector.shape
    flat = vector.reshape(parts * fields, elements)
    near, far = pl.pallas_call(
        partial(gather_kernel, rows, cols, blocks, half),
        out_shape=(
            jax.ShapeDtypeStruct((2 * half, parts * fields, width), vector.dtype),
            jax.ShapeDtypeStruct((blocks, parts * fields, elements), vector.dtype),
        ),
        in_specs=[pl.BlockSpec(memory_space=pltpu.VMEM)],
        out_specs=(pl.BlockSpec(memory_space=pltpu.VMEM), pl.BlockSpec(memory_space=pltpu.VMEM)),
        scratch_shapes=[
            pltpu.VMEM((rows, parts * fields, width), vector.dtype),
            pltpu.VMEM((blocks, parts * fields, elements), vector.dtype),
            pltpu.SemaphoreType.DMA((rows,)),
            pltpu.SemaphoreType.DMA((rows,)),
            pltpu.SemaphoreType.DMA(((cols - 1) * blocks,)),
            pltpu.SemaphoreType.DMA(((cols - 1) * blocks,)),
            pltpu.SemaphoreType.DMA((blocks + 1,)),
        ],
        compiler_params=pltpu.CompilerParams(collective_id=collective_id, has_side_effects=True),
    )(flat)
    return (
        near.reshape(2 * half, parts, fields, width),
        far.reshape(blocks, parts, fields, elements),
    )


def reduce_kernel(cols, x_ref, o_ref, parts_buf, full, first_send, first_recv, second_send, second_recv):
    me = lax.axis_index("row")
    col = lax.axis_index("col")
    width = parts_buf.shape[-1]
    barrier = pltpu.get_barrier_semaphore()

    def col_peer(e):
        return (me, lax.rem(col + e, cols))

    def window(c):
        return pl.ds(pl.multiple_of(c * width, width), width)

    def first(e):
        return pltpu.make_async_remote_copy(
            src_ref=x_ref.at[:, window(lax.rem(col + e, cols))],
            dst_ref=parts_buf.at[e],
            send_sem=first_send.at[e],
            recv_sem=first_recv.at[e],
            device_id=col_peer(e),
            device_id_type=MESH,
        )

    def second(e):
        return pltpu.make_async_remote_copy(
            src_ref=full.at[:, window(col)],
            dst_ref=full.at[:, window(col)],
            send_sem=second_send.at[e],
            recv_sem=second_recv.at[e],
            device_id=col_peer(e),
            device_id_type=MESH,
        )

    def greet(e, carry):
        pl.semaphore_signal(barrier, inc=1, device_id=col_peer(e), device_id_type=MESH)
        return carry

    def start_first(e, carry):
        first(e).start()
        return carry

    def finish_first(e, carry):
        first(e).wait()
        return carry

    def start_second(e, carry):
        second(e).start()
        return carry

    def finish_second(e, carry):
        second(e).wait_send()
        pltpu.make_async_remote_copy(
            src_ref=full.at[:, window(col)],
            dst_ref=full.at[:, window(lax.rem(col + cols - e, cols))],
            send_sem=second_send.at[e],
            recv_sem=second_recv.at[e],
            device_id=col_peer(e),
            device_id_type=MESH,
        ).wait_recv()
        return carry

    def add(source, total):
        return total + parts_buf[lax.rem(col + cols - source, cols)]

    lax.fori_loop(1, cols, greet, 0)
    pl.semaphore_wait(barrier, cols - 1)
    lax.fori_loop(1, cols, start_first, 0)
    parts_buf[0] = x_ref[:, window(col)]
    lax.fori_loop(1, cols, finish_first, 0)
    full[:, window(col)] = lax.fori_loop(1, cols, add, parts_buf[col])
    lax.fori_loop(1, cols, start_second, 0)
    lax.fori_loop(1, cols, finish_second, 0)
    o_ref[...] = full[...]


def col_reduce(partial_sum, collective_id):
    cols = lax.axis_size("col")
    parts, fields, elements = partial_sum.shape
    width = elements // cols
    flat = partial_sum.reshape(parts * fields, elements)
    summed = pl.pallas_call(
        partial(reduce_kernel, cols),
        out_shape=jax.ShapeDtypeStruct(flat.shape, jnp.float32),
        in_specs=[pl.BlockSpec(memory_space=pltpu.VMEM)],
        out_specs=pl.BlockSpec(memory_space=pltpu.VMEM),
        scratch_shapes=[
            pltpu.VMEM((cols, parts * fields, width), jnp.float32),
            pltpu.VMEM((parts * fields, elements), jnp.float32),
            pltpu.SemaphoreType.DMA((cols,)),
            pltpu.SemaphoreType.DMA((cols,)),
            pltpu.SemaphoreType.DMA((cols,)),
            pltpu.SemaphoreType.DMA((cols,)),
        ],
        compiler_params=pltpu.CompilerParams(collective_id=collective_id, has_side_effects=True),
    )(flat)
    return summed.reshape(partial_sum.shape)


def row_psum(ids, *arrays):
    flat = [a.reshape(-1) for a in arrays]
    sizes = [f.shape[0] for f in flat]
    total = sum(sizes)
    padded = -(-total // 1024) * 1024
    packed = jnp.concatenate(flat + [jnp.zeros((padded - total,), jnp.float32)]).reshape(-1, 128)
    summed = row_allreduce(packed, len(ids)).reshape(-1)
    ids.append(None)
    outs = []
    start = 0
    for a, size in zip(arrays, sizes):
        outs.append(summed[start : start + size].reshape(a.shape))
        start += size
    return outs[0] if len(outs) == 1 else tuple(outs)


def complex_lhs(values, part_axis):
    real = jnp.take(values, 0, axis=part_axis)
    imag = jnp.take(values, 1, axis=part_axis)
    return jnp.stack([jnp.stack([real, -imag]), jnp.stack([imag, real])])


def inner_products(first, second):
    return jnp.einsum("csn,ctn->st", first, second, precision=highest)


def combine_rows(matrix, vectors):
    return jnp.einsum("st,ctn->csn", matrix, vectors, precision=highest)


def matmul(left, right):
    return jnp.dot(left, right, precision=highest)


def lower_inverse(lower):
    identity = jnp.eye(lower.shape[0], dtype=lower.dtype)
    return lax.linalg.triangular_solve(lower, identity, left_side=True, lower=True)


def project(harmonics, vectors):

    def contract(left, right):
        return jnp.einsum("mn,sn->ms", left, right, precision=highest)

    real_out = contract(harmonics[0], vectors[0]) + contract(harmonics[1], vectors[1])
    imag_out = contract(harmonics[0], vectors[1]) - contract(harmonics[1], vectors[0])
    return jnp.stack([real_out, imag_out])


def body(incident, diagonal, near_blocks, left_factors, right_factors, flags, ranks, harmonics):
    blocks = left_factors.shape[1]
    slots = near_blocks.shape[1]
    width = near_blocks.shape[4]
    half_band = slots // 2
    elements = incident.shape[2]
    fields = incident.shape[1]
    clusters = lax.axis_size("row")
    row_index = lax.axis_index("row")
    column = lax.axis_index("col")
    ids = []

    def operator_terms(near_pieces, far_pieces):
        near_on = flags[0] == 1
        near_vector = jnp.where(near_on[:, None, None, None], near_pieces, 0).astype(jnp.bfloat16)
        near_out = jnp.einsum(
            "caksf,kaef->cse",
            complex_lhs(near_vector, 1),
            near_blocks[0],
            preferred_element_type=jnp.float32,
        )
        cluster = column * blocks + jnp.arange(blocks, dtype=jnp.int32)
        offset = (cluster - row_index + half_band) % clusters
        is_near = (offset < slots) & (flags[0, jnp.minimum(offset, slots - 1)] == 1)
        keep = (~is_near)[:, None] & (
            jnp.arange(right_factors.shape[3], dtype=jnp.int32)[None, :] < ranks[0][:, None]
        )
        coeffs = jnp.einsum(
            "cansf,narf->cnsr",
            complex_lhs(far_pieces, 1),
            right_factors[0],
            preferred_element_type=jnp.float32,
        )
        coeffs = jnp.where(keep[None, :, None, :], coeffs, 0.0).astype(jnp.bfloat16)
        far_out = jnp.einsum(
            "cansr,nare->cse",
            complex_lhs(coeffs, 0),
            left_factors[0],
            preferred_element_type=jnp.float32,
        )
        return near_out + far_out

    def apply_operator(vector):
        rounded = vector.astype(jnp.bfloat16)
        near_pieces, far_pieces = gather_pieces(rounded, blocks, half_band, width, 16 + len(ids))
        ids.append(None)
        total = operator_terms(near_pieces, far_pieces)
        summed = col_reduce(total, 32 + len(ids))
        ids.append(None)
        return summed + diagonal[None, None, :] * vector

    lower_first = jnp.linalg.cholesky(row_psum(ids, inner_products(incident, incident)))
    basis_one = combine_rows(lower_inverse(lower_first), incident)
    image = apply_operator(basis_one)
    coupling_one, harmonics_one, self_one = row_psum(
        ids,
        inner_products(image, basis_one),
        project(harmonics, basis_one),
        inner_products(basis_one, basis_one),
    )
    rest = image - combine_rows(coupling_one, basis_one)
    gram_one = row_psum(ids, inner_products(rest, rest))
    lower_second = jnp.linalg.cholesky(gram_one)
    basis_two = combine_rows(lower_inverse(lower_second), rest)
    image = apply_operator(basis_two)
    coupling_onetwo, coupling_two, image_gram, cross, self_two, harmonics_two = row_psum(
        ids,
        inner_products(image, basis_one),
        inner_products(image, basis_two),
        inner_products(image, image),
        inner_products(basis_one, basis_two),
        inner_products(basis_two, basis_two),
        project(harmonics, basis_two),
    )
    coupling = jnp.concatenate([coupling_onetwo, coupling_two], axis=1)
    basis_gram = jnp.concatenate(
        [
            jnp.concatenate([self_one, cross], axis=1),
            jnp.concatenate([cross.T, self_two], axis=1),
        ],
        axis=0,
    )
    gram_two = (
        image_gram
        - 2.0 * matmul(coupling, coupling.T)
        + matmul(coupling, matmul(basis_gram, coupling.T))
    )
    upper_left = matmul(coupling_one, coupling_one.T) + gram_one
    upper_right = matmul(coupling_one, coupling_onetwo.T) + matmul(lower_second, coupling_two.T)
    lower_right = (
        matmul(coupling_onetwo, coupling_onetwo.T) + matmul(coupling_two, coupling_two.T) + gram_two
    )
    normal = jnp.concatenate(
        [
            jnp.concatenate([upper_left, upper_right], axis=1),
            jnp.concatenate([upper_right.T, lower_right], axis=1),
        ],
        axis=0,
    )
    target = jnp.concatenate(
        [matmul(lower_first, coupling_one.T), matmul(lower_first, coupling_onetwo.T)], axis=1
    )
    factor_inverse = lower_inverse(jnp.linalg.cholesky(normal))
    weights = matmul(factor_inverse.T, matmul(factor_inverse, target.T)).T
    first_weights = weights[:, :fields]
    second_weights = weights[:, fields:]
    solution = combine_rows(first_weights, basis_one) + combine_rows(second_weights, basis_two)
    coefficients = jnp.einsum(
        "cmt,st->cms", harmonics_one, first_weights, precision=highest
    ) + jnp.einsum("cmt,st->cms", harmonics_two, second_weights, precision=highest)
    return (solution, coefficients)


def solution(mesh):
    in_specs = (
        P(None, None, "row"),
        P("row"),
        P("row", None, None, None, "col"),
        P("row", "col", None, None, None),
        P("row", "col", None, None, None),
        P("row", None),
        P("row", "col"),
        P(None, None, "row"),
    )
    out_specs = (P(None, None, "row"), P())
    return jax.shard_map(body, mesh=mesh, in_specs=in_specs, out_specs=out_specs, check_vma=False)
```

```python
from functools import partial

import jax
import jax.numpy as jnp
from jax import lax
from jax.experimental import pallas as pl
from jax.experimental.pallas import tpu as pltpu
from jax.sharding import PartitionSpec as P

highest = lax.Precision.HIGHEST
MESH = pl.DeviceIdType.MESH


def allreduce_kernel(inner, outer, x_ref, o_ref, buf, partial_buf,
                     first_send, first_recv, second_send, second_recv):
    me = lax.axis_index("row")
    col = lax.axis_index("col")
    high = me // inner
    low = me % inner
    barrier = pltpu.get_barrier_semaphore()

    def inner_peer(d):
        return (high * inner + lax.rem(low + d, inner), col)

    def outer_peer(d):
        return (lax.rem(high + d, outer) * inner + low, col)

    def first(d):
        return pltpu.make_async_remote_copy(
            src_ref=x_ref,
            dst_ref=buf.at[d],
            send_sem=first_send.at[d],
            recv_sem=first_recv.at[d],
            device_id=inner_peer(d),
            device_id_type=MESH,
        )

    def second(d):
        return pltpu.make_async_remote_copy(
            src_ref=partial_buf.at[0],
            dst_ref=partial_buf.at[d],
            send_sem=second_send.at[d],
            recv_sem=second_recv.at[d],
            device_id=outer_peer(d),
            device_id_type=MESH,
        )

    def greet_inner(d, carry):
        pl.semaphore_signal(barrier, inc=1, device_id=inner_peer(d), device_id_type=MESH)
        return carry

    def greet_outer(d, carry):
        pl.semaphore_signal(barrier, inc=1, device_id=outer_peer(d), device_id_type=MESH)
        return carry

    def start_first(d, carry):
        first(d).start()
        return carry

    def finish_first(d, carry):
        first(d).wait()
        return carry

    def start_second(d, carry):
        second(d).start()
        return carry

    def finish_second(d, carry):
        second(d).wait()
        return carry

    def add_inner(source, total):
        return total + buf[lax.rem(low + inner - source, inner)]

    def add_outer(source, total):
        return total + partial_buf[lax.rem(high + outer - source, outer)]

    lax.fori_loop(1, inner, greet_inner, 0)
    lax.fori_loop(1, outer, greet_outer, 0)
    pl.semaphore_wait(barrier, inner - 1 + outer - 1)
    lax.fori_loop(1, inner, start_first, 0)
    buf[0] = x_ref[...]
    lax.fori_loop(1, inner, finish_first, 0)
    partial_buf[0] = lax.fori_loop(1, inner, add_inner, buf[low])
    lax.fori_loop(1, outer, start_second, 0)
    lax.fori_loop(1, outer, finish_second, 0)
    o_ref[...] = lax.fori_loop(1, outer, add_outer, partial_buf[high])


def row_allreduce(packed, collective_id):
    n = lax.axis_size("row")
    inner = 8 if n % 8 == 0 else n
    outer = n // inner
    rows, lanes = packed.shape
    return pl.pallas_call(
        partial(allreduce_kernel, inner, outer),
        out_shape=jax.ShapeDtypeStruct((rows, lanes), jnp.float32),
        in_specs=[pl.BlockSpec(memory_space=pltpu.VMEM)],
        out_specs=pl.BlockSpec(memory_space=pltpu.VMEM),
        scratch_shapes=[
            pltpu.VMEM((inner, rows, lanes), jnp.float32),
            pltpu.VMEM((outer, rows, lanes), jnp.float32),
            pltpu.SemaphoreType.DMA((inner,)),
            pltpu.SemaphoreType.DMA((inner,)),
            pltpu.SemaphoreType.DMA((outer,)),
            pltpu.SemaphoreType.DMA((outer,)),
        ],
        compiler_params=pltpu.CompilerParams(collective_id=collective_id, has_side_effects=True),
    )(packed)


def gram(left, right):
    return lax.dot_general(
        left, right, (((1,), (1,)), ((), ())), precision=highest, preferred_element_type=jnp.float32
    )


def gather_kernel(rows, cols, blocks, half, v_ref, one_ref, cur_ref, harm_ref,
                  near_ref, far_ref, cross_ref, self_ref, proj_ref, slices, far_buf,
                  first_send, first_recv, second_send, second_recv, local_sems):
    me = lax.axis_index("row")
    col = lax.axis_index("col")
    width = slices.shape[-1]
    barrier = pltpu.get_barrier_semaphore()

    def row_peer(d):
        return (lax.rem(me + d, rows), col)

    def col_peer(e):
        return (me, lax.rem(col + e, cols))

    def window(c):
        return pl.ds(pl.multiple_of(c * width, width), width)

    own = v_ref.at[:, window(col)]

    def first(d):
        return pltpu.make_async_remote_copy(
            src_ref=own,
            dst_ref=slices.at[d],
            send_sem=first_send.at[d],
            recv_sem=first_recv.at[d],
            device_id=row_peer(d),
            device_id_type=MESH,
        )

    def second(t):
        e = 1 + t // blocks
        n = t % blocks
        target = lax.rem(col + e, cols)
        slot = lax.rem(me + rows - blocks * target - n, rows)
        return pltpu.make_async_remote_copy(
            src_ref=slices.at[slot],
            dst_ref=far_buf.at[n, :, window(col)],
            send_sem=second_send.at[t],
            recv_sem=second_recv.at[t],
            device_id=col_peer(e),
            device_id_type=MESH,
        )

    def greet_row(d, carry):
        pl.semaphore_signal(barrier, inc=1, device_id=row_peer(d), device_id_type=MESH)
        return carry

    def greet_col(e, carry):
        pl.semaphore_signal(barrier, inc=1, device_id=col_peer(e), device_id_type=MESH)
        return carry

    def start_first(d, carry):
        first(d).start()
        return carry

    def finish_second(t, carry):
        second(t).wait()
        return carry

    def arrived(slot):
        pltpu.make_async_remote_copy(
            src_ref=own,
            dst_ref=slices.at[slot],
            send_sem=first_send.at[slot],
            recv_sem=first_recv.at[slot],
            device_id=row_peer(slot),
            device_id_type=MESH,
        ).wait_recv()

    def forward(t, carry):
        target = lax.rem(col + 1 + t // blocks, cols)
        arrived(lax.rem(me + rows - blocks * target - t % blocks, rows))
        second(t).start()
        return carry

    def sent_first(d, carry):
        first(d).wait_send()
        return carry

    lax.fori_loop(1, rows, greet_row, 0)
    lax.fori_loop(1, cols, greet_col, 0)
    pl.semaphore_wait(barrier, rows - 1 + cols - 1)
    lax.fori_loop(1, rows, start_first, 0)
    pltpu.make_async_copy(own, slices.at[0], first_recv.at[0]).start()
    cross_ref[...] = gram(one_ref[0], cur_ref[0]) + gram(one_ref[1], cur_ref[1])
    self_ref[...] = gram(cur_ref[0], cur_ref[0]) + gram(cur_ref[1], cur_ref[1])
    proj_ref[0] = gram(harm_ref[0], cur_ref[0]) + gram(harm_ref[1], cur_ref[1])
    proj_ref[1] = gram(harm_ref[0], cur_ref[1]) - gram(harm_ref[1], cur_ref[0])
    lax.fori_loop(0, (cols - 1) * blocks, forward, 0)
    mine = []
    for n in range(blocks):
        slot = lax.rem(me + rows - blocks * col - n, rows)
        arrived(slot)
        copy = pltpu.make_async_copy(slices.at[slot], far_buf.at[n, :, window(col)], local_sems.at[n])
        copy.start()
        mine.append(copy)
    lax.fori_loop(1, rows, sent_first, 0)
    for k in range(2 * half):
        near_ref[k] = slices[(half - k) % rows]
    lax.fori_loop(0, (cols - 1) * blocks, finish_second, 0)
    for copy in mine:
        copy.wait()
    far_ref[...] = far_buf[...]


def gather_pieces(vector, basis_one, basis, harmonics, blocks, half, width, collective_id):
    rows = lax.axis_size("row")
    cols = lax.axis_size("col")
    parts, fields, elements = vector.shape
    flat = vector.reshape(parts * fields, elements)
    near, far, cross, self_gram, proj = pl.pallas_call(
        partial(gather_kernel, rows, cols, blocks, half),
        out_shape=(
            jax.ShapeDtypeStruct((2 * half, parts * fields, width), vector.dtype),
            jax.ShapeDtypeStruct((blocks, parts * fields, elements), vector.dtype),
            jax.ShapeDtypeStruct((fields, fields), jnp.float32),
            jax.ShapeDtypeStruct((fields, fields), jnp.float32),
            jax.ShapeDtypeStruct((2, harmonics.shape[1], fields), jnp.float32),
        ),
        in_specs=[pl.BlockSpec(memory_space=pltpu.VMEM)] * 4,
        out_specs=tuple(pl.BlockSpec(memory_space=pltpu.VMEM) for _ in range(5)),
        scratch_shapes=[
            pltpu.VMEM((rows, parts * fields, width), vector.dtype),
            pltpu.VMEM((blocks, parts * fields, elements), vector.dtype),
            pltpu.SemaphoreType.DMA((rows,)),
            pltpu.SemaphoreType.DMA((rows,)),
            pltpu.SemaphoreType.DMA(((cols - 1) * blocks,)),
            pltpu.SemaphoreType.DMA(((cols - 1) * blocks,)),
            pltpu.SemaphoreType.DMA((blocks + 1,)),
        ],
        compiler_params=pltpu.CompilerParams(collective_id=collective_id, has_side_effects=True),
    )(flat, basis_one, basis, harmonics)
    return (
        near.reshape(2 * half, parts, fields, width),
        far.reshape(blocks, parts, fields, elements),
        cross,
        self_gram,
        proj,
    )


def reduce_kernel(cols, x_ref, o_ref, parts_buf, full, first_send, first_recv, second_send, second_recv):
    me = lax.axis_index("row")
    col = lax.axis_index("col")
    width = parts_buf.shape[-1]
    barrier = pltpu.get_barrier_semaphore()

    def col_peer(e):
        return (me, lax.rem(col + e, cols))

    def window(c):
        return pl.ds(pl.multiple_of(c * width, width), width)

    def first(e):
        return pltpu.make_async_remote_copy(
            src_ref=x_ref.at[:, window(lax.rem(col + e, cols))],
            dst_ref=parts_buf.at[e],
            send_sem=first_send.at[e],
            recv_sem=first_recv.at[e],
            device_id=col_peer(e),
            device_id_type=MESH,
        )

    def second(e):
        return pltpu.make_async_remote_copy(
            src_ref=full.at[:, window(col)],
            dst_ref=full.at[:, window(col)],
            send_sem=second_send.at[e],
            recv_sem=second_recv.at[e],
            device_id=col_peer(e),
            device_id_type=MESH,
        )

    def greet(e, carry):
        pl.semaphore_signal(barrier, inc=1, device_id=col_peer(e), device_id_type=MESH)
        return carry

    def start_first(e, carry):
        first(e).start()
        return carry

    def finish_first(e, carry):
        first(e).wait()
        return carry

    def start_second(e, carry):
        second(e).start()
        return carry

    def finish_second(e, carry):
        second(e).wait_send()
        pltpu.make_async_remote_copy(
            src_ref=full.at[:, window(col)],
            dst_ref=full.at[:, window(lax.rem(col + cols - e, cols))],
            send_sem=second_send.at[e],
            recv_sem=second_recv.at[e],
            device_id=col_peer(e),
            device_id_type=MESH,
        ).wait_recv()
        return carry

    def add(source, total):
        return total + parts_buf[lax.rem(col + cols - source, cols)]

    lax.fori_loop(1, cols, greet, 0)
    pl.semaphore_wait(barrier, cols - 1)
    lax.fori_loop(1, cols, start_first, 0)
    parts_buf[0] = x_ref[:, window(col)]
    lax.fori_loop(1, cols, finish_first, 0)
    full[:, window(col)] = lax.fori_loop(1, cols, add, parts_buf[col])
    lax.fori_loop(1, cols, start_second, 0)
    lax.fori_loop(1, cols, finish_second, 0)
    o_ref[...] = full[...]


def col_reduce(partial_sum, collective_id):
    cols = lax.axis_size("col")
    parts, fields, elements = partial_sum.shape
    width = elements // cols
    flat = partial_sum.reshape(parts * fields, elements)
    summed = pl.pallas_call(
        partial(reduce_kernel, cols),
        out_shape=jax.ShapeDtypeStruct(flat.shape, jnp.float32),
        in_specs=[pl.BlockSpec(memory_space=pltpu.VMEM)],
        out_specs=pl.BlockSpec(memory_space=pltpu.VMEM),
        scratch_shapes=[
            pltpu.VMEM((cols, parts * fields, width), jnp.float32),
            pltpu.VMEM((parts * fields, elements), jnp.float32),
            pltpu.SemaphoreType.DMA((cols,)),
            pltpu.SemaphoreType.DMA((cols,)),
            pltpu.SemaphoreType.DMA((cols,)),
            pltpu.SemaphoreType.DMA((cols,)),
        ],
        compiler_params=pltpu.CompilerParams(collective_id=collective_id, has_side_effects=True),
    )(flat)
    return summed.reshape(partial_sum.shape)


def row_psum(ids, *arrays):
    flat = [a.reshape(-1) for a in arrays]
    sizes = [f.shape[0] for f in flat]
    total = sum(sizes)
    padded = -(-total // 1024) * 1024
    packed = jnp.concatenate(flat + [jnp.zeros((padded - total,), jnp.float32)]).reshape(-1, 128)
    summed = row_allreduce(packed, len(ids)).reshape(-1)
    ids.append(None)
    outs = []
    start = 0
    for a, size in zip(arrays, sizes):
        outs.append(summed[start : start + size].reshape(a.shape))
        start += size
    return outs[0] if len(outs) == 1 else tuple(outs)


def complex_lhs(values, part_axis):
    real = jnp.take(values, 0, axis=part_axis)
    imag = jnp.take(values, 1, axis=part_axis)
    return jnp.stack([jnp.stack([real, -imag]), jnp.stack([imag, real])])


def inner_products(first, second):
    return jnp.einsum("csn,ctn->st", first, second, precision=highest)


def combine_rows(matrix, vectors):
    return jnp.einsum("st,ctn->csn", matrix, vectors, precision=highest)


def matmul(left, right):
    return jnp.dot(left, right, precision=highest)


def lower_inverse(lower):
    identity = jnp.eye(lower.shape[0], dtype=lower.dtype)
    return lax.linalg.triangular_solve(lower, identity, left_side=True, lower=True)


def project(harmonics, vectors):

    def contract(left, right):
        return jnp.einsum("mn,sn->ms", left, right, precision=highest)

    real_out = contract(harmonics[0], vectors[0]) + contract(harmonics[1], vectors[1])
    imag_out = contract(harmonics[0], vectors[1]) - contract(harmonics[1], vectors[0])
    return jnp.stack([real_out, imag_out])


def body(incident, diagonal, near_blocks, left_factors, right_factors, flags, ranks, harmonics):
    blocks = left_factors.shape[1]
    slots = near_blocks.shape[1]
    width = near_blocks.shape[4]
    half_band = slots // 2
    elements = incident.shape[2]
    fields = incident.shape[1]
    clusters = lax.axis_size("row")
    row_index = lax.axis_index("row")
    column = lax.axis_index("col")
    ids = []

    def operator_terms(near_pieces, far_pieces):
        near_on = flags[0] == 1
        near_vector = jnp.where(near_on[:, None, None, None], near_pieces, 0).astype(jnp.bfloat16)
        near_out = jnp.einsum(
            "caksf,kaef->cse",
            complex_lhs(near_vector, 1),
            near_blocks[0],
            preferred_element_type=jnp.float32,
        )
        cluster = column * blocks + jnp.arange(blocks, dtype=jnp.int32)
        offset = (cluster - row_index + half_band) % clusters
        is_near = (offset < slots) & (flags[0, jnp.minimum(offset, slots - 1)] == 1)
        keep = (~is_near)[:, None] & (
            jnp.arange(right_factors.shape[3], dtype=jnp.int32)[None, :] < ranks[0][:, None]
        )
        coeffs = jnp.einsum(
            "cansf,narf->cnsr",
            complex_lhs(far_pieces, 1),
            right_factors[0],
            preferred_element_type=jnp.float32,
        )
        coeffs = jnp.where(keep[None, :, None, :], coeffs, 0.0).astype(jnp.bfloat16)
        far_out = jnp.einsum(
            "cansr,nare->cse",
            complex_lhs(coeffs, 0),
            left_factors[0],
            preferred_element_type=jnp.float32,
        )
        return near_out + far_out

    def apply_operator(vector, basis_one):
        rounded = vector.astype(jnp.bfloat16)
        near_pieces, far_pieces, cross, self_gram, proj = gather_pieces(
            rounded, basis_one, vector, harmonics, blocks, half_band, width, 16 + len(ids)
        )
        ids.append(None)
        total = operator_terms(near_pieces, far_pieces)
        summed = col_reduce(total, 32 + len(ids))
        ids.append(None)
        return summed + diagonal[None, None, :] * vector, cross, self_gram, proj

    lower_first = jnp.linalg.cholesky(row_psum(ids, inner_products(incident, incident)))
    basis_one = combine_rows(lower_inverse(lower_first), incident)
    image, _, self_one, harmonics_one = apply_operator(basis_one, basis_one)
    coupling_one, harmonics_one, self_one = row_psum(
        ids, inner_products(image, basis_one), harmonics_one, self_one
    )
    rest = image - combine_rows(coupling_one, basis_one)
    gram_one = row_psum(ids, inner_products(rest, rest))
    lower_second = jnp.linalg.cholesky(gram_one)
    basis_two = combine_rows(lower_inverse(lower_second), rest)
    image, cross, self_two, harmonics_two = apply_operator(basis_two, basis_one)
    coupling_onetwo, coupling_two, image_gram, cross, self_two, harmonics_two = row_psum(
        ids,
        inner_products(image, basis_one),
        inner_products(image, basis_two),
        inner_products(image, image),
        cross,
        self_two,
        harmonics_two,
    )
    coupling = jnp.concatenate([coupling_onetwo, coupling_two], axis=1)
    basis_gram = jnp.concatenate(
        [
            jnp.concatenate([self_one, cross], axis=1),
            jnp.concatenate([cross.T, self_two], axis=1),
        ],
        axis=0,
    )
    gram_two = (
        image_gram
        - 2.0 * matmul(coupling, coupling.T)
        + matmul(coupling, matmul(basis_gram, coupling.T))
    )
    upper_left = matmul(coupling_one, coupling_one.T) + gram_one
    upper_right = matmul(coupling_one, coupling_onetwo.T) + matmul(lower_second, coupling_two.T)
    lower_right = (
        matmul(coupling_onetwo, coupling_onetwo.T) + matmul(coupling_two, coupling_two.T) + gram_two
    )
    normal = jnp.concatenate(
        [
            jnp.concatenate([upper_left, upper_right], axis=1),
            jnp.concatenate([upper_right.T, lower_right], axis=1),
        ],
        axis=0,
    )
    target = jnp.concatenate(
        [matmul(lower_first, coupling_one.T), matmul(lower_first, coupling_onetwo.T)], axis=1
    )
    factor_inverse = lower_inverse(jnp.linalg.cholesky(normal))
    weights = matmul(factor_inverse.T, matmul(factor_inverse, target.T)).T
    first_weights = weights[:, :fields]
    second_weights = weights[:, fields:]
    solution = combine_rows(first_weights, basis_one) + combine_rows(second_weights, basis_two)
    coefficients = jnp.einsum(
        "cmt,st->cms", harmonics_one, first_weights, precision=highest
    ) + jnp.einsum("cmt,st->cms", harmonics_two, second_weights, precision=highest)
    return (solution, coefficients)


def solution(mesh):
    in_specs = (
        P(None, None, "row"),
        P("row"),
        P("row", None, None, None, "col"),
        P("row", "col", None, None, None),
        P("row", "col", None, None, None),
        P("row", None),
        P("row", "col"),
        P(None, None, "row"),
    )
    out_specs = (P(None, None, "row"), P())
    return jax.shard_map(body, mesh=mesh, in_specs=in_specs, out_specs=out_specs, check_vma=False)
```

```python
from functools import partial

import jax
import jax.numpy as jnp
from jax import lax
from jax.experimental import pallas as pl
from jax.experimental.pallas import tpu as pltpu
from jax.sharding import PartitionSpec as P

highest = lax.Precision.HIGHEST
MESH = pl.DeviceIdType.MESH


def allreduce_kernel(inner, outer, x_ref, o_ref, buf, partial_buf,
                     first_send, first_recv, second_send, second_recv):
    me = lax.axis_index("row")
    col = lax.axis_index("col")
    high = me // inner
    low = me % inner
    barrier = pltpu.get_barrier_semaphore()

    def inner_peer(d):
        return (high * inner + lax.rem(low + d, inner), col)

    def outer_peer(d):
        return (lax.rem(high + d, outer) * inner + low, col)

    def first(d):
        return pltpu.make_async_remote_copy(
            src_ref=x_ref,
            dst_ref=buf.at[d],
            send_sem=first_send.at[d],
            recv_sem=first_recv.at[d],
            device_id=inner_peer(d),
            device_id_type=MESH,
        )

    def second(d):
        return pltpu.make_async_remote_copy(
            src_ref=partial_buf.at[0],
            dst_ref=partial_buf.at[d],
            send_sem=second_send.at[d],
            recv_sem=second_recv.at[d],
            device_id=outer_peer(d),
            device_id_type=MESH,
        )

    def greet_inner(d, carry):
        pl.semaphore_signal(barrier, inc=1, device_id=inner_peer(d), device_id_type=MESH)
        return carry

    def greet_outer(d, carry):
        pl.semaphore_signal(barrier, inc=1, device_id=outer_peer(d), device_id_type=MESH)
        return carry

    def start_first(d, carry):
        first(d).start()
        return carry

    def finish_first(d, carry):
        first(d).wait()
        return carry

    def start_second(d, carry):
        second(d).start()
        return carry

    def finish_second(d, carry):
        second(d).wait()
        return carry

    def add_inner(source, total):
        return total + buf[lax.rem(low + inner - source, inner)]

    def add_outer(source, total):
        return total + partial_buf[lax.rem(high + outer - source, outer)]

    lax.fori_loop(1, inner, greet_inner, 0)
    lax.fori_loop(1, outer, greet_outer, 0)
    pl.semaphore_wait(barrier, inner - 1 + outer - 1)
    lax.fori_loop(1, inner, start_first, 0)
    buf[0] = x_ref[...]
    lax.fori_loop(1, inner, finish_first, 0)
    partial_buf[0] = lax.fori_loop(1, inner, add_inner, buf[low])
    lax.fori_loop(1, outer, start_second, 0)
    lax.fori_loop(1, outer, finish_second, 0)
    o_ref[...] = lax.fori_loop(1, outer, add_outer, partial_buf[high])


def row_allreduce(packed, collective_id):
    n = lax.axis_size("row")
    inner = 8 if n % 8 == 0 else n
    outer = n // inner
    rows, lanes = packed.shape
    return pl.pallas_call(
        partial(allreduce_kernel, inner, outer),
        out_shape=jax.ShapeDtypeStruct((rows, lanes), jnp.float32),
        in_specs=[pl.BlockSpec(memory_space=pltpu.VMEM)],
        out_specs=pl.BlockSpec(memory_space=pltpu.VMEM),
        scratch_shapes=[
            pltpu.VMEM((inner, rows, lanes), jnp.float32),
            pltpu.VMEM((outer, rows, lanes), jnp.float32),
            pltpu.SemaphoreType.DMA((inner,)),
            pltpu.SemaphoreType.DMA((inner,)),
            pltpu.SemaphoreType.DMA((outer,)),
            pltpu.SemaphoreType.DMA((outer,)),
        ],
        compiler_params=pltpu.CompilerParams(collective_id=collective_id, has_side_effects=True),
    )(packed)


def gram(left, right):
    return lax.dot_general(
        left, right, (((1,), (1,)), ((), ())), precision=highest, preferred_element_type=jnp.float32
    )


def gather_kernel(rows, cols, blocks, half, v_ref, one_ref, cur_ref, harm_ref,
                  near_ref, far_ref, cross_ref, self_ref, proj_ref, slices, far_buf,
                  first_send, first_recv, second_send, second_recv, local_sems):
    me = lax.axis_index("row")
    col = lax.axis_index("col")
    width = slices.shape[-1]
    barrier = pltpu.get_barrier_semaphore()

    def row_peer(d):
        return (lax.rem(me + d, rows), col)

    def col_peer(e):
        return (me, lax.rem(col + e, cols))

    def window(c):
        return pl.ds(pl.multiple_of(c * width, width), width)

    own = v_ref.at[:, window(col)]

    def first(d):
        return pltpu.make_async_remote_copy(
            src_ref=own,
            dst_ref=slices.at[d],
            send_sem=first_send.at[d],
            recv_sem=first_recv.at[d],
            device_id=row_peer(d),
            device_id_type=MESH,
        )

    def second(t):
        e = 1 + t // blocks
        n = t % blocks
        target = lax.rem(col + e, cols)
        slot = lax.rem(me + rows - blocks * target - n, rows)
        return pltpu.make_async_remote_copy(
            src_ref=slices.at[slot],
            dst_ref=far_buf.at[n, :, window(col)],
            send_sem=second_send.at[t],
            recv_sem=second_recv.at[t],
            device_id=col_peer(e),
            device_id_type=MESH,
        )

    def greet_row(d, carry):
        pl.semaphore_signal(barrier, inc=1, device_id=row_peer(d), device_id_type=MESH)
        return carry

    def greet_col(e, carry):
        pl.semaphore_signal(barrier, inc=1, device_id=col_peer(e), device_id_type=MESH)
        return carry

    def start_first(d, carry):
        first(d).start()
        return carry

    def finish_second(t, carry):
        second(t).wait()
        return carry

    def arrived(slot):
        pltpu.make_async_remote_copy(
            src_ref=own,
            dst_ref=slices.at[slot],
            send_sem=first_send.at[slot],
            recv_sem=first_recv.at[slot],
            device_id=row_peer(slot),
            device_id_type=MESH,
        ).wait_recv()

    def forward(t, carry):
        target = lax.rem(col + 1 + t // blocks, cols)
        arrived(lax.rem(me + rows - blocks * target - t % blocks, rows))
        second(t).start()
        return carry

    def sent_first(d, carry):
        first(d).wait_send()
        return carry

    lax.fori_loop(1, rows, greet_row, 0)
    lax.fori_loop(1, cols, greet_col, 0)
    pl.semaphore_wait(barrier, rows - 1 + cols - 1)
    lax.fori_loop(1, rows, start_first, 0)
    pltpu.make_async_copy(own, slices.at[0], first_recv.at[0]).start()
    cross_ref[...] = gram(one_ref[0], cur_ref[0]) + gram(one_ref[1], cur_ref[1])
    self_ref[...] = gram(cur_ref[0], cur_ref[0]) + gram(cur_ref[1], cur_ref[1])
    proj_ref[0] = gram(harm_ref[0], cur_ref[0]) + gram(harm_ref[1], cur_ref[1])
    proj_ref[1] = gram(harm_ref[0], cur_ref[1]) - gram(harm_ref[1], cur_ref[0])
    lax.fori_loop(0, (cols - 1) * blocks, forward, 0)
    mine = []
    for n in range(blocks):
        slot = lax.rem(me + rows - blocks * col - n, rows)
        arrived(slot)
        copy = pltpu.make_async_copy(slices.at[slot], far_buf.at[n, :, window(col)], local_sems.at[n])
        copy.start()
        mine.append(copy)
    lax.fori_loop(1, rows, sent_first, 0)
    for k in range(2 * half):
        near_ref[k] = slices[(half - k) % rows]
    lax.fori_loop(0, (cols - 1) * blocks, finish_second, 0)
    for copy in mine:
        copy.wait()
    far_ref[...] = far_buf[...]


def gather_pieces(vector, basis_one, basis, harmonics, blocks, half, width, collective_id):
    rows = lax.axis_size("row")
    cols = lax.axis_size("col")
    parts, fields, elements = vector.shape
    flat = vector.reshape(parts * fields, elements)
    near, far, cross, self_gram, proj = pl.pallas_call(
        partial(gather_kernel, rows, cols, blocks, half),
        out_shape=(
            jax.ShapeDtypeStruct((2 * half, parts * fields, width), vector.dtype),
            jax.ShapeDtypeStruct((blocks, parts * fields, elements), vector.dtype),
            jax.ShapeDtypeStruct((fields, fields), jnp.float32),
            jax.ShapeDtypeStruct((fields, fields), jnp.float32),
            jax.ShapeDtypeStruct((2, harmonics.shape[1], fields), jnp.float32),
        ),
        in_specs=[pl.BlockSpec(memory_space=pltpu.VMEM)] * 4,
        out_specs=tuple(pl.BlockSpec(memory_space=pltpu.VMEM) for _ in range(5)),
        scratch_shapes=[
            pltpu.VMEM((rows, parts * fields, width), vector.dtype),
            pltpu.VMEM((blocks, parts * fields, elements), vector.dtype),
            pltpu.SemaphoreType.DMA((rows,)),
            pltpu.SemaphoreType.DMA((rows,)),
            pltpu.SemaphoreType.DMA(((cols - 1) * blocks,)),
            pltpu.SemaphoreType.DMA(((cols - 1) * blocks,)),
            pltpu.SemaphoreType.DMA((blocks + 1,)),
        ],
        compiler_params=pltpu.CompilerParams(collective_id=collective_id, has_side_effects=True),
    )(flat, basis_one, basis, harmonics)
    return (
        near.reshape(2 * half, parts, fields, width),
        far,
        cross,
        self_gram,
        proj,
    )


def reduce_kernel(cols, x_ref, o_ref, parts_buf, full, first_send, first_recv, second_send, second_recv):
    me = lax.axis_index("row")
    col = lax.axis_index("col")
    width = parts_buf.shape[-1]
    barrier = pltpu.get_barrier_semaphore()

    def col_peer(e):
        return (me, lax.rem(col + e, cols))

    def window(c):
        return pl.ds(pl.multiple_of(c * width, width), width)

    def first(e):
        return pltpu.make_async_remote_copy(
            src_ref=x_ref.at[:, window(lax.rem(col + e, cols))],
            dst_ref=parts_buf.at[e],
            send_sem=first_send.at[e],
            recv_sem=first_recv.at[e],
            device_id=col_peer(e),
            device_id_type=MESH,
        )

    def second(e):
        return pltpu.make_async_remote_copy(
            src_ref=full.at[:, window(col)],
            dst_ref=full.at[:, window(col)],
            send_sem=second_send.at[e],
            recv_sem=second_recv.at[e],
            device_id=col_peer(e),
            device_id_type=MESH,
        )

    def greet(e, carry):
        pl.semaphore_signal(barrier, inc=1, device_id=col_peer(e), device_id_type=MESH)
        return carry

    def start_first(e, carry):
        first(e).start()
        return carry

    def finish_first(e, carry):
        first(e).wait()
        return carry

    def start_second(e, carry):
        second(e).start()
        return carry

    def finish_second(e, carry):
        second(e).wait_send()
        pltpu.make_async_remote_copy(
            src_ref=full.at[:, window(col)],
            dst_ref=full.at[:, window(lax.rem(col + cols - e, cols))],
            send_sem=second_send.at[e],
            recv_sem=second_recv.at[e],
            device_id=col_peer(e),
            device_id_type=MESH,
        ).wait_recv()
        return carry

    def add(source, total):
        return total + parts_buf[lax.rem(col + cols - source, cols)]

    lax.fori_loop(1, cols, greet, 0)
    pl.semaphore_wait(barrier, cols - 1)
    lax.fori_loop(1, cols, start_first, 0)
    parts_buf[0] = x_ref[:, window(col)]
    lax.fori_loop(1, cols, finish_first, 0)
    full[:, window(col)] = lax.fori_loop(1, cols, add, parts_buf[col])
    lax.fori_loop(1, cols, start_second, 0)
    lax.fori_loop(1, cols, finish_second, 0)
    o_ref[...] = full[...]


def col_reduce(partial_sum, collective_id):
    cols = lax.axis_size("col")
    rows, elements = partial_sum.shape
    width = elements // cols
    return pl.pallas_call(
        partial(reduce_kernel, cols),
        out_shape=jax.ShapeDtypeStruct(partial_sum.shape, jnp.float32),
        in_specs=[pl.BlockSpec(memory_space=pltpu.VMEM)],
        out_specs=pl.BlockSpec(memory_space=pltpu.VMEM),
        scratch_shapes=[
            pltpu.VMEM((cols, rows, width), jnp.float32),
            pltpu.VMEM((rows, elements), jnp.float32),
            pltpu.SemaphoreType.DMA((cols,)),
            pltpu.SemaphoreType.DMA((cols,)),
            pltpu.SemaphoreType.DMA((cols,)),
            pltpu.SemaphoreType.DMA((cols,)),
        ],
        compiler_params=pltpu.CompilerParams(collective_id=collective_id, has_side_effects=True),
    )(partial_sum)


def row_psum(ids, *arrays):
    flat = [a.reshape(-1) for a in arrays]
    sizes = [f.shape[0] for f in flat]
    total = sum(sizes)
    padded = -(-total // 1024) * 1024
    packed = jnp.concatenate(flat + [jnp.zeros((padded - total,), jnp.float32)]).reshape(-1, 128)
    summed = row_allreduce(packed, len(ids)).reshape(-1)
    ids.append(None)
    outs = []
    start = 0
    for a, size in zip(arrays, sizes):
        outs.append(summed[start : start + size].reshape(a.shape))
        start += size
    return outs[0] if len(outs) == 1 else tuple(outs)


def complex_lhs(values, part_axis):
    real = jnp.take(values, 0, axis=part_axis)
    imag = jnp.take(values, 1, axis=part_axis)
    return jnp.stack([jnp.stack([real, -imag]), jnp.stack([imag, real])])


def inner_products(first, second):
    return jnp.einsum("csn,ctn->st", first, second, precision=highest)


def combine_rows(matrix, vectors):
    return jnp.einsum("st,ctn->csn", matrix, vectors, precision=highest)


def matmul(left, right):
    return jnp.dot(left, right, precision=highest)


def lower_inverse(lower):
    identity = jnp.eye(lower.shape[0], dtype=lower.dtype)
    return lax.linalg.triangular_solve(lower, identity, left_side=True, lower=True)


def project(harmonics, vectors):

    def contract(left, right):
        return jnp.einsum("mn,sn->ms", left, right, precision=highest)

    real_out = contract(harmonics[0], vectors[0]) + contract(harmonics[1], vectors[1])
    imag_out = contract(harmonics[0], vectors[1]) - contract(harmonics[1], vectors[0])
    return jnp.stack([real_out, imag_out])


def body(incident, diagonal, near_blocks, left_factors, right_factors, flags, ranks, harmonics):
    blocks = left_factors.shape[1]
    slots = near_blocks.shape[1]
    width = near_blocks.shape[4]
    half_band = slots // 2
    elements = incident.shape[2]
    fields = incident.shape[1]
    clusters = lax.axis_size("row")
    row_index = lax.axis_index("row")
    column = lax.axis_index("col")
    ids = []

    def operator_terms(near_pieces, far_pieces):
        near_on = flags[0] == 1
        near_vector = jnp.where(near_on[:, None, None, None], near_pieces, 0).astype(jnp.bfloat16)
        near_lhs = complex_lhs(near_vector, 1).transpose(0, 3, 1, 2, 4)
        near_out = jnp.einsum(
            "xakf,kaef->xe",
            near_lhs.reshape(2 * fields, 2, slots, width),
            near_blocks[0],
            preferred_element_type=jnp.float32,
        )
        cluster = column * blocks + jnp.arange(blocks, dtype=jnp.int32)
        offset = (cluster - row_index + half_band) % clusters
        is_near = (offset < slots) & (flags[0, jnp.minimum(offset, slots - 1)] == 1)
        keep = (~is_near)[:, None] & (
            jnp.arange(right_factors.shape[3], dtype=jnp.int32)[None, :] < ranks[0][:, None]
        )
        products = jnp.einsum(
            "nxf,nbrf->nxbr", far_pieces, right_factors[0], preferred_element_type=jnp.float32
        )
        coeffs = jnp.stack(
            [
                products[:, :fields, 0] - products[:, fields:, 1],
                products[:, :fields, 1] + products[:, fields:, 0],
            ]
        )
        coeffs = jnp.where(keep[None, :, None, :], coeffs, 0.0).astype(jnp.bfloat16)
        far_lhs = complex_lhs(coeffs, 0).transpose(0, 3, 1, 2, 4)
        far_out = jnp.einsum(
            "xanr,nare->xe",
            far_lhs.reshape(2 * fields, 2, blocks, far_lhs.shape[-1]),
            left_factors[0],
            preferred_element_type=jnp.float32,
        )
        return near_out + far_out

    def apply_operator(vector, basis_one):
        rounded = vector.astype(jnp.bfloat16)
        near_pieces, far_pieces, cross, self_gram, proj = gather_pieces(
            rounded, basis_one, vector, harmonics, blocks, half_band, width, 16 + len(ids)
        )
        ids.append(None)
        total = operator_terms(near_pieces, far_pieces)
        summed = col_reduce(total, 32 + len(ids)).reshape(vector.shape)
        ids.append(None)
        return summed + diagonal[None, None, :] * vector, cross, self_gram, proj

    lower_first = jnp.linalg.cholesky(row_psum(ids, inner_products(incident, incident)))
    basis_one = combine_rows(lower_inverse(lower_first), incident)
    image, _, self_one, harmonics_one = apply_operator(basis_one, basis_one)
    coupling_one, harmonics_one, self_one = row_psum(
        ids, inner_products(image, basis_one), harmonics_one, self_one
    )
    rest = image - combine_rows(coupling_one, basis_one)
    gram_one = row_psum(ids, inner_products(rest, rest))
    lower_second = jnp.linalg.cholesky(gram_one)
    basis_two = combine_rows(lower_inverse(lower_second), rest)
    image, cross, self_two, harmonics_two = apply_operator(basis_two, basis_one)
    coupling_onetwo, coupling_two, image_gram, cross, self_two, harmonics_two = row_psum(
        ids,
        inner_products(image, basis_one),
        inner_products(image, basis_two),
        inner_products(image, image),
        cross,
        self_two,
        harmonics_two,
    )
    coupling = jnp.concatenate([coupling_onetwo, coupling_two], axis=1)
    basis_gram = jnp.concatenate(
        [
            jnp.concatenate([self_one, cross], axis=1),
            jnp.concatenate([cross.T, self_two], axis=1),
        ],
        axis=0,
    )
    gram_two = (
        image_gram
        - 2.0 * matmul(coupling, coupling.T)
        + matmul(coupling, matmul(basis_gram, coupling.T))
    )
    upper_left = matmul(coupling_one, coupling_one.T) + gram_one
    upper_right = matmul(coupling_one, coupling_onetwo.T) + matmul(lower_second, coupling_two.T)
    lower_right = (
        matmul(coupling_onetwo, coupling_onetwo.T) + matmul(coupling_two, coupling_two.T) + gram_two
    )
    normal = jnp.concatenate(
        [
            jnp.concatenate([upper_left, upper_right], axis=1),
            jnp.concatenate([upper_right.T, lower_right], axis=1),
        ],
        axis=0,
    )
    target = jnp.concatenate(
        [matmul(lower_first, coupling_one.T), matmul(lower_first, coupling_onetwo.T)], axis=1
    )
    factor_inverse = lower_inverse(jnp.linalg.cholesky(normal))
    weights = matmul(factor_inverse.T, matmul(factor_inverse, target.T)).T
    first_weights = weights[:, :fields]
    second_weights = weights[:, fields:]
    solution = combine_rows(first_weights, basis_one) + combine_rows(second_weights, basis_two)
    coefficients = jnp.einsum(
        "cmt,st->cms", harmonics_one, first_weights, precision=highest
    ) + jnp.einsum("cmt,st->cms", harmonics_two, second_weights, precision=highest)
    return (solution, coefficients)


def solution(mesh):
    in_specs = (
        P(None, None, "row"),
        P("row"),
        P("row", None, None, None, "col"),
        P("row", "col", None, None, None),
        P("row", "col", None, None, None),
        P("row", None),
        P("row", "col"),
        P(None, None, "row"),
    )
    out_specs = (P(None, None, "row"), P())
    return jax.shard_map(body, mesh=mesh, in_specs=in_specs, out_specs=out_specs, check_vma=False)
```

```python
from functools import partial

import jax
import jax.numpy as jnp
from jax import lax
from jax.experimental import pallas as pl
from jax.experimental.pallas import tpu as pltpu
from jax.sharding import PartitionSpec as P

highest = lax.Precision.HIGHEST
MESH = pl.DeviceIdType.MESH


def allreduce_kernel(inner, outer, x_ref, o_ref, buf, partial_buf,
                     first_send, first_recv, second_send, second_recv):
    me = lax.axis_index("row")
    col = lax.axis_index("col")
    high = me // inner
    low = me % inner
    barrier = pltpu.get_barrier_semaphore()

    def inner_peer(d):
        return (high * inner + lax.rem(low + d, inner), col)

    def outer_peer(d):
        return (lax.rem(high + d, outer) * inner + low, col)

    def first(d):
        return pltpu.make_async_remote_copy(
            src_ref=x_ref,
            dst_ref=buf.at[d],
            send_sem=first_send.at[d],
            recv_sem=first_recv.at[d],
            device_id=inner_peer(d),
            device_id_type=MESH,
        )

    def second(d):
        return pltpu.make_async_remote_copy(
            src_ref=partial_buf.at[0],
            dst_ref=partial_buf.at[d],
            send_sem=second_send.at[d],
            recv_sem=second_recv.at[d],
            device_id=outer_peer(d),
            device_id_type=MESH,
        )

    def greet_inner(d, carry):
        pl.semaphore_signal(barrier, inc=1, device_id=inner_peer(d), device_id_type=MESH)
        return carry

    def greet_outer(d, carry):
        pl.semaphore_signal(barrier, inc=1, device_id=outer_peer(d), device_id_type=MESH)
        return carry

    def start_first(d, carry):
        first(d).start()
        return carry

    def finish_first(d, carry):
        first(d).wait()
        return carry

    def start_second(d, carry):
        second(d).start()
        return carry

    def finish_second(d, carry):
        second(d).wait()
        return carry

    def add_inner(source, total):
        return total + buf[lax.rem(low + inner - source, inner)]

    def add_outer(source, total):
        return total + partial_buf[lax.rem(high + outer - source, outer)]

    lax.fori_loop(1, inner, greet_inner, 0)
    lax.fori_loop(1, outer, greet_outer, 0)
    pl.semaphore_wait(barrier, inner - 1 + outer - 1)
    lax.fori_loop(1, inner, start_first, 0)
    buf[0] = x_ref[...]
    lax.fori_loop(1, inner, finish_first, 0)
    partial_buf[0] = lax.fori_loop(1, inner, add_inner, buf[low])
    lax.fori_loop(1, outer, start_second, 0)
    lax.fori_loop(1, outer, finish_second, 0)
    o_ref[...] = lax.fori_loop(1, outer, add_outer, partial_buf[high])


def row_allreduce(packed, collective_id):
    n = lax.axis_size("row")
    inner = 8 if n % 8 == 0 else n
    outer = n // inner
    rows, lanes = packed.shape
    return pl.pallas_call(
        partial(allreduce_kernel, inner, outer),
        out_shape=jax.ShapeDtypeStruct((rows, lanes), jnp.float32),
        in_specs=[pl.BlockSpec(memory_space=pltpu.VMEM)],
        out_specs=pl.BlockSpec(memory_space=pltpu.VMEM),
        scratch_shapes=[
            pltpu.VMEM((inner, rows, lanes), jnp.float32),
            pltpu.VMEM((outer, rows, lanes), jnp.float32),
            pltpu.SemaphoreType.DMA((inner,)),
            pltpu.SemaphoreType.DMA((inner,)),
            pltpu.SemaphoreType.DMA((outer,)),
            pltpu.SemaphoreType.DMA((outer,)),
        ],
        compiler_params=pltpu.CompilerParams(collective_id=collective_id, has_side_effects=True),
    )(packed)


def gram(left, right):
    return lax.dot_general(
        left, right, (((1,), (1,)), ((), ())), precision=highest, preferred_element_type=jnp.float32
    )


def gather_kernel(rows, cols, blocks, half, v_ref, one_ref, cur_ref, harm_ref,
                  near_ref, far_ref, cross_ref, self_ref, proj_ref, slices, far_buf,
                  first_send, first_recv, second_send, second_recv, local_sems):
    me = lax.axis_index("row")
    col = lax.axis_index("col")
    width = slices.shape[-1]
    barrier = pltpu.get_barrier_semaphore()

    def row_peer(d):
        return (lax.rem(me + d, rows), col)

    def col_peer(e):
        return (me, lax.rem(col + e, cols))

    def window(c):
        return pl.ds(pl.multiple_of(c * width, width), width)

    own = v_ref.at[:, window(col)]

    def first(d):
        return pltpu.make_async_remote_copy(
            src_ref=own,
            dst_ref=slices.at[d],
            send_sem=first_send.at[d],
            recv_sem=first_recv.at[d],
            device_id=row_peer(d),
            device_id_type=MESH,
        )

    def second(t):
        e = 1 + t // blocks
        n = t % blocks
        target = lax.rem(col + e, cols)
        slot = lax.rem(me + rows - blocks * target - n, rows)
        return pltpu.make_async_remote_copy(
            src_ref=slices.at[slot],
            dst_ref=far_buf.at[n, :, window(col)],
            send_sem=second_send.at[t],
            recv_sem=second_recv.at[t],
            device_id=col_peer(e),
            device_id_type=MESH,
        )

    def greet_row(d, carry):
        pl.semaphore_signal(barrier, inc=1, device_id=row_peer(d), device_id_type=MESH)
        return carry

    def greet_col(e, carry):
        pl.semaphore_signal(barrier, inc=1, device_id=col_peer(e), device_id_type=MESH)
        return carry

    def start_first(d, carry):
        first(d).start()
        return carry

    def finish_second(t, carry):
        second(t).wait()
        return carry

    def arrived(slot):
        pltpu.make_async_remote_copy(
            src_ref=own,
            dst_ref=slices.at[slot],
            send_sem=first_send.at[slot],
            recv_sem=first_recv.at[slot],
            device_id=row_peer(slot),
            device_id_type=MESH,
        ).wait_recv()

    def forward(t, carry):
        target = lax.rem(col + 1 + t // blocks, cols)
        arrived(lax.rem(me + rows - blocks * target - t % blocks, rows))
        second(t).start()
        return carry

    def sent_first(d, carry):
        first(d).wait_send()
        return carry

    lax.fori_loop(1, rows, greet_row, 0)
    lax.fori_loop(1, cols, greet_col, 0)
    pl.semaphore_wait(barrier, rows - 1 + cols - 1)
    lax.fori_loop(1, rows, start_first, 0)
    pltpu.make_async_copy(own, slices.at[0], first_recv.at[0]).start()
    cross_ref[...] = gram(one_ref[0], cur_ref[0]) + gram(one_ref[1], cur_ref[1])
    self_ref[...] = gram(cur_ref[0], cur_ref[0]) + gram(cur_ref[1], cur_ref[1])
    proj_ref[0] = gram(harm_ref[0], cur_ref[0]) + gram(harm_ref[1], cur_ref[1])
    proj_ref[1] = gram(harm_ref[0], cur_ref[1]) - gram(harm_ref[1], cur_ref[0])
    lax.fori_loop(0, (cols - 1) * blocks, forward, 0)
    mine = []
    for n in range(blocks):
        slot = lax.rem(me + rows - blocks * col - n, rows)
        arrived(slot)
        copy = pltpu.make_async_copy(slices.at[slot], far_buf.at[n, :, window(col)], local_sems.at[n])
        copy.start()
        mine.append(copy)
    lax.fori_loop(1, rows, sent_first, 0)
    for k in range(2 * half):
        near_ref[k] = slices[(half - k) % rows]
    lax.fori_loop(0, (cols - 1) * blocks, finish_second, 0)
    for copy in mine:
        copy.wait()
    far_ref[...] = far_buf[...]


def gather_pieces(vector, basis_one, basis, harmonics, blocks, half, width, collective_id):
    rows = lax.axis_size("row")
    cols = lax.axis_size("col")
    parts, fields, elements = vector.shape
    flat = vector.reshape(parts * fields, elements)
    near, far, cross, self_gram, proj = pl.pallas_call(
        partial(gather_kernel, rows, cols, blocks, half),
        out_shape=(
            jax.ShapeDtypeStruct((2 * half, parts * fields, width), vector.dtype),
            jax.ShapeDtypeStruct((blocks, parts * fields, elements), vector.dtype),
            jax.ShapeDtypeStruct((fields, fields), jnp.float32),
            jax.ShapeDtypeStruct((fields, fields), jnp.float32),
            jax.ShapeDtypeStruct((2, harmonics.shape[1], fields), jnp.float32),
        ),
        in_specs=[pl.BlockSpec(memory_space=pltpu.VMEM)] * 4,
        out_specs=tuple(pl.BlockSpec(memory_space=pltpu.VMEM) for _ in range(5)),
        scratch_shapes=[
            pltpu.VMEM((rows, parts * fields, width), vector.dtype),
            pltpu.VMEM((blocks, parts * fields, elements), vector.dtype),
            pltpu.SemaphoreType.DMA((rows,)),
            pltpu.SemaphoreType.DMA((rows,)),
            pltpu.SemaphoreType.DMA(((cols - 1) * blocks,)),
            pltpu.SemaphoreType.DMA(((cols - 1) * blocks,)),
            pltpu.SemaphoreType.DMA((blocks + 1,)),
        ],
        compiler_params=pltpu.CompilerParams(collective_id=collective_id, has_side_effects=True),
    )(flat, basis_one, basis, harmonics)
    return (
        near.reshape(2 * half, parts, fields, width),
        far,
        cross,
        self_gram,
        proj,
    )


def reduce_kernel(cols, x_ref, o_ref, parts_buf, full, first_send, first_recv, second_send, second_recv):
    me = lax.axis_index("row")
    col = lax.axis_index("col")
    width = parts_buf.shape[-1]
    barrier = pltpu.get_barrier_semaphore()

    def col_peer(e):
        return (me, lax.rem(col + e, cols))

    def window(c):
        return pl.ds(pl.multiple_of(c * width, width), width)

    def first(e):
        return pltpu.make_async_remote_copy(
            src_ref=x_ref.at[:, window(lax.rem(col + e, cols))],
            dst_ref=parts_buf.at[e],
            send_sem=first_send.at[e],
            recv_sem=first_recv.at[e],
            device_id=col_peer(e),
            device_id_type=MESH,
        )

    def second(e):
        return pltpu.make_async_remote_copy(
            src_ref=full.at[:, window(col)],
            dst_ref=full.at[:, window(col)],
            send_sem=second_send.at[e],
            recv_sem=second_recv.at[e],
            device_id=col_peer(e),
            device_id_type=MESH,
        )

    def greet(e, carry):
        pl.semaphore_signal(barrier, inc=1, device_id=col_peer(e), device_id_type=MESH)
        return carry

    def start_first(e, carry):
        first(e).start()
        return carry

    def finish_first(e, carry):
        first(e).wait()
        return carry

    def start_second(e, carry):
        second(e).start()
        return carry

    def finish_second(e, carry):
        second(e).wait_send()
        pltpu.make_async_remote_copy(
            src_ref=full.at[:, window(col)],
            dst_ref=full.at[:, window(lax.rem(col + cols - e, cols))],
            send_sem=second_send.at[e],
            recv_sem=second_recv.at[e],
            device_id=col_peer(e),
            device_id_type=MESH,
        ).wait_recv()
        return carry

    def add(source, total):
        return total + parts_buf[lax.rem(col + cols - source, cols)]

    lax.fori_loop(1, cols, greet, 0)
    pl.semaphore_wait(barrier, cols - 1)
    lax.fori_loop(1, cols, start_first, 0)
    parts_buf[0] = x_ref[:, window(col)]
    lax.fori_loop(1, cols, finish_first, 0)
    full[:, window(col)] = lax.fori_loop(1, cols, add, parts_buf[col])
    lax.fori_loop(1, cols, start_second, 0)
    lax.fori_loop(1, cols, finish_second, 0)
    o_ref[...] = full[...]


def col_reduce(partial_sum, collective_id):
    cols = lax.axis_size("col")
    parts, fields, elements = partial_sum.shape
    width = elements // cols
    flat = partial_sum.reshape(parts * fields, elements)
    summed = pl.pallas_call(
        partial(reduce_kernel, cols),
        out_shape=jax.ShapeDtypeStruct(flat.shape, jnp.float32),
        in_specs=[pl.BlockSpec(memory_space=pltpu.VMEM)],
        out_specs=pl.BlockSpec(memory_space=pltpu.VMEM),
        scratch_shapes=[
            pltpu.VMEM((cols, parts * fields, width), jnp.float32),
            pltpu.VMEM((parts * fields, elements), jnp.float32),
            pltpu.SemaphoreType.DMA((cols,)),
            pltpu.SemaphoreType.DMA((cols,)),
            pltpu.SemaphoreType.DMA((cols,)),
            pltpu.SemaphoreType.DMA((cols,)),
        ],
        compiler_params=pltpu.CompilerParams(collective_id=collective_id, has_side_effects=True),
    )(flat)
    return summed.reshape(partial_sum.shape)


def row_psum(ids, *arrays):
    flat = [a.reshape(-1) for a in arrays]
    sizes = [f.shape[0] for f in flat]
    total = sum(sizes)
    padded = -(-total // 1024) * 1024
    packed = jnp.concatenate(flat + [jnp.zeros((padded - total,), jnp.float32)]).reshape(-1, 128)
    summed = row_allreduce(packed, len(ids)).reshape(-1)
    ids.append(None)
    outs = []
    start = 0
    for a, size in zip(arrays, sizes):
        outs.append(summed[start : start + size].reshape(a.shape))
        start += size
    return outs[0] if len(outs) == 1 else tuple(outs)


def complex_lhs(values, part_axis):
    real = jnp.take(values, 0, axis=part_axis)
    imag = jnp.take(values, 1, axis=part_axis)
    return jnp.stack([jnp.stack([real, -imag]), jnp.stack([imag, real])])


def inner_products(first, second):
    return jnp.einsum("csn,ctn->st", first, second, precision=highest)


def combine_rows(matrix, vectors):
    return jnp.einsum("st,ctn->csn", matrix, vectors, precision=highest)


def matmul(left, right):
    return jnp.dot(left, right, precision=highest)


def lower_inverse(lower):
    identity = jnp.eye(lower.shape[0], dtype=lower.dtype)
    return lax.linalg.triangular_solve(lower, identity, left_side=True, lower=True)


def project(harmonics, vectors):

    def contract(left, right):
        return jnp.einsum("mn,sn->ms", left, right, precision=highest)

    real_out = contract(harmonics[0], vectors[0]) + contract(harmonics[1], vectors[1])
    imag_out = contract(harmonics[0], vectors[1]) - contract(harmonics[1], vectors[0])
    return jnp.stack([real_out, imag_out])


def body(incident, diagonal, near_blocks, left_factors, right_factors, flags, ranks, harmonics):
    blocks = left_factors.shape[1]
    slots = near_blocks.shape[1]
    width = near_blocks.shape[4]
    half_band = slots // 2
    elements = incident.shape[2]
    fields = incident.shape[1]
    clusters = lax.axis_size("row")
    row_index = lax.axis_index("row")
    column = lax.axis_index("col")
    ids = []

    def operator_terms(near_pieces, far_pieces):
        near_on = flags[0] == 1
        near_vector = jnp.where(near_on[:, None, None, None], near_pieces, 0).astype(jnp.bfloat16)
        near_out = jnp.einsum(
            "caksf,kaef->cse",
            complex_lhs(near_vector, 1),
            near_blocks[0],
            preferred_element_type=jnp.float32,
        )
        cluster = column * blocks + jnp.arange(blocks, dtype=jnp.int32)
        offset = (cluster - row_index + half_band) % clusters
        is_near = (offset < slots) & (flags[0, jnp.minimum(offset, slots - 1)] == 1)
        keep = (~is_near)[:, None] & (
            jnp.arange(right_factors.shape[3], dtype=jnp.int32)[None, :] < ranks[0][:, None]
        )
        products = jnp.einsum(
            "nxf,nbrf->nxbr", far_pieces, right_factors[0], preferred_element_type=jnp.float32
        )
        coeffs = jnp.stack(
            [
                products[:, :fields, 0] - products[:, fields:, 1],
                products[:, :fields, 1] + products[:, fields:, 0],
            ]
        )
        coeffs = jnp.where(keep[None, :, None, :], coeffs, 0.0).astype(jnp.bfloat16)
        far_out = jnp.einsum(
            "cansr,nare->cse",
            complex_lhs(coeffs, 0),
            left_factors[0],
            preferred_element_type=jnp.float32,
        )
        return near_out + far_out

    def apply_operator(vector, basis_one):
        rounded = vector.astype(jnp.bfloat16)
        near_pieces, far_pieces, cross, self_gram, proj = gather_pieces(
            rounded, basis_one, vector, harmonics, blocks, half_band, width, 16 + len(ids)
        )
        ids.append(None)
        total = operator_terms(near_pieces, far_pieces)
        summed = col_reduce(total, 32 + len(ids))
        ids.append(None)
        return summed + diagonal[None, None, :] * vector, cross, self_gram, proj

    lower_first = jnp.linalg.cholesky(row_psum(ids, inner_products(incident, incident)))
    basis_one = combine_rows(lower_inverse(lower_first), incident)
    image, _, self_one, harmonics_one = apply_operator(basis_one, basis_one)
    coupling_one, harmonics_one, self_one = row_psum(
        ids, inner_products(image, basis_one), harmonics_one, self_one
    )
    rest = image - combine_rows(coupling_one, basis_one)
    gram_one = row_psum(ids, inner_products(rest, rest))
    lower_second = jnp.linalg.cholesky(gram_one)
    basis_two = combine_rows(lower_inverse(lower_second), rest)
    image, cross, self_two, harmonics_two = apply_operator(basis_two, basis_one)
    coupling_onetwo, coupling_two, image_gram, cross, self_two, harmonics_two = row_psum(
        ids,
        inner_products(image, basis_one),
        inner_products(image, basis_two),
        inner_products(image, image),
        cross,
        self_two,
        harmonics_two,
    )
    coupling = jnp.concatenate([coupling_onetwo, coupling_two], axis=1)
    basis_gram = jnp.concatenate(
        [
            jnp.concatenate([self_one, cross], axis=1),
            jnp.concatenate([cross.T, self_two], axis=1),
        ],
        axis=0,
    )
    gram_two = (
        image_gram
        - 2.0 * matmul(coupling, coupling.T)
        + matmul(coupling, matmul(basis_gram, coupling.T))
    )
    upper_left = matmul(coupling_one, coupling_one.T) + gram_one
    upper_right = matmul(coupling_one, coupling_onetwo.T) + matmul(lower_second, coupling_two.T)
    lower_right = (
        matmul(coupling_onetwo, coupling_onetwo.T) + matmul(coupling_two, coupling_two.T) + gram_two
    )
    normal = jnp.concatenate(
        [
            jnp.concatenate([upper_left, upper_right], axis=1),
            jnp.concatenate([upper_right.T, lower_right], axis=1),
        ],
        axis=0,
    )
    target = jnp.concatenate(
        [matmul(lower_first, coupling_one.T), matmul(lower_first, coupling_onetwo.T)], axis=1
    )
    factor_inverse = lower_inverse(jnp.linalg.cholesky(normal))
    weights = matmul(factor_inverse.T, matmul(factor_inverse, target.T)).T
    first_weights = weights[:, :fields]
    second_weights = weights[:, fields:]
    solution = combine_rows(first_weights, basis_one) + combine_rows(second_weights, basis_two)
    coefficients = jnp.einsum(
        "cmt,st->cms", harmonics_one, first_weights, precision=highest
    ) + jnp.einsum("cmt,st->cms", harmonics_two, second_weights, precision=highest)
    return (solution, coefficients)


def solution(mesh):
    in_specs = (
        P(None, None, "row"),
        P("row"),
        P("row", None, None, None, "col"),
        P("row", "col", None, None, None),
        P("row", "col", None, None, None),
        P("row", None),
        P("row", "col"),
        P(None, None, "row"),
    )
    out_specs = (P(None, None, "row"), P())
    return jax.shard_map(body, mesh=mesh, in_specs=in_specs, out_specs=out_specs, check_vma=False)
```

```python
from functools import partial

import jax
import jax.numpy as jnp
from jax import lax
from jax.experimental import pallas as pl
from jax.experimental.pallas import tpu as pltpu
from jax.sharding import PartitionSpec as P

highest = lax.Precision.HIGHEST
MESH = pl.DeviceIdType.MESH


def allreduce_kernel(inner, outer, x_ref, o_ref, buf, partial_buf,
                     first_send, first_recv, second_send, second_recv):
    me = lax.axis_index("row")
    col = lax.axis_index("col")
    high = me // inner
    low = me % inner
    barrier = pltpu.get_barrier_semaphore()

    def inner_peer(d):
        return (high * inner + lax.rem(low + d, inner), col)

    def outer_peer(d):
        return (lax.rem(high + d, outer) * inner + low, col)

    def first(d):
        return pltpu.make_async_remote_copy(
            src_ref=x_ref,
            dst_ref=buf.at[d],
            send_sem=first_send.at[d],
            recv_sem=first_recv.at[d],
            device_id=inner_peer(d),
            device_id_type=MESH,
        )

    def second(d):
        return pltpu.make_async_remote_copy(
            src_ref=partial_buf.at[0],
            dst_ref=partial_buf.at[d],
            send_sem=second_send.at[d],
            recv_sem=second_recv.at[d],
            device_id=outer_peer(d),
            device_id_type=MESH,
        )

    def greet_inner(d, carry):
        pl.semaphore_signal(barrier, inc=1, device_id=inner_peer(d), device_id_type=MESH)
        return carry

    def greet_outer(d, carry):
        pl.semaphore_signal(barrier, inc=1, device_id=outer_peer(d), device_id_type=MESH)
        return carry

    def start_first(d, carry):
        first(d).start()
        return carry

    def finish_first(d, carry):
        first(d).wait()
        return carry

    def start_second(d, carry):
        second(d).start()
        return carry

    def finish_second(d, carry):
        second(d).wait()
        return carry

    def add_inner(source, total):
        return total + buf[lax.rem(low + inner - source, inner)]

    def add_outer(source, total):
        return total + partial_buf[lax.rem(high + outer - source, outer)]

    lax.fori_loop(1, inner, greet_inner, 0)
    lax.fori_loop(1, outer, greet_outer, 0)
    pl.semaphore_wait(barrier, inner - 1 + outer - 1)
    lax.fori_loop(1, inner, start_first, 0)
    buf[0] = x_ref[...]
    lax.fori_loop(1, inner, finish_first, 0)
    partial_buf[0] = lax.fori_loop(1, inner, add_inner, buf[low])
    lax.fori_loop(1, outer, start_second, 0)
    lax.fori_loop(1, outer, finish_second, 0)
    o_ref[...] = lax.fori_loop(1, outer, add_outer, partial_buf[high])


def row_allreduce(packed, collective_id):
    n = lax.axis_size("row")
    inner = 8 if n % 8 == 0 else n
    outer = n // inner
    rows, lanes = packed.shape
    return pl.pallas_call(
        partial(allreduce_kernel, inner, outer),
        out_shape=jax.ShapeDtypeStruct((rows, lanes), jnp.float32),
        in_specs=[pl.BlockSpec(memory_space=pltpu.VMEM)],
        out_specs=pl.BlockSpec(memory_space=pltpu.VMEM),
        scratch_shapes=[
            pltpu.VMEM((inner, rows, lanes), jnp.float32),
            pltpu.VMEM((outer, rows, lanes), jnp.float32),
            pltpu.SemaphoreType.DMA((inner,)),
            pltpu.SemaphoreType.DMA((inner,)),
            pltpu.SemaphoreType.DMA((outer,)),
            pltpu.SemaphoreType.DMA((outer,)),
        ],
        compiler_params=pltpu.CompilerParams(collective_id=collective_id, has_side_effects=True),
    )(packed)


def gram(left, right):
    return lax.dot_general(
        left, right, (((1,), (1,)), ((), ())), precision=highest, preferred_element_type=jnp.float32
    )


def gather_kernel(rows, cols, blocks, half, v_ref, one_ref, cur_ref, harm_ref,
                  near_ref, far_ref, cross_ref, self_ref, proj_ref, slices, far_buf,
                  first_send, first_recv, second_send, second_recv, local_sems):
    me = lax.axis_index("row")
    col = lax.axis_index("col")
    width = slices.shape[-1]
    barrier = pltpu.get_barrier_semaphore()

    def row_peer(d):
        return (lax.rem(me + d, rows), col)

    def col_peer(e):
        return (me, lax.rem(col + e, cols))

    def window(c):
        return pl.ds(pl.multiple_of(c * width, width), width)

    own = v_ref.at[:, window(col)]

    def first(d):
        return pltpu.make_async_remote_copy(
            src_ref=own,
            dst_ref=slices.at[d],
            send_sem=first_send.at[d],
            recv_sem=first_recv.at[d],
            device_id=row_peer(d),
            device_id_type=MESH,
        )

    def second(t):
        e = 1 + t // blocks
        n = t % blocks
        target = lax.rem(col + e, cols)
        slot = lax.rem(me + rows - blocks * target - n, rows)
        return pltpu.make_async_remote_copy(
            src_ref=slices.at[slot],
            dst_ref=far_buf.at[n, :, window(col)],
            send_sem=second_send.at[t],
            recv_sem=second_recv.at[t],
            device_id=col_peer(e),
            device_id_type=MESH,
        )

    def greet_row(d, carry):
        pl.semaphore_signal(barrier, inc=1, device_id=row_peer(d), device_id_type=MESH)
        return carry

    def greet_col(e, carry):
        pl.semaphore_signal(barrier, inc=1, device_id=col_peer(e), device_id_type=MESH)
        return carry

    def start_first(d, carry):
        first(d).start()
        return carry

    def finish_second(t, carry):
        second(t).wait()
        return carry

    def arrived(slot):
        pltpu.make_async_remote_copy(
            src_ref=own,
            dst_ref=slices.at[slot],
            send_sem=first_send.at[slot],
            recv_sem=first_recv.at[slot],
            device_id=row_peer(slot),
            device_id_type=MESH,
        ).wait_recv()

    def forward(t, carry):
        target = lax.rem(col + 1 + t // blocks, cols)
        arrived(lax.rem(me + rows - blocks * target - t % blocks, rows))
        second(t).start()
        return carry

    def sent_first(d, carry):
        first(d).wait_send()
        return carry

    lax.fori_loop(1, rows, greet_row, 0)
    lax.fori_loop(1, cols, greet_col, 0)
    pl.semaphore_wait(barrier, rows - 1 + cols - 1)
    lax.fori_loop(1, rows, start_first, 0)
    pltpu.make_async_copy(own, slices.at[0], first_recv.at[0]).start()
    cross_ref[...] = gram(one_ref[0], cur_ref[0]) + gram(one_ref[1], cur_ref[1])
    self_ref[...] = gram(cur_ref[0], cur_ref[0]) + gram(cur_ref[1], cur_ref[1])
    proj_ref[0] = gram(harm_ref[0], cur_ref[0]) + gram(harm_ref[1], cur_ref[1])
    proj_ref[1] = gram(harm_ref[0], cur_ref[1]) - gram(harm_ref[1], cur_ref[0])
    lax.fori_loop(0, (cols - 1) * blocks, forward, 0)
    mine = []
    for n in range(blocks):
        slot = lax.rem(me + rows - blocks * col - n, rows)
        arrived(slot)
        copy = pltpu.make_async_copy(slices.at[slot], far_buf.at[n, :, window(col)], local_sems.at[n])
        copy.start()
        mine.append(copy)
    lax.fori_loop(1, rows, sent_first, 0)
    for k in range(2 * half):
        near_ref[k] = slices[(half - k) % rows]
    lax.fori_loop(0, (cols - 1) * blocks, finish_second, 0)
    for copy in mine:
        copy.wait()
    far_ref[...] = far_buf[...]


def gather_pieces(vector, basis_one, basis, harmonics, blocks, half, width, collective_id):
    rows = lax.axis_size("row")
    cols = lax.axis_size("col")
    parts, fields, elements = vector.shape
    flat = vector.reshape(parts * fields, elements)
    near, far, cross, self_gram, proj = pl.pallas_call(
        partial(gather_kernel, rows, cols, blocks, half),
        out_shape=(
            jax.ShapeDtypeStruct((2 * half, parts * fields, width), vector.dtype),
            jax.ShapeDtypeStruct((blocks, parts * fields, elements), vector.dtype),
            jax.ShapeDtypeStruct((fields, fields), jnp.float32),
            jax.ShapeDtypeStruct((fields, fields), jnp.float32),
            jax.ShapeDtypeStruct((2, harmonics.shape[1], fields), jnp.float32),
        ),
        in_specs=[pl.BlockSpec(memory_space=pltpu.VMEM)] * 4,
        out_specs=tuple(pl.BlockSpec(memory_space=pltpu.VMEM) for _ in range(5)),
        scratch_shapes=[
            pltpu.VMEM((rows, parts * fields, width), vector.dtype),
            pltpu.VMEM((blocks, parts * fields, elements), vector.dtype),
            pltpu.SemaphoreType.DMA((rows,)),
            pltpu.SemaphoreType.DMA((rows,)),
            pltpu.SemaphoreType.DMA(((cols - 1) * blocks,)),
            pltpu.SemaphoreType.DMA(((cols - 1) * blocks,)),
            pltpu.SemaphoreType.DMA((blocks + 1,)),
        ],
        compiler_params=pltpu.CompilerParams(collective_id=collective_id, has_side_effects=True),
    )(flat, basis_one, basis, harmonics)
    return (
        near.reshape(2 * half, parts, fields, width),
        far,
        cross,
        self_gram,
        proj,
    )


def reduce_kernel(cols, x_ref, o_ref, parts_buf, full, first_send, first_recv, second_send, second_recv):
    me = lax.axis_index("row")
    col = lax.axis_index("col")
    width = parts_buf.shape[-1]
    barrier = pltpu.get_barrier_semaphore()

    def col_peer(e):
        return (me, lax.rem(col + e, cols))

    def window(c):
        return pl.ds(pl.multiple_of(c * width, width), width)

    def first(e):
        return pltpu.make_async_remote_copy(
            src_ref=x_ref.at[:, window(lax.rem(col + e, cols))],
            dst_ref=parts_buf.at[e],
            send_sem=first_send.at[e],
            recv_sem=first_recv.at[e],
            device_id=col_peer(e),
            device_id_type=MESH,
        )

    def second(e):
        return pltpu.make_async_remote_copy(
            src_ref=full.at[:, window(col)],
            dst_ref=full.at[:, window(col)],
            send_sem=second_send.at[e],
            recv_sem=second_recv.at[e],
            device_id=col_peer(e),
            device_id_type=MESH,
        )

    def greet(e, carry):
        pl.semaphore_signal(barrier, inc=1, device_id=col_peer(e), device_id_type=MESH)
        return carry

    def start_first(e, carry):
        first(e).start()
        return carry

    def finish_first(e, carry):
        first(e).wait()
        return carry

    def start_second(e, carry):
        second(e).start()
        return carry

    def finish_second(e, carry):
        second(e).wait_send()
        pltpu.make_async_remote_copy(
            src_ref=full.at[:, window(col)],
            dst_ref=full.at[:, window(lax.rem(col + cols - e, cols))],
            send_sem=second_send.at[e],
            recv_sem=second_recv.at[e],
            device_id=col_peer(e),
            device_id_type=MESH,
        ).wait_recv()
        return carry

    def add(source, total):
        return total + parts_buf[lax.rem(col + cols - source, cols)]

    lax.fori_loop(1, cols, greet, 0)
    pl.semaphore_wait(barrier, cols - 1)
    lax.fori_loop(1, cols, start_first, 0)
    parts_buf[0] = x_ref[:, window(col)]
    lax.fori_loop(1, cols, finish_first, 0)
    full[:, window(col)] = lax.fori_loop(1, cols, add, parts_buf[col])
    lax.fori_loop(1, cols, start_second, 0)
    lax.fori_loop(1, cols, finish_second, 0)
    o_ref[...] = full[...]


def col_reduce(partial_sum, collective_id):
    cols = lax.axis_size("col")
    parts, fields, elements = partial_sum.shape
    width = elements // cols
    flat = partial_sum.reshape(parts * fields, elements)
    summed = pl.pallas_call(
        partial(reduce_kernel, cols),
        out_shape=jax.ShapeDtypeStruct(flat.shape, jnp.float32),
        in_specs=[pl.BlockSpec(memory_space=pltpu.VMEM)],
        out_specs=pl.BlockSpec(memory_space=pltpu.VMEM),
        scratch_shapes=[
            pltpu.VMEM((cols, parts * fields, width), jnp.float32),
            pltpu.VMEM((parts * fields, elements), jnp.float32),
            pltpu.SemaphoreType.DMA((cols,)),
            pltpu.SemaphoreType.DMA((cols,)),
            pltpu.SemaphoreType.DMA((cols,)),
            pltpu.SemaphoreType.DMA((cols,)),
        ],
        compiler_params=pltpu.CompilerParams(collective_id=collective_id, has_side_effects=True),
    )(flat)
    return summed.reshape(partial_sum.shape)


def row_psum(ids, *arrays):
    flat = [a.reshape(-1) for a in arrays]
    sizes = [f.shape[0] for f in flat]
    total = sum(sizes)
    padded = -(-total // 1024) * 1024
    packed = jnp.concatenate(flat + [jnp.zeros((padded - total,), jnp.float32)]).reshape(-1, 128)
    summed = row_allreduce(packed, len(ids)).reshape(-1)
    ids.append(None)
    outs = []
    start = 0
    for a, size in zip(arrays, sizes):
        outs.append(summed[start : start + size].reshape(a.shape))
        start += size
    return outs[0] if len(outs) == 1 else tuple(outs)


def complex_lhs(values, part_axis):
    real = jnp.take(values, 0, axis=part_axis)
    imag = jnp.take(values, 1, axis=part_axis)
    return jnp.stack([jnp.stack([real, -imag]), jnp.stack([imag, real])])


def inner_products(first, second):
    return jnp.einsum("csn,ctn->st", first, second, precision=highest)


def combine_rows(matrix, vectors):
    return jnp.einsum("st,ctn->csn", matrix, vectors, precision=highest)


def matmul(left, right):
    return jnp.dot(left, right, precision=highest)


def lower_solve(lower, vectors):
    factor = jnp.broadcast_to(lower, (vectors.shape[0],) + lower.shape)
    return lax.linalg.triangular_solve(factor, vectors, left_side=True, lower=True)


def lower_inverse(lower):
    identity = jnp.eye(lower.shape[0], dtype=lower.dtype)
    return lax.linalg.triangular_solve(lower, identity, left_side=True, lower=True)


def project(harmonics, vectors):

    def contract(left, right):
        return jnp.einsum("mn,sn->ms", left, right, precision=highest)

    real_out = contract(harmonics[0], vectors[0]) + contract(harmonics[1], vectors[1])
    imag_out = contract(harmonics[0], vectors[1]) - contract(harmonics[1], vectors[0])
    return jnp.stack([real_out, imag_out])


def body(incident, diagonal, near_blocks, left_factors, right_factors, flags, ranks, harmonics):
    blocks = left_factors.shape[1]
    slots = near_blocks.shape[1]
    width = near_blocks.shape[4]
    half_band = slots // 2
    elements = incident.shape[2]
    fields = incident.shape[1]
    clusters = lax.axis_size("row")
    row_index = lax.axis_index("row")
    column = lax.axis_index("col")
    ids = []

    def operator_terms(near_pieces, far_pieces):
        near_on = flags[0] == 1
        near_vector = jnp.where(near_on[:, None, None, None], near_pieces, 0).astype(jnp.bfloat16)
        near_out = jnp.einsum(
            "caksf,kaef->cse",
            complex_lhs(near_vector, 1),
            near_blocks[0],
            preferred_element_type=jnp.float32,
        )
        cluster = column * blocks + jnp.arange(blocks, dtype=jnp.int32)
        offset = (cluster - row_index + half_band) % clusters
        is_near = (offset < slots) & (flags[0, jnp.minimum(offset, slots - 1)] == 1)
        keep = (~is_near)[:, None] & (
            jnp.arange(right_factors.shape[3], dtype=jnp.int32)[None, :] < ranks[0][:, None]
        )
        products = jnp.einsum(
            "nxf,nbrf->nxbr", far_pieces, right_factors[0], preferred_element_type=jnp.float32
        )
        coeffs = jnp.stack(
            [
                products[:, :fields, 0] - products[:, fields:, 1],
                products[:, :fields, 1] + products[:, fields:, 0],
            ]
        )
        coeffs = jnp.where(keep[None, :, None, :], coeffs, 0.0).astype(jnp.bfloat16)
        far_out = jnp.einsum(
            "cansr,nare->cse",
            complex_lhs(coeffs, 0),
            left_factors[0],
            preferred_element_type=jnp.float32,
        )
        return near_out + far_out

    def apply_operator(vector, basis_one):
        rounded = vector.astype(jnp.bfloat16)
        near_pieces, far_pieces, cross, self_gram, proj = gather_pieces(
            rounded, basis_one, vector, harmonics, blocks, half_band, width, 16 + len(ids)
        )
        ids.append(None)
        total = operator_terms(near_pieces, far_pieces)
        summed = col_reduce(total, 32 + len(ids))
        ids.append(None)
        return summed + diagonal[None, None, :] * vector, cross, self_gram, proj

    lower_first = jnp.linalg.cholesky(row_psum(ids, inner_products(incident, incident)))
    basis_one = lower_solve(lower_first, incident)
    image, _, self_one, harmonics_one = apply_operator(basis_one, basis_one)
    coupling_one, harmonics_one, self_one = row_psum(
        ids, inner_products(image, basis_one), harmonics_one, self_one
    )
    rest = image - combine_rows(coupling_one, basis_one)
    gram_one = row_psum(ids, inner_products(rest, rest))
    lower_second = jnp.linalg.cholesky(gram_one)
    basis_two = lower_solve(lower_second, rest)
    image, cross, self_two, harmonics_two = apply_operator(basis_two, basis_one)
    coupling_onetwo, coupling_two, image_gram, cross, self_two, harmonics_two = row_psum(
        ids,
        inner_products(image, basis_one),
        inner_products(image, basis_two),
        inner_products(image, image),
        cross,
        self_two,
        harmonics_two,
    )
    coupling = jnp.concatenate([coupling_onetwo, coupling_two], axis=1)
    basis_gram = jnp.concatenate(
        [
            jnp.concatenate([self_one, cross], axis=1),
            jnp.concatenate([cross.T, self_two], axis=1),
        ],
        axis=0,
    )
    gram_two = (
        image_gram
        - 2.0 * matmul(coupling, coupling.T)
        + matmul(coupling, matmul(basis_gram, coupling.T))
    )
    upper_left = matmul(coupling_one, coupling_one.T) + gram_one
    upper_right = matmul(coupling_one, coupling_onetwo.T) + matmul(lower_second, coupling_two.T)
    lower_right = (
        matmul(coupling_onetwo, coupling_onetwo.T) + matmul(coupling_two, coupling_two.T) + gram_two
    )
    normal = jnp.concatenate(
        [
            jnp.concatenate([upper_left, upper_right], axis=1),
            jnp.concatenate([upper_right.T, lower_right], axis=1),
        ],
        axis=0,
    )
    target = jnp.concatenate(
        [matmul(lower_first, coupling_one.T), matmul(lower_first, coupling_onetwo.T)], axis=1
    )
    factor_inverse = lower_inverse(jnp.linalg.cholesky(normal))
    weights = matmul(factor_inverse.T, matmul(factor_inverse, target.T)).T
    first_weights = weights[:, :fields]
    second_weights = weights[:, fields:]
    solution = combine_rows(first_weights, basis_one) + combine_rows(second_weights, basis_two)
    coefficients = jnp.einsum(
        "cmt,st->cms", harmonics_one, first_weights, precision=highest
    ) + jnp.einsum("cmt,st->cms", harmonics_two, second_weights, precision=highest)
    return (solution, coefficients)


def solution(mesh):
    in_specs = (
        P(None, None, "row"),
        P("row"),
        P("row", None, None, None, "col"),
        P("row", "col", None, None, None),
        P("row", "col", None, None, None),
        P("row", None),
        P("row", "col"),
        P(None, None, "row"),
    )
    out_specs = (P(None, None, "row"), P())
    return jax.shard_map(body, mesh=mesh, in_specs=in_specs, out_specs=out_specs, check_vma=False)
```

```python
from functools import partial

import jax
import jax.numpy as jnp
from jax import lax
from jax.experimental import pallas as pl
from jax.experimental.pallas import tpu as pltpu
from jax.sharding import PartitionSpec as P

highest = lax.Precision.HIGHEST
MESH = pl.DeviceIdType.MESH


def allreduce_kernel(inner, outer, x_ref, o_ref, buf, partial_buf,
                     first_send, first_recv, second_send, second_recv):
    me = lax.axis_index("row")
    col = lax.axis_index("col")
    high = me // inner
    low = me % inner
    barrier = pltpu.get_barrier_semaphore()

    def inner_peer(d):
        return (high * inner + lax.rem(low + d, inner), col)

    def outer_peer(d):
        return (lax.rem(high + d, outer) * inner + low, col)

    def first(d):
        return pltpu.make_async_remote_copy(
            src_ref=x_ref,
            dst_ref=buf.at[d],
            send_sem=first_send.at[d],
            recv_sem=first_recv.at[d],
            device_id=inner_peer(d),
            device_id_type=MESH,
        )

    def second(d):
        return pltpu.make_async_remote_copy(
            src_ref=partial_buf.at[0],
            dst_ref=partial_buf.at[d],
            send_sem=second_send.at[d],
            recv_sem=second_recv.at[d],
            device_id=outer_peer(d),
            device_id_type=MESH,
        )

    def greet_inner(d, carry):
        pl.semaphore_signal(barrier, inc=1, device_id=inner_peer(d), device_id_type=MESH)
        return carry

    def greet_outer(d, carry):
        pl.semaphore_signal(barrier, inc=1, device_id=outer_peer(d), device_id_type=MESH)
        return carry

    def start_first(d, carry):
        first(d).start()
        return carry

    def finish_first(d, carry):
        first(d).wait()
        return carry

    def start_second(d, carry):
        second(d).start()
        return carry

    def finish_second(d, carry):
        second(d).wait()
        return carry

    def add_inner(source, total):
        return total + buf[lax.rem(low + inner - source, inner)]

    def add_outer(source, total):
        return total + partial_buf[lax.rem(high + outer - source, outer)]

    lax.fori_loop(1, inner, greet_inner, 0)
    lax.fori_loop(1, outer, greet_outer, 0)
    pl.semaphore_wait(barrier, inner - 1 + outer - 1)
    lax.fori_loop(1, inner, start_first, 0)
    buf[0] = x_ref[...]
    lax.fori_loop(1, inner, finish_first, 0)
    partial_buf[0] = lax.fori_loop(1, inner, add_inner, buf[low])
    lax.fori_loop(1, outer, start_second, 0)
    lax.fori_loop(1, outer, finish_second, 0)
    o_ref[...] = lax.fori_loop(1, outer, add_outer, partial_buf[high])


def row_allreduce(packed, collective_id):
    n = lax.axis_size("row")
    inner = 8 if n % 8 == 0 else n
    outer = n // inner
    rows, lanes = packed.shape
    return pl.pallas_call(
        partial(allreduce_kernel, inner, outer),
        out_shape=jax.ShapeDtypeStruct((rows, lanes), jnp.float32),
        in_specs=[pl.BlockSpec(memory_space=pltpu.VMEM)],
        out_specs=pl.BlockSpec(memory_space=pltpu.VMEM),
        scratch_shapes=[
            pltpu.VMEM((inner, rows, lanes), jnp.float32),
            pltpu.VMEM((outer, rows, lanes), jnp.float32),
            pltpu.SemaphoreType.DMA((inner,)),
            pltpu.SemaphoreType.DMA((inner,)),
            pltpu.SemaphoreType.DMA((outer,)),
            pltpu.SemaphoreType.DMA((outer,)),
        ],
        compiler_params=pltpu.CompilerParams(collective_id=collective_id, has_side_effects=True),
    )(packed)


def gram(left, right):
    return lax.dot_general(
        left, right, (((1,), (1,)), ((), ())), precision=highest, preferred_element_type=jnp.float32
    )


def gather_kernel(rows, cols, blocks, half, v_ref, one_ref, cur_ref, harm_ref,
                  near_ref, far_ref, cross_ref, self_ref, proj_ref, slices, far_buf,
                  first_send, first_recv, second_send, second_recv, local_sems):
    me = lax.axis_index("row")
    col = lax.axis_index("col")
    width = slices.shape[-1]
    barrier = pltpu.get_barrier_semaphore()

    def row_peer(d):
        return (lax.rem(me + d, rows), col)

    def col_peer(e):
        return (me, lax.rem(col + e, cols))

    def window(c):
        return pl.ds(pl.multiple_of(c * width, width), width)

    own = v_ref.at[:, window(col)]

    def first(d):
        return pltpu.make_async_remote_copy(
            src_ref=own,
            dst_ref=slices.at[d],
            send_sem=first_send.at[d],
            recv_sem=first_recv.at[d],
            device_id=row_peer(d),
            device_id_type=MESH,
        )

    def second(t):
        e = 1 + t // blocks
        n = t % blocks
        target = lax.rem(col + e, cols)
        slot = lax.rem(me + rows - blocks * target - n, rows)
        return pltpu.make_async_remote_copy(
            src_ref=slices.at[slot],
            dst_ref=far_buf.at[n, :, window(col)],
            send_sem=second_send.at[t],
            recv_sem=second_recv.at[t],
            device_id=col_peer(e),
            device_id_type=MESH,
        )

    def greet_row(d, carry):
        pl.semaphore_signal(barrier, inc=1, device_id=row_peer(d), device_id_type=MESH)
        return carry

    def greet_col(e, carry):
        pl.semaphore_signal(barrier, inc=1, device_id=col_peer(e), device_id_type=MESH)
        return carry

    def start_first(d, carry):
        first(d).start()
        return carry

    def finish_second(t, carry):
        second(t).wait()
        return carry

    def arrived(slot):
        pltpu.make_async_remote_copy(
            src_ref=own,
            dst_ref=slices.at[slot],
            send_sem=first_send.at[slot],
            recv_sem=first_recv.at[slot],
            device_id=row_peer(slot),
            device_id_type=MESH,
        ).wait_recv()

    def forward(t, carry):
        target = lax.rem(col + 1 + t // blocks, cols)
        arrived(lax.rem(me + rows - blocks * target - t % blocks, rows))
        second(t).start()
        return carry

    def sent_first(d, carry):
        first(d).wait_send()
        return carry

    lax.fori_loop(1, rows, greet_row, 0)
    lax.fori_loop(1, cols, greet_col, 0)
    pl.semaphore_wait(barrier, rows - 1 + cols - 1)
    lax.fori_loop(1, rows, start_first, 0)
    pltpu.make_async_copy(own, slices.at[0], first_recv.at[0]).start()
    cross_ref[...] = gram(one_ref[0], cur_ref[0]) + gram(one_ref[1], cur_ref[1])
    self_ref[...] = gram(cur_ref[0], cur_ref[0]) + gram(cur_ref[1], cur_ref[1])
    harm_real = harm_ref[:, 0, :]
    harm_imag = harm_ref[:, 1, :]
    proj_ref[0] = gram(harm_real, cur_ref[0]) + gram(harm_imag, cur_ref[1])
    proj_ref[1] = gram(harm_real, cur_ref[1]) - gram(harm_imag, cur_ref[0])
    lax.fori_loop(0, (cols - 1) * blocks, forward, 0)
    mine = []
    for n in range(blocks):
        slot = lax.rem(me + rows - blocks * col - n, rows)
        arrived(slot)
        copy = pltpu.make_async_copy(slices.at[slot], far_buf.at[n, :, window(col)], local_sems.at[n])
        copy.start()
        mine.append(copy)
    lax.fori_loop(1, rows, sent_first, 0)
    for k in range(2 * half):
        near_ref[k] = slices[(half - k) % rows]
    lax.fori_loop(0, (cols - 1) * blocks, finish_second, 0)
    for copy in mine:
        copy.wait()
    far_ref[...] = far_buf[...]


def gather_pieces(vector, basis_one, basis, harmonics, blocks, half, width, collective_id):
    rows = lax.axis_size("row")
    cols = lax.axis_size("col")
    parts, fields, elements = vector.shape
    flat = vector.reshape(parts * fields, elements)
    near, far, cross, self_gram, proj = pl.pallas_call(
        partial(gather_kernel, rows, cols, blocks, half),
        out_shape=(
            jax.ShapeDtypeStruct((2 * half, parts * fields, width), vector.dtype),
            jax.ShapeDtypeStruct((blocks, parts * fields, elements), vector.dtype),
            jax.ShapeDtypeStruct((fields, fields), jnp.float32),
            jax.ShapeDtypeStruct((fields, fields), jnp.float32),
            jax.ShapeDtypeStruct((2, harmonics.shape[0], fields), jnp.float32),
        ),
        in_specs=[pl.BlockSpec(memory_space=pltpu.VMEM)] * 4,
        out_specs=tuple(pl.BlockSpec(memory_space=pltpu.VMEM) for _ in range(5)),
        scratch_shapes=[
            pltpu.VMEM((rows, parts * fields, width), vector.dtype),
            pltpu.VMEM((blocks, parts * fields, elements), vector.dtype),
            pltpu.SemaphoreType.DMA((rows,)),
            pltpu.SemaphoreType.DMA((rows,)),
            pltpu.SemaphoreType.DMA(((cols - 1) * blocks,)),
            pltpu.SemaphoreType.DMA(((cols - 1) * blocks,)),
            pltpu.SemaphoreType.DMA((blocks + 1,)),
        ],
        compiler_params=pltpu.CompilerParams(collective_id=collective_id, has_side_effects=True),
    )(flat, basis_one, basis, harmonics)
    return (
        near.reshape(2 * half, parts, fields, width),
        far,
        cross,
        self_gram,
        proj,
    )


def reduce_kernel(cols, x_ref, o_ref, parts_buf, full, first_send, first_recv, second_send, second_recv):
    me = lax.axis_index("row")
    col = lax.axis_index("col")
    width = parts_buf.shape[-1]
    barrier = pltpu.get_barrier_semaphore()

    def col_peer(e):
        return (me, lax.rem(col + e, cols))

    def window(c):
        return pl.ds(pl.multiple_of(c * width, width), width)

    def first(e):
        return pltpu.make_async_remote_copy(
            src_ref=x_ref.at[:, window(lax.rem(col + e, cols))],
            dst_ref=parts_buf.at[e],
            send_sem=first_send.at[e],
            recv_sem=first_recv.at[e],
            device_id=col_peer(e),
            device_id_type=MESH,
        )

    def second(e):
        return pltpu.make_async_remote_copy(
            src_ref=full.at[:, window(col)],
            dst_ref=full.at[:, window(col)],
            send_sem=second_send.at[e],
            recv_sem=second_recv.at[e],
            device_id=col_peer(e),
            device_id_type=MESH,
        )

    def greet(e, carry):
        pl.semaphore_signal(barrier, inc=1, device_id=col_peer(e), device_id_type=MESH)
        return carry

    def start_first(e, carry):
        first(e).start()
        return carry

    def finish_first(e, carry):
        first(e).wait()
        return carry

    def start_second(e, carry):
        second(e).start()
        return carry

    def finish_second(e, carry):
        second(e).wait_send()
        pltpu.make_async_remote_copy(
            src_ref=full.at[:, window(col)],
            dst_ref=full.at[:, window(lax.rem(col + cols - e, cols))],
            send_sem=second_send.at[e],
            recv_sem=second_recv.at[e],
            device_id=col_peer(e),
            device_id_type=MESH,
        ).wait_recv()
        return carry

    def add(source, total):
        return total + parts_buf[lax.rem(col + cols - source, cols)]

    lax.fori_loop(1, cols, greet, 0)
    pl.semaphore_wait(barrier, cols - 1)
    lax.fori_loop(1, cols, start_first, 0)
    parts_buf[0] = x_ref[:, window(col)]
    lax.fori_loop(1, cols, finish_first, 0)
    full[:, window(col)] = lax.fori_loop(1, cols, add, parts_buf[col])
    lax.fori_loop(1, cols, start_second, 0)
    lax.fori_loop(1, cols, finish_second, 0)
    o_ref[...] = full[...]


def col_reduce(partial_sum, collective_id):
    cols = lax.axis_size("col")
    parts, fields, elements = partial_sum.shape
    width = elements // cols
    flat = partial_sum.reshape(parts * fields, elements)
    summed = pl.pallas_call(
        partial(reduce_kernel, cols),
        out_shape=jax.ShapeDtypeStruct(flat.shape, jnp.float32),
        in_specs=[pl.BlockSpec(memory_space=pltpu.VMEM)],
        out_specs=pl.BlockSpec(memory_space=pltpu.VMEM),
        scratch_shapes=[
            pltpu.VMEM((cols, parts * fields, width), jnp.float32),
            pltpu.VMEM((parts * fields, elements), jnp.float32),
            pltpu.SemaphoreType.DMA((cols,)),
            pltpu.SemaphoreType.DMA((cols,)),
            pltpu.SemaphoreType.DMA((cols,)),
            pltpu.SemaphoreType.DMA((cols,)),
        ],
        compiler_params=pltpu.CompilerParams(collective_id=collective_id, has_side_effects=True),
    )(flat)
    return summed.reshape(partial_sum.shape)


def row_psum(ids, *arrays):
    flat = [a.reshape(-1) for a in arrays]
    sizes = [f.shape[0] for f in flat]
    total = sum(sizes)
    padded = -(-total // 1024) * 1024
    packed = jnp.concatenate(flat + [jnp.zeros((padded - total,), jnp.float32)]).reshape(-1, 128)
    summed = row_allreduce(packed, len(ids)).reshape(-1)
    ids.append(None)
    outs = []
    start = 0
    for a, size in zip(arrays, sizes):
        outs.append(summed[start : start + size].reshape(a.shape))
        start += size
    return outs[0] if len(outs) == 1 else tuple(outs)


def complex_lhs(values, part_axis):
    real = jnp.take(values, 0, axis=part_axis)
    imag = jnp.take(values, 1, axis=part_axis)
    return jnp.stack([jnp.stack([real, -imag]), jnp.stack([imag, real])])


def inner_products(first, second):
    return jnp.einsum("csn,ctn->st", first, second, precision=highest)


def combine_rows(matrix, vectors):
    return jnp.einsum("st,ctn->csn", matrix, vectors, precision=highest)


def matmul(left, right):
    return jnp.dot(left, right, precision=highest)


def lower_inverse(lower):
    identity = jnp.eye(lower.shape[0], dtype=lower.dtype)
    return lax.linalg.triangular_solve(lower, identity, left_side=True, lower=True)


def project(harmonics, vectors):

    def contract(left, right):
        return jnp.einsum("mn,sn->ms", left, right, precision=highest)

    real_out = contract(harmonics[0], vectors[0]) + contract(harmonics[1], vectors[1])
    imag_out = contract(harmonics[0], vectors[1]) - contract(harmonics[1], vectors[0])
    return jnp.stack([real_out, imag_out])


def body(incident, diagonal, near_blocks, left_factors, right_factors, flags, ranks, harmonics):
    blocks = left_factors.shape[1]
    slots = near_blocks.shape[1]
    width = near_blocks.shape[4]
    half_band = slots // 2
    elements = incident.shape[2]
    fields = incident.shape[1]
    clusters = lax.axis_size("row")
    row_index = lax.axis_index("row")
    column = lax.axis_index("col")
    ids = []

    def operator_terms(near_pieces, far_pieces):
        near_on = flags[0] == 1
        near_vector = jnp.where(near_on[:, None, None, None], near_pieces, 0).astype(jnp.bfloat16)
        near_out = jnp.einsum(
            "caksf,kaef->cse",
            complex_lhs(near_vector, 1),
            near_blocks[0],
            preferred_element_type=jnp.float32,
        )
        cluster = column * blocks + jnp.arange(blocks, dtype=jnp.int32)
        offset = (cluster - row_index + half_band) % clusters
        is_near = (offset < slots) & (flags[0, jnp.minimum(offset, slots - 1)] == 1)
        keep = (~is_near)[:, None] & (
            jnp.arange(right_factors.shape[3], dtype=jnp.int32)[None, :] < ranks[0][:, None]
        )
        products = jnp.einsum(
            "nxf,nbrf->nxbr", far_pieces, right_factors[0], preferred_element_type=jnp.float32
        )
        coeffs = jnp.stack(
            [
                products[:, :fields, 0] - products[:, fields:, 1],
                products[:, :fields, 1] + products[:, fields:, 0],
            ]
        )
        coeffs = jnp.where(keep[None, :, None, :], coeffs, 0.0).astype(jnp.bfloat16)
        far_out = jnp.einsum(
            "cansr,nare->cse",
            complex_lhs(coeffs, 0),
            left_factors[0],
            preferred_element_type=jnp.float32,
        )
        return near_out + far_out

    def apply_operator(vector, basis_one):
        rounded = vector.astype(jnp.bfloat16)
        near_pieces, far_pieces, cross, self_gram, proj = gather_pieces(
            rounded, basis_one, vector, jnp.transpose(harmonics, (1, 0, 2)), blocks, half_band, width, 16 + len(ids)
        )
        ids.append(None)
        total = operator_terms(near_pieces, far_pieces)
        summed = col_reduce(total, 32 + len(ids))
        ids.append(None)
        return summed + diagonal[None, None, :] * vector, cross, self_gram, proj

    lower_first = jnp.linalg.cholesky(row_psum(ids, inner_products(incident, incident)))
    basis_one = combine_rows(lower_inverse(lower_first), incident)
    image, _, self_one, harmonics_one = apply_operator(basis_one, basis_one)
    coupling_one, harmonics_one, self_one = row_psum(
        ids, inner_products(image, basis_one), harmonics_one, self_one
    )
    rest = image - combine_rows(coupling_one, basis_one)
    gram_one = row_psum(ids, inner_products(rest, rest))
    lower_second = jnp.linalg.cholesky(gram_one)
    basis_two = combine_rows(lower_inverse(lower_second), rest)
    image, cross, self_two, harmonics_two = apply_operator(basis_two, basis_one)
    coupling_onetwo, coupling_two, image_gram, cross, self_two, harmonics_two = row_psum(
        ids,
        inner_products(image, basis_one),
        inner_products(image, basis_two),
        inner_products(image, image),
        cross,
        self_two,
        harmonics_two,
    )
    coupling = jnp.concatenate([coupling_onetwo, coupling_two], axis=1)
    basis_gram = jnp.concatenate(
        [
            jnp.concatenate([self_one, cross], axis=1),
            jnp.concatenate([cross.T, self_two], axis=1),
        ],
        axis=0,
    )
    gram_two = (
        image_gram
        - 2.0 * matmul(coupling, coupling.T)
        + matmul(coupling, matmul(basis_gram, coupling.T))
    )
    upper_left = matmul(coupling_one, coupling_one.T) + gram_one
    upper_right = matmul(coupling_one, coupling_onetwo.T) + matmul(lower_second, coupling_two.T)
    lower_right = (
        matmul(coupling_onetwo, coupling_onetwo.T) + matmul(coupling_two, coupling_two.T) + gram_two
    )
    normal = jnp.concatenate(
        [
            jnp.concatenate([upper_left, upper_right], axis=1),
            jnp.concatenate([upper_right.T, lower_right], axis=1),
        ],
        axis=0,
    )
    target = jnp.concatenate(
        [matmul(lower_first, coupling_one.T), matmul(lower_first, coupling_onetwo.T)], axis=1
    )
    factor_inverse = lower_inverse(jnp.linalg.cholesky(normal))
    weights = matmul(factor_inverse.T, matmul(factor_inverse, target.T)).T
    first_weights = weights[:, :fields]
    second_weights = weights[:, fields:]
    solution = combine_rows(first_weights, basis_one) + combine_rows(second_weights, basis_two)
    coefficients = jnp.einsum(
        "cmt,st->cms", harmonics_one, first_weights, precision=highest
    ) + jnp.einsum("cmt,st->cms", harmonics_two, second_weights, precision=highest)
    return (solution, coefficients)


def solution(mesh):
    in_specs = (
        P(None, None, "row"),
        P("row"),
        P("row", None, None, None, "col"),
        P("row", "col", None, None, None),
        P("row", "col", None, None, None),
        P("row", None),
        P("row", "col"),
        P(None, None, "row"),
    )
    out_specs = (P(None, None, "row"), P())
    return jax.shard_map(body, mesh=mesh, in_specs=in_specs, out_specs=out_specs, check_vma=False)
```

```python
from functools import partial

import jax
import jax.numpy as jnp
from jax import lax
from jax.experimental import pallas as pl
from jax.experimental.pallas import tpu as pltpu
from jax.sharding import PartitionSpec as P

highest = lax.Precision.HIGHEST
MESH = pl.DeviceIdType.MESH


def allreduce_kernel(inner, outer, x_ref, o_ref, buf, partial_buf,
                     first_send, first_recv, second_send, second_recv):
    me = lax.axis_index("row")
    col = lax.axis_index("col")
    high = me // inner
    low = me % inner
    barrier = pltpu.get_barrier_semaphore()

    def inner_peer(d):
        return (high * inner + lax.rem(low + d, inner), col)

    def outer_peer(d):
        return (lax.rem(high + d, outer) * inner + low, col)

    def first(d):
        return pltpu.make_async_remote_copy(
            src_ref=x_ref,
            dst_ref=buf.at[d],
            send_sem=first_send.at[d],
            recv_sem=first_recv.at[d],
            device_id=inner_peer(d),
            device_id_type=MESH,
        )

    def second(d):
        return pltpu.make_async_remote_copy(
            src_ref=partial_buf.at[0],
            dst_ref=partial_buf.at[d],
            send_sem=second_send.at[d],
            recv_sem=second_recv.at[d],
            device_id=outer_peer(d),
            device_id_type=MESH,
        )

    def greet_inner(d, carry):
        pl.semaphore_signal(barrier, inc=1, device_id=inner_peer(d), device_id_type=MESH)
        return carry

    def greet_outer(d, carry):
        pl.semaphore_signal(barrier, inc=1, device_id=outer_peer(d), device_id_type=MESH)
        return carry

    def start_first(d, carry):
        first(d).start()
        return carry

    def finish_first(d, carry):
        first(d).wait()
        return carry

    def start_second(d, carry):
        second(d).start()
        return carry

    def finish_second(d, carry):
        second(d).wait()
        return carry

    def add_inner(source, total):
        return total + buf[lax.rem(low + inner - source, inner)]

    def add_outer(source, total):
        return total + partial_buf[lax.rem(high + outer - source, outer)]

    lax.fori_loop(1, inner, greet_inner, 0)
    lax.fori_loop(1, outer, greet_outer, 0)
    pl.semaphore_wait(barrier, inner - 1 + outer - 1)
    lax.fori_loop(1, inner, start_first, 0)
    buf[0] = x_ref[...]
    lax.fori_loop(1, inner, finish_first, 0)
    partial_buf[0] = lax.fori_loop(1, inner, add_inner, buf[low])
    lax.fori_loop(1, outer, start_second, 0)
    lax.fori_loop(1, outer, finish_second, 0)
    o_ref[...] = lax.fori_loop(1, outer, add_outer, partial_buf[high])


def row_allreduce(packed, collective_id):
    n = lax.axis_size("row")
    inner = 8 if n % 8 == 0 else n
    outer = n // inner
    rows, lanes = packed.shape
    return pl.pallas_call(
        partial(allreduce_kernel, inner, outer),
        out_shape=jax.ShapeDtypeStruct((rows, lanes), jnp.float32),
        in_specs=[pl.BlockSpec(memory_space=pltpu.VMEM)],
        out_specs=pl.BlockSpec(memory_space=pltpu.VMEM),
        scratch_shapes=[
            pltpu.VMEM((inner, rows, lanes), jnp.float32),
            pltpu.VMEM((outer, rows, lanes), jnp.float32),
            pltpu.SemaphoreType.DMA((inner,)),
            pltpu.SemaphoreType.DMA((inner,)),
            pltpu.SemaphoreType.DMA((outer,)),
            pltpu.SemaphoreType.DMA((outer,)),
        ],
        compiler_params=pltpu.CompilerParams(collective_id=collective_id, has_side_effects=True),
    )(packed)


def gram(left, right):
    return lax.dot_general(
        left, right, (((1,), (1,)), ((), ())), precision=highest, preferred_element_type=jnp.float32
    )


def gather_kernel(rows, cols, blocks, half, v_ref, one_ref, cur_ref, harm_ref,
                  near_ref, far_ref, cross_ref, self_ref, proj_ref, slices, far_buf,
                  first_send, first_recv, second_send, second_recv, local_sems):
    me = lax.axis_index("row")
    col = lax.axis_index("col")
    width = slices.shape[-1]
    barrier = pltpu.get_barrier_semaphore()

    def row_peer(d):
        return (lax.rem(me + d, rows), col)

    def col_peer(e):
        return (me, lax.rem(col + e, cols))

    def window(c):
        return pl.ds(pl.multiple_of(c * width, width), width)

    own = v_ref.at[:, window(col)]

    def first(d):
        return pltpu.make_async_remote_copy(
            src_ref=own,
            dst_ref=slices.at[d],
            send_sem=first_send.at[d],
            recv_sem=first_recv.at[d],
            device_id=row_peer(d),
            device_id_type=MESH,
        )

    def second(t):
        e = 1 + t // blocks
        n = t % blocks
        target = lax.rem(col + e, cols)
        slot = lax.rem(me + rows - blocks * target - n, rows)
        return pltpu.make_async_remote_copy(
            src_ref=slices.at[slot],
            dst_ref=far_buf.at[n, :, window(col)],
            send_sem=second_send.at[t],
            recv_sem=second_recv.at[t],
            device_id=col_peer(e),
            device_id_type=MESH,
        )

    def greet_row(d, carry):
        pl.semaphore_signal(barrier, inc=1, device_id=row_peer(d), device_id_type=MESH)
        return carry

    def greet_col(e, carry):
        pl.semaphore_signal(barrier, inc=1, device_id=col_peer(e), device_id_type=MESH)
        return carry

    def start_first(d, carry):
        first(d).start()
        return carry

    def finish_second(t, carry):
        second(t).wait()
        return carry

    def arrived(slot):
        pltpu.make_async_remote_copy(
            src_ref=own,
            dst_ref=slices.at[slot],
            send_sem=first_send.at[slot],
            recv_sem=first_recv.at[slot],
            device_id=row_peer(slot),
            device_id_type=MESH,
        ).wait_recv()

    def forward(t, carry):
        target = lax.rem(col + 1 + t // blocks, cols)
        arrived(lax.rem(me + rows - blocks * target - t % blocks, rows))
        second(t).start()
        return carry

    def sent_first(d, carry):
        first(d).wait_send()
        return carry

    lax.fori_loop(1, rows, greet_row, 0)
    lax.fori_loop(1, cols, greet_col, 0)
    pl.semaphore_wait(barrier, rows - 1 + cols - 1)
    lax.fori_loop(1, rows, start_first, 0)
    pltpu.make_async_copy(own, slices.at[0], first_recv.at[0]).start()
    cross_ref[...] = gram(one_ref[0], cur_ref[0]) + gram(one_ref[1], cur_ref[1])
    self_ref[...] = gram(cur_ref[0], cur_ref[0]) + gram(cur_ref[1], cur_ref[1])
    harm_real = harm_ref[:, 0, :]
    harm_imag = harm_ref[:, 1, :]
    proj_ref[0] = gram(harm_real, cur_ref[0]) + gram(harm_imag, cur_ref[1])
    proj_ref[1] = gram(harm_real, cur_ref[1]) - gram(harm_imag, cur_ref[0])
    lax.fori_loop(0, (cols - 1) * blocks, forward, 0)
    mine = []
    for n in range(blocks):
        slot = lax.rem(me + rows - blocks * col - n, rows)
        arrived(slot)
        copy = pltpu.make_async_copy(slices.at[slot], far_buf.at[n, :, window(col)], local_sems.at[n])
        copy.start()
        mine.append(copy)
    lax.fori_loop(1, rows, sent_first, 0)
    for k in range(2 * half):
        near_ref[k] = slices[(half - k) % rows]
    lax.fori_loop(0, (cols - 1) * blocks, finish_second, 0)
    for copy in mine:
        copy.wait()
    far_ref[...] = far_buf[...]


def gather_pieces(vector, basis_one, basis, harmonics, blocks, half, width, collective_id):
    rows = lax.axis_size("row")
    cols = lax.axis_size("col")
    parts, fields, elements = vector.shape
    flat = vector.reshape(parts * fields, elements)
    near, far, cross, self_gram, proj = pl.pallas_call(
        partial(gather_kernel, rows, cols, blocks, half),
        out_shape=(
            jax.ShapeDtypeStruct((2 * half, parts * fields, width), vector.dtype),
            jax.ShapeDtypeStruct((blocks, parts * fields, elements), vector.dtype),
            jax.ShapeDtypeStruct((fields, fields), jnp.float32),
            jax.ShapeDtypeStruct((fields, fields), jnp.float32),
            jax.ShapeDtypeStruct((2, harmonics.shape[0], fields), jnp.float32),
        ),
        in_specs=[pl.BlockSpec(memory_space=pltpu.VMEM)] * 4,
        out_specs=tuple(pl.BlockSpec(memory_space=pltpu.VMEM) for _ in range(5)),
        scratch_shapes=[
            pltpu.VMEM((rows, parts * fields, width), vector.dtype),
            pltpu.VMEM((blocks, parts * fields, elements), vector.dtype),
            pltpu.SemaphoreType.DMA((rows,)),
            pltpu.SemaphoreType.DMA((rows,)),
            pltpu.SemaphoreType.DMA(((cols - 1) * blocks,)),
            pltpu.SemaphoreType.DMA(((cols - 1) * blocks,)),
            pltpu.SemaphoreType.DMA((blocks + 1,)),
        ],
        compiler_params=pltpu.CompilerParams(collective_id=collective_id, has_side_effects=True),
    )(flat, basis_one, basis, harmonics)
    return (
        near.reshape(2 * half, parts, fields, width),
        far,
        cross,
        self_gram,
        proj,
    )


def reduce_kernel(cols, x_ref, o_ref, parts_buf, full, first_send, first_recv, second_send, second_recv):
    me = lax.axis_index("row")
    col = lax.axis_index("col")
    width = parts_buf.shape[-1]
    barrier = pltpu.get_barrier_semaphore()

    def col_peer(e):
        return (me, lax.rem(col + e, cols))

    def window(c):
        return pl.ds(pl.multiple_of(c * width, width), width)

    def first(e):
        return pltpu.make_async_remote_copy(
            src_ref=x_ref.at[:, window(lax.rem(col + e, cols))],
            dst_ref=parts_buf.at[e],
            send_sem=first_send.at[e],
            recv_sem=first_recv.at[e],
            device_id=col_peer(e),
            device_id_type=MESH,
        )

    def second(e):
        return pltpu.make_async_remote_copy(
            src_ref=full.at[:, window(col)],
            dst_ref=full.at[:, window(col)],
            send_sem=second_send.at[e],
            recv_sem=second_recv.at[e],
            device_id=col_peer(e),
            device_id_type=MESH,
        )

    def greet(e, carry):
        pl.semaphore_signal(barrier, inc=1, device_id=col_peer(e), device_id_type=MESH)
        return carry

    def start_first(e, carry):
        first(e).start()
        return carry

    def finish_first(e, carry):
        first(e).wait()
        return carry

    def start_second(e, carry):
        second(e).start()
        return carry

    def finish_second(e, carry):
        second(e).wait_send()
        pltpu.make_async_remote_copy(
            src_ref=full.at[:, window(col)],
            dst_ref=full.at[:, window(lax.rem(col + cols - e, cols))],
            send_sem=second_send.at[e],
            recv_sem=second_recv.at[e],
            device_id=col_peer(e),
            device_id_type=MESH,
        ).wait_recv()
        return carry

    def add(source, total):
        return total + parts_buf[lax.rem(col + cols - source, cols)]

    lax.fori_loop(1, cols, greet, 0)
    pl.semaphore_wait(barrier, cols - 1)
    lax.fori_loop(1, cols, start_first, 0)
    parts_buf[0] = x_ref[:, window(col)]
    lax.fori_loop(1, cols, finish_first, 0)
    full[:, window(col)] = lax.fori_loop(1, cols, add, parts_buf[col])
    lax.fori_loop(1, cols, start_second, 0)
    lax.fori_loop(1, cols, finish_second, 0)
    o_ref[...] = full[...]


def col_reduce(partial_sum, collective_id):
    cols = lax.axis_size("col")
    parts, fields, elements = partial_sum.shape
    width = elements // cols
    flat = partial_sum.reshape(parts * fields, elements)
    summed = pl.pallas_call(
        partial(reduce_kernel, cols),
        out_shape=jax.ShapeDtypeStruct(flat.shape, jnp.float32),
        in_specs=[pl.BlockSpec(memory_space=pltpu.VMEM)],
        out_specs=pl.BlockSpec(memory_space=pltpu.VMEM),
        scratch_shapes=[
            pltpu.VMEM((cols, parts * fields, width), jnp.float32),
            pltpu.VMEM((parts * fields, elements), jnp.float32),
            pltpu.SemaphoreType.DMA((cols,)),
            pltpu.SemaphoreType.DMA((cols,)),
            pltpu.SemaphoreType.DMA((cols,)),
            pltpu.SemaphoreType.DMA((cols,)),
        ],
        compiler_params=pltpu.CompilerParams(collective_id=collective_id, has_side_effects=True),
    )(flat)
    return summed.reshape(partial_sum.shape)


def combine_kernel(first_ref, second_ref, one_ref, two_ref, o_ref):
    for part in range(one_ref.shape[0]):
        o_ref[:, part, :] = jnp.dot(
            first_ref[...], one_ref[part], precision=highest, preferred_element_type=jnp.float32
        ) + jnp.dot(second_ref[...], two_ref[part], precision=highest, preferred_element_type=jnp.float32)


def final_combine(first_weights, second_weights, basis_one, basis_two):
    parts, fields, elements = basis_one.shape
    return pl.pallas_call(
        combine_kernel,
        out_shape=jax.ShapeDtypeStruct((fields, parts, elements), jnp.float32),
        in_specs=[pl.BlockSpec(memory_space=pltpu.VMEM)] * 4,
        out_specs=pl.BlockSpec(memory_space=pltpu.VMEM),
    )(first_weights, second_weights, basis_one, basis_two)


def row_psum(ids, *arrays):
    flat = [a.reshape(-1) for a in arrays]
    sizes = [f.shape[0] for f in flat]
    total = sum(sizes)
    padded = -(-total // 1024) * 1024
    packed = jnp.concatenate(flat + [jnp.zeros((padded - total,), jnp.float32)]).reshape(-1, 128)
    summed = row_allreduce(packed, len(ids)).reshape(-1)
    ids.append(None)
    outs = []
    start = 0
    for a, size in zip(arrays, sizes):
        outs.append(summed[start : start + size].reshape(a.shape))
        start += size
    return outs[0] if len(outs) == 1 else tuple(outs)


def complex_lhs(values, part_axis):
    real = jnp.take(values, 0, axis=part_axis)
    imag = jnp.take(values, 1, axis=part_axis)
    return jnp.stack([jnp.stack([real, -imag]), jnp.stack([imag, real])])


def inner_products(first, second):
    return jnp.einsum("csn,ctn->st", first, second, precision=highest)


def combine_rows(matrix, vectors):
    return jnp.einsum("st,ctn->csn", matrix, vectors, precision=highest)


def matmul(left, right):
    return jnp.dot(left, right, precision=highest)


def lower_inverse(lower):
    identity = jnp.eye(lower.shape[0], dtype=lower.dtype)
    return lax.linalg.triangular_solve(lower, identity, left_side=True, lower=True)


def project(harmonics, vectors):

    def contract(left, right):
        return jnp.einsum("mn,sn->ms", left, right, precision=highest)

    real_out = contract(harmonics[0], vectors[0]) + contract(harmonics[1], vectors[1])
    imag_out = contract(harmonics[0], vectors[1]) - contract(harmonics[1], vectors[0])
    return jnp.stack([real_out, imag_out])


def body(incident, diagonal, near_blocks, left_factors, right_factors, flags, ranks, harmonics):
    blocks = left_factors.shape[1]
    slots = near_blocks.shape[1]
    width = near_blocks.shape[4]
    half_band = slots // 2
    elements = incident.shape[2]
    fields = incident.shape[1]
    clusters = lax.axis_size("row")
    row_index = lax.axis_index("row")
    column = lax.axis_index("col")
    ids = []

    def operator_terms(near_pieces, far_pieces):
        near_on = flags[0] == 1
        near_vector = jnp.where(near_on[:, None, None, None], near_pieces, 0).astype(jnp.bfloat16)
        near_out = jnp.einsum(
            "caksf,kaef->cse",
            complex_lhs(near_vector, 1),
            near_blocks[0],
            preferred_element_type=jnp.float32,
        )
        cluster = column * blocks + jnp.arange(blocks, dtype=jnp.int32)
        offset = (cluster - row_index + half_band) % clusters
        is_near = (offset < slots) & (flags[0, jnp.minimum(offset, slots - 1)] == 1)
        keep = (~is_near)[:, None] & (
            jnp.arange(right_factors.shape[3], dtype=jnp.int32)[None, :] < ranks[0][:, None]
        )
        products = jnp.einsum(
            "nxf,nbrf->nxbr", far_pieces, right_factors[0], preferred_element_type=jnp.float32
        )
        coeffs = jnp.stack(
            [
                products[:, :fields, 0] - products[:, fields:, 1],
                products[:, :fields, 1] + products[:, fields:, 0],
            ]
        )
        coeffs = jnp.where(keep[None, :, None, :], coeffs, 0.0).astype(jnp.bfloat16)
        far_out = jnp.einsum(
            "cansr,nare->cse",
            complex_lhs(coeffs, 0),
            left_factors[0],
            preferred_element_type=jnp.float32,
        )
        return near_out + far_out

    def apply_operator(vector, basis_one):
        rounded = vector.astype(jnp.bfloat16)
        near_pieces, far_pieces, cross, self_gram, proj = gather_pieces(
            rounded, basis_one, vector, jnp.transpose(harmonics, (1, 0, 2)), blocks, half_band, width, 16 + len(ids)
        )
        ids.append(None)
        total = operator_terms(near_pieces, far_pieces)
        summed = col_reduce(total, 32 + len(ids))
        ids.append(None)
        return summed + diagonal[None, None, :] * vector, cross, self_gram, proj

    lower_first = jnp.linalg.cholesky(row_psum(ids, inner_products(incident, incident)))
    basis_one = combine_rows(lower_inverse(lower_first), incident)
    image, _, self_one, harmonics_one = apply_operator(basis_one, basis_one)
    coupling_one, harmonics_one, self_one = row_psum(
        ids, inner_products(image, basis_one), harmonics_one, self_one
    )
    rest = image - combine_rows(coupling_one, basis_one)
    gram_one = row_psum(ids, inner_products(rest, rest))
    lower_second = jnp.linalg.cholesky(gram_one)
    basis_two = combine_rows(lower_inverse(lower_second), rest)
    image, cross, self_two, harmonics_two = apply_operator(basis_two, basis_one)
    coupling_onetwo, coupling_two, image_gram, cross, self_two, harmonics_two = row_psum(
        ids,
        inner_products(image, basis_one),
        inner_products(image, basis_two),
        inner_products(image, image),
        cross,
        self_two,
        harmonics_two,
    )
    coupling = jnp.concatenate([coupling_onetwo, coupling_two], axis=1)
    basis_gram = jnp.concatenate(
        [
            jnp.concatenate([self_one, cross], axis=1),
            jnp.concatenate([cross.T, self_two], axis=1),
        ],
        axis=0,
    )
    gram_two = (
        image_gram
        - 2.0 * matmul(coupling, coupling.T)
        + matmul(coupling, matmul(basis_gram, coupling.T))
    )
    upper_left = matmul(coupling_one, coupling_one.T) + gram_one
    upper_right = matmul(coupling_one, coupling_onetwo.T) + matmul(lower_second, coupling_two.T)
    lower_right = (
        matmul(coupling_onetwo, coupling_onetwo.T) + matmul(coupling_two, coupling_two.T) + gram_two
    )
    normal = jnp.concatenate(
        [
            jnp.concatenate([upper_left, upper_right], axis=1),
            jnp.concatenate([upper_right.T, lower_right], axis=1),
        ],
        axis=0,
    )
    target = jnp.concatenate(
        [matmul(lower_first, coupling_one.T), matmul(lower_first, coupling_onetwo.T)], axis=1
    )
    factor_inverse = lower_inverse(jnp.linalg.cholesky(normal))
    weights = matmul(factor_inverse.T, matmul(factor_inverse, target.T)).T
    first_weights = weights[:, :fields]
    second_weights = weights[:, fields:]
    solution = final_combine(first_weights, second_weights, basis_one, basis_two).transpose(1, 0, 2)
    coefficients = jnp.einsum(
        "cmt,st->cms", harmonics_one, first_weights, precision=highest
    ) + jnp.einsum("cmt,st->cms", harmonics_two, second_weights, precision=highest)
    return (solution, coefficients)


def solution(mesh):
    in_specs = (
        P(None, None, "row"),
        P("row"),
        P("row", None, None, None, "col"),
        P("row", "col", None, None, None),
        P("row", "col", None, None, None),
        P("row", None),
        P("row", "col"),
        P(None, None, "row"),
    )
    out_specs = (P(None, None, "row"), P())
    return jax.shard_map(body, mesh=mesh, in_specs=in_specs, out_specs=out_specs, check_vma=False)
```

```python
from functools import partial

import jax
import jax.numpy as jnp
from jax import lax
from jax.experimental import pallas as pl
from jax.experimental.pallas import tpu as pltpu
from jax.sharding import PartitionSpec as P

highest = lax.Precision.HIGHEST
MESH = pl.DeviceIdType.MESH


def allreduce_kernel(inner, outer, x_ref, o_ref, buf, partial_buf,
                     first_send, first_recv, second_send, second_recv):
    me = lax.axis_index("row")
    col = lax.axis_index("col")
    high = me // inner
    low = me % inner
    barrier = pltpu.get_barrier_semaphore()

    def inner_peer(d):
        return (high * inner + lax.rem(low + d, inner), col)

    def outer_peer(d):
        return (lax.rem(high + d, outer) * inner + low, col)

    def first(d):
        return pltpu.make_async_remote_copy(
            src_ref=x_ref,
            dst_ref=buf.at[d],
            send_sem=first_send.at[d],
            recv_sem=first_recv.at[d],
            device_id=inner_peer(d),
            device_id_type=MESH,
        )

    def second(d):
        return pltpu.make_async_remote_copy(
            src_ref=partial_buf.at[0],
            dst_ref=partial_buf.at[d],
            send_sem=second_send.at[d],
            recv_sem=second_recv.at[d],
            device_id=outer_peer(d),
            device_id_type=MESH,
        )

    def greet_inner(d, carry):
        pl.semaphore_signal(barrier, inc=1, device_id=inner_peer(d), device_id_type=MESH)
        return carry

    def greet_outer(d, carry):
        pl.semaphore_signal(barrier, inc=1, device_id=outer_peer(d), device_id_type=MESH)
        return carry

    def start_first(d, carry):
        first(d).start()
        return carry

    def finish_first(d, carry):
        first(d).wait()
        return carry

    def start_second(d, carry):
        second(d).start()
        return carry

    def finish_second(d, carry):
        second(d).wait()
        return carry

    def add_inner(source, total):
        return total + buf[lax.rem(low + inner - source, inner)]

    def add_outer(source, total):
        return total + partial_buf[lax.rem(high + outer - source, outer)]

    lax.fori_loop(1, inner, greet_inner, 0)
    lax.fori_loop(1, outer, greet_outer, 0)
    pl.semaphore_wait(barrier, inner - 1 + outer - 1)
    lax.fori_loop(1, inner, start_first, 0)
    buf[0] = x_ref[...]
    lax.fori_loop(1, inner, finish_first, 0)
    partial_buf[0] = lax.fori_loop(1, inner, add_inner, buf[low])
    lax.fori_loop(1, outer, start_second, 0)
    lax.fori_loop(1, outer, finish_second, 0)
    o_ref[...] = lax.fori_loop(1, outer, add_outer, partial_buf[high])


def row_allreduce(packed, collective_id):
    n = lax.axis_size("row")
    inner = 8 if n % 8 == 0 else n
    outer = n // inner
    rows, lanes = packed.shape
    return pl.pallas_call(
        partial(allreduce_kernel, inner, outer),
        out_shape=jax.ShapeDtypeStruct((rows, lanes), jnp.float32),
        in_specs=[pl.BlockSpec(memory_space=pltpu.VMEM)],
        out_specs=pl.BlockSpec(memory_space=pltpu.VMEM),
        scratch_shapes=[
            pltpu.VMEM((inner, rows, lanes), jnp.float32),
            pltpu.VMEM((outer, rows, lanes), jnp.float32),
            pltpu.SemaphoreType.DMA((inner,)),
            pltpu.SemaphoreType.DMA((inner,)),
            pltpu.SemaphoreType.DMA((outer,)),
            pltpu.SemaphoreType.DMA((outer,)),
        ],
        compiler_params=pltpu.CompilerParams(collective_id=collective_id, has_side_effects=True),
    )(packed)


def gram(left, right):
    return lax.dot_general(
        left, right, (((1,), (1,)), ((), ())), precision=highest, preferred_element_type=jnp.float32
    )


def gather_kernel(rows, cols, blocks, half, v_ref, one_ref, cur_ref, harm_ref,
                  near_ref, far_ref, cross_ref, self_ref, proj_ref, slices, far_buf,
                  first_send, first_recv, second_send, second_recv, local_sems):
    me = lax.axis_index("row")
    col = lax.axis_index("col")
    width = slices.shape[-1]
    barrier = pltpu.get_barrier_semaphore()

    def row_peer(d):
        return (lax.rem(me + d, rows), col)

    def col_peer(e):
        return (me, lax.rem(col + e, cols))

    def window(c):
        return pl.ds(pl.multiple_of(c * width, width), width)

    own = v_ref.at[:, window(col)]

    def first(d):
        return pltpu.make_async_remote_copy(
            src_ref=own,
            dst_ref=slices.at[d],
            send_sem=first_send.at[d],
            recv_sem=first_recv.at[d],
            device_id=row_peer(d),
            device_id_type=MESH,
        )

    def second(t):
        e = 1 + t // blocks
        n = t % blocks
        target = lax.rem(col + e, cols)
        slot = lax.rem(me + rows - blocks * target - n, rows)
        return pltpu.make_async_remote_copy(
            src_ref=slices.at[slot],
            dst_ref=far_buf.at[n, :, window(col)],
            send_sem=second_send.at[t],
            recv_sem=second_recv.at[t],
            device_id=col_peer(e),
            device_id_type=MESH,
        )

    def greet_row(d, carry):
        pl.semaphore_signal(barrier, inc=1, device_id=row_peer(d), device_id_type=MESH)
        return carry

    def greet_col(e, carry):
        pl.semaphore_signal(barrier, inc=1, device_id=col_peer(e), device_id_type=MESH)
        return carry

    def start_first(d, carry):
        first(d).start()
        return carry

    def finish_second(t, carry):
        second(t).wait()
        return carry

    def arrived(slot):
        pltpu.make_async_remote_copy(
            src_ref=own,
            dst_ref=slices.at[slot],
            send_sem=first_send.at[slot],
            recv_sem=first_recv.at[slot],
            device_id=row_peer(slot),
            device_id_type=MESH,
        ).wait_recv()

    def forward(t, carry):
        target = lax.rem(col + 1 + t // blocks, cols)
        arrived(lax.rem(me + rows - blocks * target - t % blocks, rows))
        second(t).start()
        return carry

    def sent_first(d, carry):
        first(d).wait_send()
        return carry

    lax.fori_loop(1, rows, greet_row, 0)
    lax.fori_loop(1, cols, greet_col, 0)
    pl.semaphore_wait(barrier, rows - 1 + cols - 1)
    lax.fori_loop(1, rows, start_first, 0)
    pltpu.make_async_copy(own, slices.at[0], first_recv.at[0]).start()
    cross_ref[...] = gram(one_ref[0], cur_ref[0]) + gram(one_ref[1], cur_ref[1])
    self_ref[...] = gram(cur_ref[0], cur_ref[0]) + gram(cur_ref[1], cur_ref[1])
    harm_real = harm_ref[:, 0, :]
    harm_imag = harm_ref[:, 1, :]
    proj_ref[0] = gram(harm_real, cur_ref[0]) + gram(harm_imag, cur_ref[1])
    proj_ref[1] = gram(harm_real, cur_ref[1]) - gram(harm_imag, cur_ref[0])
    lax.fori_loop(0, (cols - 1) * blocks, forward, 0)
    mine = []
    for n in range(blocks):
        slot = lax.rem(me + rows - blocks * col - n, rows)
        arrived(slot)
        copy = pltpu.make_async_copy(slices.at[slot], far_buf.at[n, :, window(col)], local_sems.at[n])
        copy.start()
        mine.append(copy)
    lax.fori_loop(1, rows, sent_first, 0)
    for k in range(2 * half):
        near_ref[k] = slices[(half - k) % rows]
    lax.fori_loop(0, (cols - 1) * blocks, finish_second, 0)
    for copy in mine:
        copy.wait()
    far_ref[...] = far_buf[...]


def gather_pieces(vector, basis_one, basis, harmonics, blocks, half, width, collective_id):
    rows = lax.axis_size("row")
    cols = lax.axis_size("col")
    parts, fields, elements = vector.shape
    flat = vector.reshape(parts * fields, elements)
    near, far, cross, self_gram, proj = pl.pallas_call(
        partial(gather_kernel, rows, cols, blocks, half),
        out_shape=(
            jax.ShapeDtypeStruct((2 * half, parts * fields, width), vector.dtype),
            jax.ShapeDtypeStruct((blocks, parts * fields, elements), vector.dtype),
            jax.ShapeDtypeStruct((fields, fields), jnp.float32),
            jax.ShapeDtypeStruct((fields, fields), jnp.float32),
            jax.ShapeDtypeStruct((2, harmonics.shape[0], fields), jnp.float32),
        ),
        in_specs=[pl.BlockSpec(memory_space=pltpu.VMEM)] * 4,
        out_specs=tuple(pl.BlockSpec(memory_space=pltpu.VMEM) for _ in range(5)),
        scratch_shapes=[
            pltpu.VMEM((rows, parts * fields, width), vector.dtype),
            pltpu.VMEM((blocks, parts * fields, elements), vector.dtype),
            pltpu.SemaphoreType.DMA((rows,)),
            pltpu.SemaphoreType.DMA((rows,)),
            pltpu.SemaphoreType.DMA(((cols - 1) * blocks,)),
            pltpu.SemaphoreType.DMA(((cols - 1) * blocks,)),
            pltpu.SemaphoreType.DMA((blocks + 1,)),
        ],
        compiler_params=pltpu.CompilerParams(collective_id=collective_id, has_side_effects=True),
    )(flat, basis_one, basis, harmonics)
    return (
        near.reshape(2 * half, parts, fields, width),
        far,
        cross,
        self_gram,
        proj,
    )


def reduce_kernel(cols, x_ref, o_ref, parts_buf, full, first_send, first_recv, second_send, second_recv):
    me = lax.axis_index("row")
    col = lax.axis_index("col")
    width = parts_buf.shape[-1]
    barrier = pltpu.get_barrier_semaphore()

    def col_peer(e):
        return (me, lax.rem(col + e, cols))

    def window(c):
        return pl.ds(pl.multiple_of(c * width, width), width)

    def first(e):
        return pltpu.make_async_remote_copy(
            src_ref=x_ref.at[:, window(lax.rem(col + e, cols))],
            dst_ref=parts_buf.at[e],
            send_sem=first_send.at[e],
            recv_sem=first_recv.at[e],
            device_id=col_peer(e),
            device_id_type=MESH,
        )

    def second(e):
        return pltpu.make_async_remote_copy(
            src_ref=full.at[:, window(col)],
            dst_ref=full.at[:, window(col)],
            send_sem=second_send.at[e],
            recv_sem=second_recv.at[e],
            device_id=col_peer(e),
            device_id_type=MESH,
        )

    def greet(e, carry):
        pl.semaphore_signal(barrier, inc=1, device_id=col_peer(e), device_id_type=MESH)
        return carry

    def start_first(e, carry):
        first(e).start()
        return carry

    def finish_first(e, carry):
        first(e).wait()
        return carry

    def start_second(e, carry):
        second(e).start()
        return carry

    def finish_second(e, carry):
        second(e).wait_send()
        pltpu.make_async_remote_copy(
            src_ref=full.at[:, window(col)],
            dst_ref=full.at[:, window(lax.rem(col + cols - e, cols))],
            send_sem=second_send.at[e],
            recv_sem=second_recv.at[e],
            device_id=col_peer(e),
            device_id_type=MESH,
        ).wait_recv()
        return carry

    def add(source, total):
        return total + parts_buf[lax.rem(col + cols - source, cols)]

    lax.fori_loop(1, cols, greet, 0)
    pl.semaphore_wait(barrier, cols - 1)
    lax.fori_loop(1, cols, start_first, 0)
    parts_buf[0] = x_ref[:, window(col)]
    lax.fori_loop(1, cols, finish_first, 0)
    full[:, window(col)] = lax.fori_loop(1, cols, add, parts_buf[col])
    lax.fori_loop(1, cols, start_second, 0)
    lax.fori_loop(1, cols, finish_second, 0)
    o_ref[...] = full[...]


def col_reduce(partial_sum, collective_id):
    cols = lax.axis_size("col")
    parts, fields, elements = partial_sum.shape
    width = elements // cols
    flat = partial_sum.reshape(parts * fields, elements)
    summed = pl.pallas_call(
        partial(reduce_kernel, cols),
        out_shape=jax.ShapeDtypeStruct(flat.shape, jnp.float32),
        in_specs=[pl.BlockSpec(memory_space=pltpu.VMEM)],
        out_specs=pl.BlockSpec(memory_space=pltpu.VMEM),
        scratch_shapes=[
            pltpu.VMEM((cols, parts * fields, width), jnp.float32),
            pltpu.VMEM((parts * fields, elements), jnp.float32),
            pltpu.SemaphoreType.DMA((cols,)),
            pltpu.SemaphoreType.DMA((cols,)),
            pltpu.SemaphoreType.DMA((cols,)),
            pltpu.SemaphoreType.DMA((cols,)),
        ],
        compiler_params=pltpu.CompilerParams(collective_id=collective_id, has_side_effects=True),
    )(flat)
    return summed.reshape(partial_sum.shape)


def row_psum(ids, *arrays):
    if len(arrays) == 1 and arrays[0].ndim == 2 and arrays[0].shape[1] <= 128:
        matrix = arrays[0]
        rows, columns = matrix.shape
        padded = jnp.pad(matrix, ((0, -rows % 8), (0, 128 - columns)))
        summed = row_allreduce(padded, len(ids))
        ids.append(None)
        return summed[:rows, :columns]
    flat = [a.reshape(-1) for a in arrays]
    sizes = [f.shape[0] for f in flat]
    total = sum(sizes)
    padded = -(-total // 1024) * 1024
    packed = jnp.concatenate(flat + [jnp.zeros((padded - total,), jnp.float32)]).reshape(-1, 128)
    summed = row_allreduce(packed, len(ids)).reshape(-1)
    ids.append(None)
    outs = []
    start = 0
    for a, size in zip(arrays, sizes):
        outs.append(summed[start : start + size].reshape(a.shape))
        start += size
    return outs[0] if len(outs) == 1 else tuple(outs)


def complex_lhs(values, part_axis):
    real = jnp.take(values, 0, axis=part_axis)
    imag = jnp.take(values, 1, axis=part_axis)
    return jnp.stack([jnp.stack([real, -imag]), jnp.stack([imag, real])])


def inner_products(first, second):
    return jnp.einsum("csn,ctn->st", first, second, precision=highest)


def combine_rows(matrix, vectors):
    return jnp.einsum("st,ctn->csn", matrix, vectors, precision=highest)


def matmul(left, right):
    return jnp.dot(left, right, precision=highest)


def lower_inverse(lower):
    identity = jnp.eye(lower.shape[0], dtype=lower.dtype)
    return lax.linalg.triangular_solve(lower, identity, left_side=True, lower=True)


def project(harmonics, vectors):

    def contract(left, right):
        return jnp.einsum("mn,sn->ms", left, right, precision=highest)

    real_out = contract(harmonics[0], vectors[0]) + contract(harmonics[1], vectors[1])
    imag_out = contract(harmonics[0], vectors[1]) - contract(harmonics[1], vectors[0])
    return jnp.stack([real_out, imag_out])


def body(incident, diagonal, near_blocks, left_factors, right_factors, flags, ranks, harmonics):
    blocks = left_factors.shape[1]
    slots = near_blocks.shape[1]
    width = near_blocks.shape[4]
    half_band = slots // 2
    elements = incident.shape[2]
    fields = incident.shape[1]
    clusters = lax.axis_size("row")
    row_index = lax.axis_index("row")
    column = lax.axis_index("col")
    ids = []

    def operator_terms(near_pieces, far_pieces):
        near_on = flags[0] == 1
        near_vector = jnp.where(near_on[:, None, None, None], near_pieces, 0).astype(jnp.bfloat16)
        near_out = jnp.einsum(
            "caksf,kaef->cse",
            complex_lhs(near_vector, 1),
            near_blocks[0],
            preferred_element_type=jnp.float32,
        )
        cluster = column * blocks + jnp.arange(blocks, dtype=jnp.int32)
        offset = (cluster - row_index + half_band) % clusters
        is_near = (offset < slots) & (flags[0, jnp.minimum(offset, slots - 1)] == 1)
        keep = (~is_near)[:, None] & (
            jnp.arange(right_factors.shape[3], dtype=jnp.int32)[None, :] < ranks[0][:, None]
        )
        products = jnp.einsum(
            "nxf,nbrf->nxbr", far_pieces, right_factors[0], preferred_element_type=jnp.float32
        )
        coeffs = jnp.stack(
            [
                products[:, :fields, 0] - products[:, fields:, 1],
                products[:, :fields, 1] + products[:, fields:, 0],
            ]
        )
        coeffs = jnp.where(keep[None, :, None, :], coeffs, 0.0).astype(jnp.bfloat16)
        far_out = jnp.einsum(
            "cansr,nare->cse",
            complex_lhs(coeffs, 0),
            left_factors[0],
            preferred_element_type=jnp.float32,
        )
        return near_out + far_out

    def apply_operator(vector, basis_one):
        rounded = vector.astype(jnp.bfloat16)
        near_pieces, far_pieces, cross, self_gram, proj = gather_pieces(
            rounded, basis_one, vector, jnp.transpose(harmonics, (1, 0, 2)), blocks, half_band, width, 16 + len(ids)
        )
        ids.append(None)
        total = operator_terms(near_pieces, far_pieces)
        summed = col_reduce(total, 32 + len(ids))
        ids.append(None)
        return summed + diagonal[None, None, :] * vector, cross, self_gram, proj

    lower_first = jnp.linalg.cholesky(row_psum(ids, inner_products(incident, incident)))
    basis_one = combine_rows(lower_inverse(lower_first), incident)
    image, _, self_one, harmonics_one = apply_operator(basis_one, basis_one)
    coupling_one, harmonics_one, self_one = row_psum(
        ids, inner_products(image, basis_one), harmonics_one, self_one
    )
    rest = image - combine_rows(coupling_one, basis_one)
    gram_one = row_psum(ids, inner_products(rest, rest))
    lower_second = jnp.linalg.cholesky(gram_one)
    basis_two = combine_rows(lower_inverse(lower_second), rest)
    image, cross, self_two, harmonics_two = apply_operator(basis_two, basis_one)
    coupling_onetwo, coupling_two, image_gram, cross, self_two, harmonics_two = row_psum(
        ids,
        inner_products(image, basis_one),
        inner_products(image, basis_two),
        inner_products(image, image),
        cross,
        self_two,
        harmonics_two,
    )
    coupling = jnp.concatenate([coupling_onetwo, coupling_two], axis=1)
    basis_gram = jnp.concatenate(
        [
            jnp.concatenate([self_one, cross], axis=1),
            jnp.concatenate([cross.T, self_two], axis=1),
        ],
        axis=0,
    )
    gram_two = (
        image_gram
        - 2.0 * matmul(coupling, coupling.T)
        + matmul(coupling, matmul(basis_gram, coupling.T))
    )
    upper_left = matmul(coupling_one, coupling_one.T) + gram_one
    upper_right = matmul(coupling_one, coupling_onetwo.T) + matmul(lower_second, coupling_two.T)
    lower_right = (
        matmul(coupling_onetwo, coupling_onetwo.T) + matmul(coupling_two, coupling_two.T) + gram_two
    )
    normal = jnp.concatenate(
        [
            jnp.concatenate([upper_left, upper_right], axis=1),
            jnp.concatenate([upper_right.T, lower_right], axis=1),
        ],
        axis=0,
    )
    target = jnp.concatenate(
        [matmul(lower_first, coupling_one.T), matmul(lower_first, coupling_onetwo.T)], axis=1
    )
    factor_inverse = lower_inverse(jnp.linalg.cholesky(normal))
    weights = matmul(factor_inverse.T, matmul(factor_inverse, target.T)).T
    first_weights = weights[:, :fields]
    second_weights = weights[:, fields:]
    solution = combine_rows(first_weights, basis_one) + combine_rows(second_weights, basis_two)
    coefficients = jnp.einsum(
        "cmt,st->cms", harmonics_one, first_weights, precision=highest
    ) + jnp.einsum("cmt,st->cms", harmonics_two, second_weights, precision=highest)
    return (solution, coefficients)


def solution(mesh):
    in_specs = (
        P(None, None, "row"),
        P("row"),
        P("row", None, None, None, "col"),
        P("row", "col", None, None, None),
        P("row", "col", None, None, None),
        P("row", None),
        P("row", "col"),
        P(None, None, "row"),
    )
    out_specs = (P(None, None, "row"), P())
    return jax.shard_map(body, mesh=mesh, in_specs=in_specs, out_specs=out_specs, check_vma=False)
```

```python
from functools import partial

import jax
import jax.numpy as jnp
from jax import lax
from jax.experimental import pallas as pl
from jax.experimental.pallas import tpu as pltpu
from jax.sharding import PartitionSpec as P

highest = lax.Precision.HIGHEST
MESH = pl.DeviceIdType.MESH


def allreduce_kernel(inner, outer, x_ref, o_ref, buf, partial_buf,
                     first_send, first_recv, second_send, second_recv):
    me = lax.axis_index("row")
    col = lax.axis_index("col")
    high = me // inner
    low = me % inner
    barrier = pltpu.get_barrier_semaphore()

    def inner_peer(d):
        return (high * inner + lax.rem(low + d, inner), col)

    def outer_peer(d):
        return (lax.rem(high + d, outer) * inner + low, col)

    def first(d):
        return pltpu.make_async_remote_copy(
            src_ref=x_ref,
            dst_ref=buf.at[d],
            send_sem=first_send.at[d],
            recv_sem=first_recv.at[d],
            device_id=inner_peer(d),
            device_id_type=MESH,
        )

    def second(d):
        return pltpu.make_async_remote_copy(
            src_ref=partial_buf.at[0],
            dst_ref=partial_buf.at[d],
            send_sem=second_send.at[d],
            recv_sem=second_recv.at[d],
            device_id=outer_peer(d),
            device_id_type=MESH,
        )

    def greet_inner(d, carry):
        pl.semaphore_signal(barrier, inc=1, device_id=inner_peer(d), device_id_type=MESH)
        return carry

    def greet_outer(d, carry):
        pl.semaphore_signal(barrier, inc=1, device_id=outer_peer(d), device_id_type=MESH)
        return carry

    def start_first(d, carry):
        first(d).start()
        return carry

    def finish_first(d, carry):
        first(d).wait()
        return carry

    def start_second(d, carry):
        second(d).start()
        return carry

    def finish_second(d, carry):
        second(d).wait()
        return carry

    def add_inner(source, total):
        return total + buf[lax.rem(low + inner - source, inner)]

    def add_outer(source, total):
        return total + partial_buf[lax.rem(high + outer - source, outer)]

    lax.fori_loop(1, inner, greet_inner, 0)
    lax.fori_loop(1, outer, greet_outer, 0)
    pl.semaphore_wait(barrier, inner - 1 + outer - 1)
    lax.fori_loop(1, inner, start_first, 0)
    buf[0] = x_ref[...]
    lax.fori_loop(1, inner, finish_first, 0)
    partial_buf[0] = lax.fori_loop(1, inner, add_inner, buf[low])
    lax.fori_loop(1, outer, start_second, 0)
    lax.fori_loop(1, outer, finish_second, 0)
    o_ref[...] = lax.fori_loop(1, outer, add_outer, partial_buf[high])


def row_allreduce(packed, collective_id):
    n = lax.axis_size("row")
    inner = 8 if n % 8 == 0 else n
    outer = n // inner
    rows, lanes = packed.shape
    return pl.pallas_call(
        partial(allreduce_kernel, inner, outer),
        out_shape=jax.ShapeDtypeStruct((rows, lanes), jnp.float32),
        in_specs=[pl.BlockSpec(memory_space=pltpu.VMEM)],
        out_specs=pl.BlockSpec(memory_space=pltpu.VMEM),
        scratch_shapes=[
            pltpu.VMEM((inner, rows, lanes), jnp.float32),
            pltpu.VMEM((outer, rows, lanes), jnp.float32),
            pltpu.SemaphoreType.DMA((inner,)),
            pltpu.SemaphoreType.DMA((inner,)),
            pltpu.SemaphoreType.DMA((outer,)),
            pltpu.SemaphoreType.DMA((outer,)),
        ],
        compiler_params=pltpu.CompilerParams(collective_id=collective_id, has_side_effects=True),
    )(packed)


def gram(left, right):
    return lax.dot_general(
        left, right, (((1,), (1,)), ((), ())), precision=highest, preferred_element_type=jnp.float32
    )


def gather_kernel(rows, cols, blocks, half, v_ref, one_ref, cur_ref, harm_ref,
                  near_ref, far_ref, cross_ref, self_ref, proj_ref, slices, far_buf,
                  first_send, first_recv, second_send, second_recv, local_sems):
    me = lax.axis_index("row")
    col = lax.axis_index("col")
    width = slices.shape[-1]
    barrier = pltpu.get_barrier_semaphore()

    def row_peer(d):
        return (lax.rem(me + d, rows), col)

    def col_peer(e):
        return (me, lax.rem(col + e, cols))

    def window(c):
        return pl.ds(pl.multiple_of(c * width, width), width)

    own = v_ref.at[:, window(col)]

    def first(d):
        return pltpu.make_async_remote_copy(
            src_ref=own,
            dst_ref=slices.at[d],
            send_sem=first_send.at[d],
            recv_sem=first_recv.at[d],
            device_id=row_peer(d),
            device_id_type=MESH,
        )

    def second(t):
        e = 1 + t // blocks
        n = t % blocks
        target = lax.rem(col + e, cols)
        slot = lax.rem(me + rows - blocks * target - n, rows)
        return pltpu.make_async_remote_copy(
            src_ref=slices.at[slot],
            dst_ref=far_buf.at[n, :, window(col)],
            send_sem=second_send.at[t],
            recv_sem=second_recv.at[t],
            device_id=col_peer(e),
            device_id_type=MESH,
        )

    def greet_row(d, carry):
        pl.semaphore_signal(barrier, inc=1, device_id=row_peer(d), device_id_type=MESH)
        return carry

    def greet_col(e, carry):
        pl.semaphore_signal(barrier, inc=1, device_id=col_peer(e), device_id_type=MESH)
        return carry

    def start_first(d, carry):
        first(d).start()
        return carry

    def finish_second(t, carry):
        second(t).wait()
        return carry

    def arrived(slot):
        pltpu.make_async_remote_copy(
            src_ref=own,
            dst_ref=slices.at[slot],
            send_sem=first_send.at[slot],
            recv_sem=first_recv.at[slot],
            device_id=row_peer(slot),
            device_id_type=MESH,
        ).wait_recv()

    def forward(t, carry):
        target = lax.rem(col + 1 + t // blocks, cols)
        arrived(lax.rem(me + rows - blocks * target - t % blocks, rows))
        second(t).start()
        return carry

    def sent_first(d, carry):
        first(d).wait_send()
        return carry

    lax.fori_loop(1, rows, greet_row, 0)
    lax.fori_loop(1, cols, greet_col, 0)
    pl.semaphore_wait(barrier, rows - 1 + cols - 1)
    lax.fori_loop(1, rows, start_first, 0)
    pltpu.make_async_copy(own, slices.at[0], first_recv.at[0]).start()
    cross_ref[...] = gram(one_ref[0], cur_ref[0]) + gram(one_ref[1], cur_ref[1])
    self_ref[...] = gram(cur_ref[0], cur_ref[0]) + gram(cur_ref[1], cur_ref[1])
    harm_real = harm_ref[:, 0, :]
    harm_imag = harm_ref[:, 1, :]
    proj_ref[0] = gram(harm_real, cur_ref[0]) + gram(harm_imag, cur_ref[1])
    proj_ref[1] = gram(harm_real, cur_ref[1]) - gram(harm_imag, cur_ref[0])
    lax.fori_loop(0, (cols - 1) * blocks, forward, 0)
    mine = []
    for n in range(blocks):
        slot = lax.rem(me + rows - blocks * col - n, rows)
        arrived(slot)
        copy = pltpu.make_async_copy(slices.at[slot], far_buf.at[n, :, window(col)], local_sems.at[n])
        copy.start()
        mine.append(copy)
    lax.fori_loop(1, rows, sent_first, 0)
    for k in range(2 * half):
        near_ref[k] = slices[(half - k) % rows]
    lax.fori_loop(0, (cols - 1) * blocks, finish_second, 0)
    for copy in mine:
        copy.wait()
    far_ref[...] = far_buf[...]


def gather_pieces(vector, basis_one, basis, harmonics, blocks, half, width, collective_id):
    rows = lax.axis_size("row")
    cols = lax.axis_size("col")
    parts, fields, elements = vector.shape
    flat = vector.reshape(parts * fields, elements)
    near, far, cross, self_gram, proj = pl.pallas_call(
        partial(gather_kernel, rows, cols, blocks, half),
        out_shape=(
            jax.ShapeDtypeStruct((2 * half, parts * fields, width), vector.dtype),
            jax.ShapeDtypeStruct((blocks, parts * fields, elements), vector.dtype),
            jax.ShapeDtypeStruct((fields, fields), jnp.float32),
            jax.ShapeDtypeStruct((fields, fields), jnp.float32),
            jax.ShapeDtypeStruct((2, harmonics.shape[0], fields), jnp.float32),
        ),
        in_specs=[pl.BlockSpec(memory_space=pltpu.VMEM)] * 4,
        out_specs=tuple(pl.BlockSpec(memory_space=pltpu.VMEM) for _ in range(5)),
        scratch_shapes=[
            pltpu.VMEM((rows, parts * fields, width), vector.dtype),
            pltpu.VMEM((blocks, parts * fields, elements), vector.dtype),
            pltpu.SemaphoreType.DMA((rows,)),
            pltpu.SemaphoreType.DMA((rows,)),
            pltpu.SemaphoreType.DMA(((cols - 1) * blocks,)),
            pltpu.SemaphoreType.DMA(((cols - 1) * blocks,)),
            pltpu.SemaphoreType.DMA((blocks + 1,)),
        ],
        compiler_params=pltpu.CompilerParams(collective_id=collective_id, has_side_effects=True),
    )(flat, basis_one, basis, harmonics)
    return (
        near.reshape(2 * half, parts, fields, width),
        far,
        cross,
        self_gram,
        proj,
    )


def reduce_kernel(cols, x_ref, o_ref, parts_buf, full, first_send, first_recv, second_send, second_recv):
    me = lax.axis_index("row")
    col = lax.axis_index("col")
    width = parts_buf.shape[-1]
    barrier = pltpu.get_barrier_semaphore()

    def col_peer(e):
        return (me, lax.rem(col + e, cols))

    def window(c):
        return pl.ds(pl.multiple_of(c * width, width), width)

    def first(e):
        return pltpu.make_async_remote_copy(
            src_ref=x_ref.at[:, window(lax.rem(col + e, cols))],
            dst_ref=parts_buf.at[e],
            send_sem=first_send.at[e],
            recv_sem=first_recv.at[e],
            device_id=col_peer(e),
            device_id_type=MESH,
        )

    def second(e):
        return pltpu.make_async_remote_copy(
            src_ref=full.at[:, window(col)],
            dst_ref=full.at[:, window(col)],
            send_sem=second_send.at[e],
            recv_sem=second_recv.at[e],
            device_id=col_peer(e),
            device_id_type=MESH,
        )

    def greet(e, carry):
        pl.semaphore_signal(barrier, inc=1, device_id=col_peer(e), device_id_type=MESH)
        return carry

    def start_first(e, carry):
        first(e).start()
        return carry

    def finish_first(e, carry):
        first(e).wait()
        return carry

    def start_second(e, carry):
        second(e).start()
        return carry

    def finish_second(e, carry):
        second(e).wait_send()
        pltpu.make_async_remote_copy(
            src_ref=full.at[:, window(col)],
            dst_ref=full.at[:, window(lax.rem(col + cols - e, cols))],
            send_sem=second_send.at[e],
            recv_sem=second_recv.at[e],
            device_id=col_peer(e),
            device_id_type=MESH,
        ).wait_recv()
        return carry

    def add(source, total):
        return total + parts_buf[lax.rem(col + cols - source, cols)]

    lax.fori_loop(1, cols, greet, 0)
    pl.semaphore_wait(barrier, cols - 1)
    lax.fori_loop(1, cols, start_first, 0)
    parts_buf[0] = x_ref[:, window(col)]
    lax.fori_loop(1, cols, finish_first, 0)
    full[:, window(col)] = lax.fori_loop(1, cols, add, parts_buf[col])
    lax.fori_loop(1, cols, start_second, 0)
    lax.fori_loop(1, cols, finish_second, 0)
    o_ref[...] = full[...]


def col_reduce(partial_sum, collective_id):
    cols = lax.axis_size("col")
    parts, fields, elements = partial_sum.shape
    width = elements // cols
    flat = partial_sum.reshape(parts * fields, elements)
    summed = pl.pallas_call(
        partial(reduce_kernel, cols),
        out_shape=jax.ShapeDtypeStruct(flat.shape, jnp.float32),
        in_specs=[pl.BlockSpec(memory_space=pltpu.VMEM)],
        out_specs=pl.BlockSpec(memory_space=pltpu.VMEM),
        scratch_shapes=[
            pltpu.VMEM((cols, parts * fields, width), jnp.float32),
            pltpu.VMEM((parts * fields, elements), jnp.float32),
            pltpu.SemaphoreType.DMA((cols,)),
            pltpu.SemaphoreType.DMA((cols,)),
            pltpu.SemaphoreType.DMA((cols,)),
            pltpu.SemaphoreType.DMA((cols,)),
        ],
        compiler_params=pltpu.CompilerParams(collective_id=collective_id, has_side_effects=True),
    )(flat)
    return summed.reshape(partial_sum.shape)


def row_psum(ids, *arrays):
    flat = [a.reshape(-1) for a in arrays]
    sizes = [f.shape[0] for f in flat]
    total = sum(sizes)
    padded = -(-total // 1024) * 1024
    packed = jnp.concatenate(flat + [jnp.zeros((padded - total,), jnp.float32)]).reshape(-1, 128)
    summed = row_allreduce(packed, len(ids)).reshape(-1)
    ids.append(None)
    outs = []
    start = 0
    for a, size in zip(arrays, sizes):
        outs.append(summed[start : start + size].reshape(a.shape))
        start += size
    return outs[0] if len(outs) == 1 else tuple(outs)


def complex_lhs(values, part_axis):
    real = jnp.take(values, 0, axis=part_axis)
    imag = jnp.take(values, 1, axis=part_axis)
    return jnp.stack([jnp.stack([real, -imag]), jnp.stack([imag, real])])


def inner_products(first, second):
    return jnp.einsum("csn,ctn->st", first, second, precision=highest)


def combine_rows(matrix, vectors):
    return jnp.einsum("st,ctn->csn", matrix, vectors, precision=highest)


def matmul(left, right):
    return jnp.dot(left, right, precision=highest)


def lower_inverse(lower):
    identity = jnp.eye(lower.shape[0], dtype=lower.dtype)
    return lax.linalg.triangular_solve(lower, identity, left_side=True, lower=True)


def project(harmonics, vectors):

    def contract(left, right):
        return jnp.einsum("mn,sn->ms", left, right, precision=highest)

    real_out = contract(harmonics[0], vectors[0]) + contract(harmonics[1], vectors[1])
    imag_out = contract(harmonics[0], vectors[1]) - contract(harmonics[1], vectors[0])
    return jnp.stack([real_out, imag_out])


def body(incident, diagonal, near_blocks, left_factors, right_factors, flags, ranks, harmonics):
    blocks = left_factors.shape[1]
    slots = near_blocks.shape[1]
    width = near_blocks.shape[4]
    half_band = slots // 2
    elements = incident.shape[2]
    fields = incident.shape[1]
    clusters = lax.axis_size("row")
    row_index = lax.axis_index("row")
    column = lax.axis_index("col")
    ids = []

    def operator_terms(near_pieces, far_pieces):
        near_on = flags[0] == 1
        near_vector = jnp.where(near_on[:, None, None, None], near_pieces, 0).astype(jnp.bfloat16)
        near_out = jnp.einsum(
            "caksf,kaef->cse",
            complex_lhs(near_vector, 1),
            near_blocks[0],
            preferred_element_type=jnp.float32,
        )
        cluster = column * blocks + jnp.arange(blocks, dtype=jnp.int32)
        offset = (cluster - row_index + half_band) % clusters
        is_near = (offset < slots) & (flags[0, jnp.minimum(offset, slots - 1)] == 1)
        keep = (~is_near)[:, None] & (
            jnp.arange(right_factors.shape[3], dtype=jnp.int32)[None, :] < ranks[0][:, None]
        )
        products = jnp.einsum(
            "nxf,nbrf->nxbr", far_pieces, right_factors[0], preferred_element_type=jnp.float32
        )
        coeffs = jnp.stack(
            [
                products[:, :fields, 0] - products[:, fields:, 1],
                products[:, :fields, 1] + products[:, fields:, 0],
            ]
        )
        coeffs = jnp.where(keep[None, :, None, :], coeffs, 0.0).astype(jnp.bfloat16)
        far_out = jnp.einsum(
            "cansr,nare->cse",
            complex_lhs(coeffs, 0),
            left_factors[0],
            preferred_element_type=jnp.float32,
        )
        return near_out + far_out

    def apply_operator(vector, basis_one):
        rounded = vector.astype(jnp.bfloat16)
        near_pieces, far_pieces, cross, self_gram, proj = gather_pieces(
            rounded, basis_one, vector, jnp.transpose(harmonics, (1, 0, 2)), blocks, half_band, width, 16 + len(ids)
        )
        ids.append(None)
        total = operator_terms(near_pieces, far_pieces)
        summed = col_reduce(total, 32 + len(ids))
        ids.append(None)
        return summed + diagonal[None, None, :] * vector, cross, self_gram, proj

    lower_first = lax.linalg.cholesky(row_psum(ids, inner_products(incident, incident)), symmetrize_input=False)
    basis_one = combine_rows(lower_inverse(lower_first), incident)
    image, _, self_one, harmonics_one = apply_operator(basis_one, basis_one)
    coupling_one, harmonics_one, self_one = row_psum(
        ids, inner_products(image, basis_one), harmonics_one, self_one
    )
    rest = image - combine_rows(coupling_one, basis_one)
    gram_one = row_psum(ids, inner_products(rest, rest))
    lower_second = lax.linalg.cholesky(gram_one, symmetrize_input=False)
    basis_two = combine_rows(lower_inverse(lower_second), rest)
    image, cross, self_two, harmonics_two = apply_operator(basis_two, basis_one)
    coupling_onetwo, coupling_two, image_gram, cross, self_two, harmonics_two = row_psum(
        ids,
        inner_products(image, basis_one),
        inner_products(image, basis_two),
        inner_products(image, image),
        cross,
        self_two,
        harmonics_two,
    )
    coupling = jnp.concatenate([coupling_onetwo, coupling_two], axis=1)
    basis_gram = jnp.concatenate(
        [
            jnp.concatenate([self_one, cross], axis=1),
            jnp.concatenate([cross.T, self_two], axis=1),
        ],
        axis=0,
    )
    gram_two = (
        image_gram
        - 2.0 * matmul(coupling, coupling.T)
        + matmul(coupling, matmul(basis_gram, coupling.T))
    )
    upper_left = matmul(coupling_one, coupling_one.T) + gram_one
    upper_right = matmul(coupling_one, coupling_onetwo.T) + matmul(lower_second, coupling_two.T)
    lower_right = (
        matmul(coupling_onetwo, coupling_onetwo.T) + matmul(coupling_two, coupling_two.T) + gram_two
    )
    normal = jnp.concatenate(
        [
            jnp.concatenate([upper_left, upper_right], axis=1),
            jnp.concatenate([upper_right.T, lower_right], axis=1),
        ],
        axis=0,
    )
    target = jnp.concatenate(
        [matmul(lower_first, coupling_one.T), matmul(lower_first, coupling_onetwo.T)], axis=1
    )
    factor_inverse = lower_inverse(lax.linalg.cholesky(normal, symmetrize_input=False))
    weights = matmul(factor_inverse.T, matmul(factor_inverse, target.T)).T
    first_weights = weights[:, :fields]
    second_weights = weights[:, fields:]
    solution = combine_rows(first_weights, basis_one) + combine_rows(second_weights, basis_two)
    coefficients = jnp.einsum(
        "cmt,st->cms", harmonics_one, first_weights, precision=highest
    ) + jnp.einsum("cmt,st->cms", harmonics_two, second_weights, precision=highest)
    return (solution, coefficients)


def solution(mesh):
    in_specs = (
        P(None, None, "row"),
        P("row"),
        P("row", None, None, None, "col"),
        P("row", "col", None, None, None),
        P("row", "col", None, None, None),
        P("row", None),
        P("row", "col"),
        P(None, None, "row"),
    )
    out_specs = (P(None, None, "row"), P())
    return jax.shard_map(body, mesh=mesh, in_specs=in_specs, out_specs=out_specs, check_vma=False)
```

```python
from functools import partial

import jax
import jax.numpy as jnp
from jax import lax
from jax.experimental import pallas as pl
from jax.experimental.pallas import tpu as pltpu
from jax.sharding import PartitionSpec as P

highest = lax.Precision.HIGHEST
MESH = pl.DeviceIdType.MESH


def allreduce_kernel(inner, outer, x_ref, o_ref, buf, partial_buf,
                     first_send, first_recv, second_send, second_recv):
    me = lax.axis_index("row")
    col = lax.axis_index("col")
    high = me // inner
    low = me % inner
    barrier = pltpu.get_barrier_semaphore()

    def inner_peer(d):
        return (high * inner + lax.rem(low + d, inner), col)

    def outer_peer(d):
        return (lax.rem(high + d, outer) * inner + low, col)

    def first(d):
        return pltpu.make_async_remote_copy(
            src_ref=x_ref,
            dst_ref=buf.at[d],
            send_sem=first_send.at[d],
            recv_sem=first_recv.at[d],
            device_id=inner_peer(d),
            device_id_type=MESH,
        )

    def second(d):
        return pltpu.make_async_remote_copy(
            src_ref=partial_buf.at[0],
            dst_ref=partial_buf.at[d],
            send_sem=second_send.at[d],
            recv_sem=second_recv.at[d],
            device_id=outer_peer(d),
            device_id_type=MESH,
        )

    def greet_inner(d, carry):
        pl.semaphore_signal(barrier, inc=1, device_id=inner_peer(d), device_id_type=MESH)
        return carry

    def greet_outer(d, carry):
        pl.semaphore_signal(barrier, inc=1, device_id=outer_peer(d), device_id_type=MESH)
        return carry

    def start_first(d, carry):
        first(d).start()
        return carry

    def finish_first(d, carry):
        first(d).wait()
        return carry

    def start_second(d, carry):
        second(d).start()
        return carry

    def finish_second(d, carry):
        second(d).wait()
        return carry

    def add_inner(source, total):
        return total + buf[lax.rem(low + inner - source, inner)]

    def add_outer(source, total):
        return total + partial_buf[lax.rem(high + outer - source, outer)]

    lax.fori_loop(1, inner, greet_inner, 0)
    lax.fori_loop(1, outer, greet_outer, 0)
    pl.semaphore_wait(barrier, inner - 1 + outer - 1)
    lax.fori_loop(1, inner, start_first, 0)
    buf[0] = x_ref[...]
    lax.fori_loop(1, inner, finish_first, 0)
    partial_buf[0] = lax.fori_loop(1, inner, add_inner, buf[low])
    lax.fori_loop(1, outer, start_second, 0)
    lax.fori_loop(1, outer, finish_second, 0)
    o_ref[...] = lax.fori_loop(1, outer, add_outer, partial_buf[high])


def row_allreduce(packed, collective_id):
    n = lax.axis_size("row")
    inner = 8 if n % 8 == 0 else n
    outer = n // inner
    rows, lanes = packed.shape
    return pl.pallas_call(
        partial(allreduce_kernel, inner, outer),
        out_shape=jax.ShapeDtypeStruct((rows, lanes), jnp.float32),
        in_specs=[pl.BlockSpec(memory_space=pltpu.VMEM)],
        out_specs=pl.BlockSpec(memory_space=pltpu.VMEM),
        scratch_shapes=[
            pltpu.VMEM((inner, rows, lanes), jnp.float32),
            pltpu.VMEM((outer, rows, lanes), jnp.float32),
            pltpu.SemaphoreType.DMA((inner,)),
            pltpu.SemaphoreType.DMA((inner,)),
            pltpu.SemaphoreType.DMA((outer,)),
            pltpu.SemaphoreType.DMA((outer,)),
        ],
        compiler_params=pltpu.CompilerParams(collective_id=collective_id, has_side_effects=True),
    )(packed)


def gram(left, right):
    return lax.dot_general(
        left, right, (((1,), (1,)), ((), ())), precision=highest, preferred_element_type=jnp.float32
    )


def gather_kernel(rows, cols, blocks, half, v_ref, one_ref, cur_ref, harm_ref,
                  near_ref, far_ref, cross_ref, self_ref, proj_ref, slices, far_buf,
                  first_send, first_recv, second_send, second_recv, local_sems):
    me = lax.axis_index("row")
    col = lax.axis_index("col")
    width = slices.shape[-1]
    barrier = pltpu.get_barrier_semaphore()

    def row_peer(d):
        return (lax.rem(me + d, rows), col)

    def col_peer(e):
        return (me, lax.rem(col + e, cols))

    def window(c):
        return pl.ds(pl.multiple_of(c * width, width), width)

    own = v_ref.at[:, window(col)]

    def first(d):
        return pltpu.make_async_remote_copy(
            src_ref=own,
            dst_ref=slices.at[d],
            send_sem=first_send.at[d],
            recv_sem=first_recv.at[d],
            device_id=row_peer(d),
            device_id_type=MESH,
        )

    def second(t):
        e = 1 + t // blocks
        n = t % blocks
        target = lax.rem(col + e, cols)
        slot = lax.rem(me + rows - blocks * target - n, rows)
        return pltpu.make_async_remote_copy(
            src_ref=slices.at[slot],
            dst_ref=far_buf.at[n, :, window(col)],
            send_sem=second_send.at[t],
            recv_sem=second_recv.at[t],
            device_id=col_peer(e),
            device_id_type=MESH,
        )

    def greet_row(d, carry):
        pl.semaphore_signal(barrier, inc=1, device_id=row_peer(d), device_id_type=MESH)
        return carry

    def greet_col(e, carry):
        pl.semaphore_signal(barrier, inc=1, device_id=col_peer(e), device_id_type=MESH)
        return carry

    def start_first(d, carry):
        first(d).start()
        return carry

    def finish_second(t, carry):
        second(t).wait()
        return carry

    def arrived(slot):
        pltpu.make_async_remote_copy(
            src_ref=own,
            dst_ref=slices.at[slot],
            send_sem=first_send.at[slot],
            recv_sem=first_recv.at[slot],
            device_id=row_peer(slot),
            device_id_type=MESH,
        ).wait_recv()

    def forward(t, carry):
        target = lax.rem(col + 1 + t // blocks, cols)
        arrived(lax.rem(me + rows - blocks * target - t % blocks, rows))
        second(t).start()
        return carry

    def sent_first(d, carry):
        first(d).wait_send()
        return carry

    lax.fori_loop(1, rows, greet_row, 0)
    lax.fori_loop(1, cols, greet_col, 0)
    pl.semaphore_wait(barrier, rows - 1 + cols - 1)
    lax.fori_loop(1, rows, start_first, 0)
    pltpu.make_async_copy(own, slices.at[0], first_recv.at[0]).start()
    cross_ref[...] = gram(one_ref[0], cur_ref[0]) + gram(one_ref[1], cur_ref[1])
    self_ref[...] = gram(cur_ref[0], cur_ref[0]) + gram(cur_ref[1], cur_ref[1])
    harm_real = harm_ref[:, 0, :]
    harm_imag = harm_ref[:, 1, :]
    proj_ref[0] = gram(harm_real, cur_ref[0]) + gram(harm_imag, cur_ref[1])
    proj_ref[1] = gram(harm_real, cur_ref[1]) - gram(harm_imag, cur_ref[0])
    lax.fori_loop(0, (cols - 1) * blocks, forward, 0)
    mine = []
    for n in range(blocks):
        slot = lax.rem(me + rows - blocks * col - n, rows)
        arrived(slot)
        copy = pltpu.make_async_copy(slices.at[slot], far_buf.at[n, :, window(col)], local_sems.at[n])
        copy.start()
        mine.append(copy)
    lax.fori_loop(1, rows, sent_first, 0)
    for k in range(2 * half):
        near_ref[k] = slices[(half - k) % rows]
    lax.fori_loop(0, (cols - 1) * blocks, finish_second, 0)
    for copy in mine:
        copy.wait()
    far_ref[...] = far_buf[...]


def gather_pieces(vector, basis_one, basis, harmonics, blocks, half, width, collective_id):
    rows = lax.axis_size("row")
    cols = lax.axis_size("col")
    parts, fields, elements = vector.shape
    flat = vector.reshape(parts * fields, elements)
    near, far, cross, self_gram, proj = pl.pallas_call(
        partial(gather_kernel, rows, cols, blocks, half),
        out_shape=(
            jax.ShapeDtypeStruct((2 * half, parts * fields, width), vector.dtype),
            jax.ShapeDtypeStruct((blocks, parts * fields, elements), vector.dtype),
            jax.ShapeDtypeStruct((fields, fields), jnp.float32),
            jax.ShapeDtypeStruct((fields, fields), jnp.float32),
            jax.ShapeDtypeStruct((2, harmonics.shape[0], fields), jnp.float32),
        ),
        in_specs=[pl.BlockSpec(memory_space=pltpu.VMEM)] * 4,
        out_specs=tuple(pl.BlockSpec(memory_space=pltpu.VMEM) for _ in range(5)),
        scratch_shapes=[
            pltpu.VMEM((rows, parts * fields, width), vector.dtype),
            pltpu.VMEM((blocks, parts * fields, elements), vector.dtype),
            pltpu.SemaphoreType.DMA((rows,)),
            pltpu.SemaphoreType.DMA((rows,)),
            pltpu.SemaphoreType.DMA(((cols - 1) * blocks,)),
            pltpu.SemaphoreType.DMA(((cols - 1) * blocks,)),
            pltpu.SemaphoreType.DMA((blocks + 1,)),
        ],
        compiler_params=pltpu.CompilerParams(collective_id=collective_id, has_side_effects=True),
    )(flat, basis_one, basis, harmonics)
    return (
        near.reshape(2 * half, parts, fields, width),
        far,
        cross,
        self_gram,
        proj,
    )


def reduce_kernel(cols, x_ref, o_ref, parts_buf, full, first_send, first_recv, second_send, second_recv):
    me = lax.axis_index("row")
    col = lax.axis_index("col")
    width = parts_buf.shape[-1]
    barrier = pltpu.get_barrier_semaphore()

    def col_peer(e):
        return (me, lax.rem(col + e, cols))

    def window(c):
        return pl.ds(pl.multiple_of(c * width, width), width)

    def first(e):
        return pltpu.make_async_remote_copy(
            src_ref=x_ref.at[:, window(lax.rem(col + e, cols))],
            dst_ref=parts_buf.at[e],
            send_sem=first_send.at[e],
            recv_sem=first_recv.at[e],
            device_id=col_peer(e),
            device_id_type=MESH,
        )

    def second(e):
        return pltpu.make_async_remote_copy(
            src_ref=full.at[:, window(col)],
            dst_ref=full.at[:, window(col)],
            send_sem=second_send.at[e],
            recv_sem=second_recv.at[e],
            device_id=col_peer(e),
            device_id_type=MESH,
        )

    def greet(e, carry):
        pl.semaphore_signal(barrier, inc=1, device_id=col_peer(e), device_id_type=MESH)
        return carry

    def start_first(e, carry):
        first(e).start()
        return carry

    def finish_first(e, carry):
        first(e).wait()
        return carry

    def start_second(e, carry):
        second(e).start()
        return carry

    def finish_second(e, carry):
        second(e).wait_send()
        pltpu.make_async_remote_copy(
            src_ref=full.at[:, window(col)],
            dst_ref=full.at[:, window(lax.rem(col + cols - e, cols))],
            send_sem=second_send.at[e],
            recv_sem=second_recv.at[e],
            device_id=col_peer(e),
            device_id_type=MESH,
        ).wait_recv()
        return carry

    def add(source, total):
        return total + parts_buf[lax.rem(col + cols - source, cols)]

    lax.fori_loop(1, cols, greet, 0)
    pl.semaphore_wait(barrier, cols - 1)
    lax.fori_loop(1, cols, start_first, 0)
    parts_buf[0] = x_ref[:, window(col)]
    lax.fori_loop(1, cols, finish_first, 0)
    full[:, window(col)] = lax.fori_loop(1, cols, add, parts_buf[col])
    lax.fori_loop(1, cols, start_second, 0)
    lax.fori_loop(1, cols, finish_second, 0)
    o_ref[...] = full[...]


def col_reduce(partial_sum, collective_id):
    cols = lax.axis_size("col")
    parts, fields, elements = partial_sum.shape
    width = elements // cols
    flat = partial_sum.reshape(parts * fields, elements)
    summed = pl.pallas_call(
        partial(reduce_kernel, cols),
        out_shape=jax.ShapeDtypeStruct(flat.shape, jnp.float32),
        in_specs=[pl.BlockSpec(memory_space=pltpu.VMEM)],
        out_specs=pl.BlockSpec(memory_space=pltpu.VMEM),
        scratch_shapes=[
            pltpu.VMEM((cols, parts * fields, width), jnp.float32),
            pltpu.VMEM((parts * fields, elements), jnp.float32),
            pltpu.SemaphoreType.DMA((cols,)),
            pltpu.SemaphoreType.DMA((cols,)),
            pltpu.SemaphoreType.DMA((cols,)),
            pltpu.SemaphoreType.DMA((cols,)),
        ],
        compiler_params=pltpu.CompilerParams(collective_id=collective_id, has_side_effects=True),
    )(flat)
    return summed.reshape(partial_sum.shape)


def row_psum(ids, *arrays):
    flat = [a.reshape(-1) for a in arrays]
    sizes = [f.shape[0] for f in flat]
    total = sum(sizes)
    padded = -(-total // 1024) * 1024
    packed = jnp.concatenate(flat + [jnp.zeros((padded - total,), jnp.float32)]).reshape(-1, 128)
    summed = row_allreduce(packed, len(ids)).reshape(-1)
    ids.append(None)
    outs = []
    start = 0
    for a, size in zip(arrays, sizes):
        outs.append(summed[start : start + size].reshape(a.shape))
        start += size
    return outs[0] if len(outs) == 1 else tuple(outs)


def complex_lhs(values, part_axis):
    real = jnp.take(values, 0, axis=part_axis)
    imag = jnp.take(values, 1, axis=part_axis)
    return jnp.stack([jnp.stack([real, -imag]), jnp.stack([imag, real])])


def inner_products(first, second):
    return jnp.einsum("csn,ctn->st", first, second, precision=highest)


def combine_rows(matrix, vectors):
    return jnp.einsum("st,ctn->csn", matrix, vectors, precision=highest)


def matmul(left, right):
    return jnp.dot(left, right, precision=highest)


def lower_inverse(lower):
    identity = jnp.eye(lower.shape[0], dtype=lower.dtype)
    return lax.linalg.triangular_solve(lower, identity, left_side=True, lower=True)


def project(harmonics, vectors):

    def contract(left, right):
        return jnp.einsum("mn,sn->ms", left, right, precision=highest)

    real_out = contract(harmonics[0], vectors[0]) + contract(harmonics[1], vectors[1])
    imag_out = contract(harmonics[0], vectors[1]) - contract(harmonics[1], vectors[0])
    return jnp.stack([real_out, imag_out])


def body(incident, diagonal, near_blocks, left_factors, right_factors, flags, ranks, harmonics):
    blocks = left_factors.shape[1]
    slots = near_blocks.shape[1]
    width = near_blocks.shape[4]
    half_band = slots // 2
    elements = incident.shape[2]
    fields = incident.shape[1]
    clusters = lax.axis_size("row")
    row_index = lax.axis_index("row")
    column = lax.axis_index("col")
    ids = []

    def operator_terms(near_pieces, far_pieces):
        near_on = flags[0] == 1
        near_vector = jnp.where(near_on[:, None, None, None], near_pieces, 0).astype(jnp.bfloat16)
        near_out = jnp.einsum(
            "caksf,kaef->cse",
            complex_lhs(near_vector, 1),
            near_blocks[0],
            preferred_element_type=jnp.float32,
        )
        cluster = column * blocks + jnp.arange(blocks, dtype=jnp.int32)
        offset = (cluster - row_index + half_band) % clusters
        is_near = (offset < slots) & (flags[0, jnp.minimum(offset, slots - 1)] == 1)
        keep = (~is_near)[:, None] & (
            jnp.arange(right_factors.shape[3], dtype=jnp.int32)[None, :] < ranks[0][:, None]
        )
        products = jnp.einsum(
            "nxf,nbrf->nxbr", far_pieces, right_factors[0], preferred_element_type=jnp.float32
        )
        coeffs = jnp.stack(
            [
                products[:, :fields, 0] - products[:, fields:, 1],
                products[:, :fields, 1] + products[:, fields:, 0],
            ]
        )
        coeffs = jnp.where(keep[None, :, None, :], coeffs, 0.0).astype(jnp.bfloat16)
        far_out = jnp.einsum(
            "cansr,nare->cse",
            complex_lhs(coeffs, 0),
            left_factors[0],
            preferred_element_type=jnp.float32,
        )
        return near_out + far_out

    def apply_operator(vector, basis_one):
        rounded = vector.astype(jnp.bfloat16)
        near_pieces, far_pieces, cross, self_gram, proj = gather_pieces(
            rounded, basis_one, vector, jnp.transpose(harmonics, (1, 0, 2)), blocks, half_band, width, 16 + len(ids)
        )
        ids.append(None)
        total = operator_terms(near_pieces, far_pieces)
        summed = col_reduce(total, 32 + len(ids))
        ids.append(None)
        return summed + diagonal[None, None, :] * vector, cross, self_gram, proj

    lower_first = lax.linalg.cholesky(row_psum(ids, inner_products(incident, incident)), symmetrize_input=False)
    basis_one = combine_rows(lower_inverse(lower_first), incident)
    image, _, self_one, harmonics_one = apply_operator(basis_one, basis_one)
    coupling_one, harmonics_one, self_one = row_psum(
        ids, inner_products(image, basis_one), harmonics_one, self_one
    )
    rest = image - combine_rows(coupling_one, basis_one)
    gram_one = row_psum(ids, inner_products(rest, rest))
    lower_second = lax.linalg.cholesky(gram_one, symmetrize_input=False)
    basis_two = combine_rows(lower_inverse(lower_second), rest)
    image, cross, self_two, harmonics_two = apply_operator(basis_two, basis_one)
    coupling_onetwo, coupling_two, image_gram, cross, self_two, harmonics_two = row_psum(
        ids,
        inner_products(image, basis_one),
        inner_products(image, basis_two),
        inner_products(image, image),
        cross,
        self_two,
        harmonics_two,
    )
    coupling = jnp.concatenate([coupling_onetwo, coupling_two], axis=1)
    basis_gram = jnp.concatenate(
        [
            jnp.concatenate([self_one, cross], axis=1),
            jnp.concatenate([cross.T, self_two], axis=1),
        ],
        axis=0,
    )
    gram_two = (
        image_gram
        - 2.0 * matmul(coupling, coupling.T)
        + matmul(coupling, matmul(basis_gram, coupling.T))
    )
    upper_left = matmul(coupling_one, coupling_one.T) + gram_one
    upper_right = matmul(coupling_one, coupling_onetwo.T) + matmul(lower_second, coupling_two.T)
    lower_right = (
        matmul(coupling_onetwo, coupling_onetwo.T) + matmul(coupling_two, coupling_two.T) + gram_two
    )
    normal = jnp.concatenate(
        [
            jnp.concatenate([upper_left, upper_right], axis=1),
            jnp.concatenate([upper_right.T, lower_right], axis=1),
        ],
        axis=0,
    )
    target = jnp.concatenate(
        [matmul(lower_first, coupling_one.T), matmul(lower_first, coupling_onetwo.T)], axis=1
    )
    factor_inverse = lower_inverse(lax.linalg.cholesky(normal, symmetrize_input=False))
    weights = matmul(factor_inverse.T, matmul(factor_inverse, target.T)).T
    first_weights = weights[:, :fields]
    second_weights = weights[:, fields:]
    solution = combine_rows(first_weights, basis_one) + combine_rows(second_weights, basis_two)
    coefficients = jnp.einsum(
        "cmt,st->cms",
        jnp.concatenate([harmonics_one, harmonics_two], axis=2),
        weights,
        precision=highest,
    )
    return (solution, coefficients)


def solution(mesh):
    in_specs = (
        P(None, None, "row"),
        P("row"),
        P("row", None, None, None, "col"),
        P("row", "col", None, None, None),
        P("row", "col", None, None, None),
        P("row", None),
        P("row", "col"),
        P(None, None, "row"),
    )
    out_specs = (P(None, None, "row"), P())
    return jax.shard_map(body, mesh=mesh, in_specs=in_specs, out_specs=out_specs, check_vma=False)
```
